32 devices in a mesh: dp: 8 (over z, x), fsdp: 4 (over y, core).
Axes of the slice: x: 2, y: 2, z: 4, core: 2. Of those that a mesh axis runs over, the one named last changes fastest.
Arguments:
- tokens: bfloat16 [2, 8, 1024, 768], P(None, None, ('dp', 'fsdp')), may hold values from -6 to 6
- lengths: int32 [2, 8], replicated, may hold values from 1 to 1024, 5120 in all within a row
- deal: int32 [2, 8], replicated, may hold values from 0 to 7, each once within a row
- w_qkv: bfloat16 [1769472], P(('dp', 'fsdp')), may hold values from -0.21875 to 0.21875
- b_qkv: bfloat16 [2304], P(('dp', 'fsdp')), may hold values from -2 to 2
- w_out: bfloat16 [589824], P(('dp', 'fsdp')), may hold values from -3.5 to 3.5
- b_out: bfloat16 [768], P(('dp', 'fsdp')), may hold values from -2 to 2
- norm1_gain: bfloat16 [768], P(('dp', 'fsdp')), may hold values from 0.5 to 1.5
- norm1_bias: bfloat16 [768], P(('dp', 'fsdp')), may hold values from -2 to 2
- w_up: bfloat16 [2359296], P(('dp', 'fsdp')), may hold values from -0.21875 to 0.21875
- b_up: bfloat16 [3072], P(('dp', 'fsdp')), may hold values from -2 to 2
- w_down: bfloat16 [2359296], P(('dp', 'fsdp')), may hold values from -0.109375 to 0.109375
- b_down: bfloat16 [768], P(('dp', 'fsdp')), may hold values from -2 to 2
- norm2_gain: bfloat16 [768], P(('dp', 'fsdp')), may hold values from 0.5 to 1.5
- norm2_bias: bfloat16 [768], P(('dp', 'fsdp')), may hold values from -2 to 2
- cotangent: bfloat16 [2, 8, 1024, 768], P(None, None, ('dp', 'fsdp')), may hold values from -6 to 6
Outputs:
- output: bfloat16 [2, 8, 1024, 768], P(None, None, ('dp', 'fsdp'))
- tokens_grad: bfloat16 [2, 8, 1024, 768], P(None, None, ('dp', 'fsdp'))
- w_qkv_grad: float32 [1769472], P(('dp', 'fsdp'))
- b_qkv_grad: float32 [2304], P(('dp', 'fsdp'))
- w_out_grad: float32 [589824], P(('dp', 'fsdp'))
- b_out_grad: float32 [768], P(('dp', 'fsdp'))
- norm1_gain_grad: float32 [768], P(('dp', 'fsdp'))
- norm1_bias_grad: float32 [768], P(('dp', 'fsdp'))
- w_up_grad: float32 [2359296], P(('dp', 'fsdp'))
- b_up_grad: float32 [3072], P(('dp', 'fsdp'))
- w_down_grad: float32 [2359296], P(('dp', 'fsdp'))
- b_down_grad: float32 [768], P(('dp', 'fsdp'))
- norm2_gain_grad: float32 [768], P(('dp', 'fsdp'))
- norm2_bias_grad: float32 [768], P(('dp', 'fsdp'))
The draws below stay inside these ranges and needn't reach their ends.
Inputs may be any that keep to these rules, and one draw needn't show every extreme that they name: In each micro-batch the lengths sum to 5120 and the largest is 1024. Each row of deal is a permutation of the slots of its micro-batch.
All inputs are finite; a program needn't handle non-finite values.
Results may differ from the reference program's by a relative error of at most 0.017.
Values may be sent and summed in bfloat16 or wider, within the bound.
No kernel may reach another device: no remote copies, remote signals or barrier semaphores. Data moves between devices by JAX's collectives and lax.ppermute only.
A program may use at most 256 MiB of HBM per device.

```python
import math
import jax
import jax.numpy as jnp
import numpy as np
from jax import lax

D = 768
HEADS = 12
HD = 64
FF = 3072
L = 1024
MB = 2
SLOTS = 8


def shard_levels(stream_key, extent, cuts, least, top_value):
    loudness = 1.0
    for axis_at, shards_of in cuts:
        heights = jax.random.uniform(jax.random.fold_in(jax.random.fold_in(stream_key, 6), axis_at), (shards_of,), jnp.float32, least / len(cuts), top_value / len(cuts))
        loudness = loudness * jnp.repeat(jnp.exp(heights), extent[axis_at] // shards_of).reshape((-1,) + (1,) * (len(extent) - 1 - axis_at))
    return loudness


def split_up(amount, total, limit, skew):
    loads = [(1 << 20) // math.isqrt(rank ** skew) + 1 for rank in range(2, amount + 1)]
    spare, holding = total - limit - (amount - 1), [1] * (amount - 1)
    while spare > 0:
        candidates = [i for i in range(amount - 1) if holding[i] < limit]
        whole, budget = sum([loads[i] for i in candidates]), spare
        for i in candidates:
            addition = min(limit - holding[i], max(1, budget * loads[i] // whole), spare)
            holding[i] = holding[i] + addition
            spare = spare - addition
    return np.array([limit] + holding)


def uneven(stream_key, amount, total, most, skew):
    if amount == 2:
        one = jax.random.randint(stream_key, (), max(1, total - most), min(most, total - 1) + 1)
        return jnp.stack([one, total - one])
    sizes = jnp.asarray(split_up(amount, total, most, skew), jnp.int32)
    pairs = (amount - 1) // 2
    donor, sink = sizes[1:1 + 2 * pairs:2], sizes[2:2 + 2 * pairs:2]
    room = jnp.minimum(donor - 1, most - sink)
    moved = jax.random.randint(jax.random.fold_in(stream_key, 1), (pairs,), 0, 1 << 20) % (room + 1)
    sizes = sizes.at[1:1 + 2 * pairs:2].set(donor - moved).at[2:2 + 2 * pairs:2].set(sink + moved)
    return sizes[jax.random.permutation(jax.random.fold_in(stream_key, 2), amount)]


def centred(stream_key, shape, width, most, shards=(), held_as=jnp.bfloat16):
    factor_of = shard_levels(stream_key, shape, shards, -0.22, 0.18) if shards else 1.0
    array = jax.random.normal(stream_key, shape, jnp.float32) * width * factor_of
    return jnp.minimum(jnp.maximum(array, -most), most).astype(held_as)


def setup_inputs(seed: int = 0) -> dict:
    key_list = jax.random.split(jax.random.key(seed), 17)
    return {
        "tokens": centred(key_list[0], (MB, SLOTS, L, D), 1.0, 6.0, ((2, 32),)),
        "lengths": jax.vmap(lambda own: uneven(own, SLOTS, SLOTS * L * 5 // 8, L, 2))(jax.random.split(key_list[1], MB)).reshape((MB, SLOTS)).astype(jnp.int32),
        "deal": jax.vmap(lambda own: jax.random.permutation(own, SLOTS))(jax.random.split(key_list[2], MB)).reshape((MB, SLOTS)).astype(jnp.int32),
        "w_qkv": centred(key_list[3], (3 * D * D,), D ** -0.5, 0.21875, ((0, 32),)),
        "b_qkv": centred(key_list[4], (3 * D,), 0.3, 2.0, ((0, 32),)),
        "w_out": centred(key_list[5], (D * D,), (D // 256) ** -0.5, 3.5, ((0, 32),)),
        "b_out": centred(key_list[6], (D,), 0.3, 2.0, ((0, 32),)),
        "norm1_gain": jnp.clip(1.0 + 0.1 * jax.random.normal(key_list[7], (D,), jnp.float32), 0.5, 1.5).astype(jnp.bfloat16),
        "norm1_bias": centred(key_list[8], (D,), 0.3, 2.0, ((0, 32),)),
        "w_up": centred(key_list[9], (D * FF,), D ** -0.5, 0.21875, ((0, 32),)),
        "b_up": centred(key_list[10], (FF,), 0.3, 2.0, ((0, 32),)),
        "w_down": centred(key_list[11], (FF * D,), FF ** -0.5, 0.109375, ((0, 32),)),
        "b_down": centred(key_list[12], (D,), 0.3, 2.0, ((0, 32),)),
        "norm2_gain": jnp.clip(1.0 + 0.1 * jax.random.normal(key_list[13], (D,), jnp.float32), 0.5, 1.5).astype(jnp.bfloat16),
        "norm2_bias": centred(key_list[14], (D,), 0.3, 2.0, ((0, 32),)),
        "cotangent": centred(key_list[15], (MB, SLOTS, L, D), 1.0, 6.0, ((2, 32),)),
    }


@jax.custom_vjp
def low(v):
    return lax.optimization_barrier(v.astype(jnp.bfloat16)).astype(jnp.float32)

@jax.custom_vjp
def low_back(v):
    return v

def low_keep(v):
    return (low(v), None)

def low_pass(kept, grad):
    return (grad,)

def back_keep(v):
    return (v, None)

def back_low(kept, grad):
    return (low(grad),)
low.defvjp(low_keep, low_pass)
low_back.defvjp(back_keep, back_low)

def rotate(values_in, places):
    half_dim = HD // 2
    frequency = 10000.0 ** (-(2.0 * jnp.arange(half_dim, dtype=jnp.float32)) / HD)
    angles = places.astype(jnp.float32)[:, None] * frequency[None, :]
    cosine = jnp.cos(angles)[:, None, :]
    sine_part = jnp.sin(angles)[:, None, :]
    shaped = values_in.reshape(values_in.shape[:-1] + (HEADS, half_dim, 2))
    even_part = shaped[..., 0]
    odd_part = shaped[..., 1]
    turned = jnp.stack([even_part * cosine - odd_part * sine_part, even_part * sine_part + odd_part * cosine], axis=-1)
    return turned.reshape(values_in.shape)

def normalize(row_data, norm_gain, offset):
    average = lax.optimization_barrier(jnp.mean(row_data, axis=-1, keepdims=True))
    centered = row_data - average
    variance = lax.optimization_barrier(jnp.mean(centered * centered, axis=-1, keepdims=True))
    return centered * lax.rsqrt(variance + 1e-05) * norm_gain + offset

def layer(inputs, visible, weights):
    qkv_flat, qkv_bias, out_flat, out_bias, gain_one, bias_one, up_flat, up_bias, down_flat, down_bias, gain_two, bias_two = weights
    highest = lax.Precision.HIGHEST
    batch_count = inputs.shape[0]
    projected = jnp.einsum('bld,de->ble', inputs, qkv_flat.reshape(D, 3 * D), precision=highest) + qkv_bias
    projected = low_back(projected)
    places = jnp.arange(L, dtype=jnp.int32)
    queries = low(rotate(projected[..., :D], places)).reshape(batch_count, L, HEADS, HD)
    keys_rot = low(rotate(projected[..., D:2 * D], places)).reshape(batch_count, L, HEADS, HD)
    values = low(projected[..., 2 * D:]).reshape(batch_count, L, HEADS, HD)
    scores = jnp.einsum('bqhd,bkhd->bhqk', queries, keys_rot, precision=highest) * (1.0 / math.sqrt(HD))
    scores = low_back(jnp.where(visible[:, None, None, :], scores, -1000000000.0))
    probabilities = jax.nn.softmax(scores, axis=-1)
    attended = jnp.einsum('bhqk,bkhd->bqhd', low(probabilities), values, precision=highest).reshape(batch_count, L, D)
    merged = low(low_back(attended))
    branch = low_back(jnp.einsum('bld,de->ble', merged, out_flat.reshape(D, D), precision=highest) + out_bias)
    normed = normalize(inputs + branch, gain_one, bias_one)
    hidden = low_back(jnp.einsum('bld,df->blf', low(normed), up_flat.reshape(D, FF), precision=highest) + up_bias)
    active = jax.nn.gelu(hidden, approximate=False)
    down_out = low_back(jnp.einsum('blf,fd->bld', low(active), down_flat.reshape(FF, D), precision=highest) + down_bias)
    return normalize(normed + down_out, gain_two, bias_two)

def reference(tokens, lengths, deal, w_qkv, b_qkv, w_out, b_out, norm1_gain, norm1_bias, w_up, b_up, w_down, b_down, norm2_gain, norm2_bias, cotangent):
    params = tuple((piece.astype(jnp.float32) for piece in (w_qkv, b_qkv, w_out, b_out, norm1_gain, norm1_bias, w_up, b_up, w_down, b_down, norm2_gain, norm2_bias)))
    batch_ids = jnp.arange(MB, dtype=jnp.int32)[:, None]
    home_len = jnp.zeros((MB, SLOTS), jnp.int32).at[batch_ids, deal].set(lengths)
    sequences = MB * SLOTS
    per_step = math.gcd(sequences, max(1, 4096 // L))
    step_count = sequences // per_step
    inputs = tokens.astype(jnp.float32).reshape(step_count, per_step, L, D)
    grads_in = cotangent.astype(jnp.float32).reshape(step_count, per_step, L, D)
    len_steps = home_len.reshape(step_count, per_step)
    places = jnp.arange(L, dtype=jnp.int32)

    def advance(totals, item):
        block_in, wanted, seq_len = item
        visible = places[None, :] < seq_len[:, None]

        def forward(block_x, *weights):
            return layer(block_x, visible, weights)
        result, pullback = jax.vjp(forward, block_in, *params)
        gradient = pullback(wanted)
        totals = tuple((total_part + grad_part for total_part, grad_part in zip(totals, gradient[1:])))
        return (totals, (result.astype(jnp.bfloat16), gradient[0].astype(jnp.bfloat16)))
    zeroed = tuple((jnp.zeros_like(piece) for piece in params))
    totals, (outputs, input_grad) = lax.scan(advance, zeroed, (inputs, grads_in, len_steps))
    return (outputs.reshape(MB, SLOTS, L, D), input_grad.reshape(MB, SLOTS, L, D), totals[0], totals[1], totals[2], totals[3], totals[4], totals[5], totals[6], totals[7], totals[8], totals[9], totals[10], totals[11])
```

```python
import math

import jax
import jax.numpy as jnp
from jax import lax
from jax.sharding import PartitionSpec as P

D = 768
HEADS = 12
HD = 64
FF = 3072
AXES = ("dp", "fsdp")
F32 = jnp.float32
BF16 = jnp.bfloat16


class Plan:
    def __init__(self, n_dp, n_fsdp):
        self.n = n_dp * n_fsdp
        self.chips = self.n // 2
        bits = [1 << k for k in range(1, self.n.bit_length() - 1)]
        near, far = bits[:2], bits[2:]
        first = [b | (b >> 1) if b >> 1 in far else b for b in reversed(far)]
        self.masks = [first + near[::-1], first + near]
        self.levels = len(bits)
        self.combos = []
        for masks in self.masks:
            row = []
            for rel in range(self.chips):
                total = 0
                for k in range(self.levels):
                    if rel >> k & 1:
                        total ^= masks[k]
                row.append(total)
            self.combos.append(row)

    def pairs(self, level):
        return [(i, i ^ self.masks[i & 1][level]) for i in range(self.n)]

    def core_pairs(self):
        return [(i, i ^ 1) for i in range(self.n)]

    def order(self, me, core):
        table = jnp.asarray(self.combos, jnp.int32)
        return (me ^ jnp.where(core == 0, table[0], table[1])) // 2


def swap(value, pairs):
    return lax.ppermute(value, AXES, pairs)


def gather_chips(plan, piece):
    held = piece[None]
    for level in range(plan.levels):
        held = jnp.concatenate([held, swap(held, plan.pairs(level))], axis=0)
    return held


def reduce_chips(plan, pieces):
    held = pieces
    for level in reversed(range(plan.levels)):
        half = held.shape[0] // 2
        got = swap(held[half:].astype(BF16), plan.pairs(level))
        held = held[:half].astype(F32) + got.astype(F32)
        if level > 0:
            held = held.astype(BF16)
    return held[0]


def split_columns(plan, core, shard):
    half = shard.shape[1] // 2
    left, right = shard[:, :half], shard[:, half:]
    keep = jnp.where(core == 0, left, right)
    got = swap(jnp.where(core == 0, right, left), plan.core_pairs())
    return jnp.where(core == 0, jnp.concatenate([keep, got], 0), jnp.concatenate([got, keep], 0))


def unsplit_columns(plan, core, block):
    rows = block.shape[0] // 2
    upper, lower = block[:rows], block[rows:]
    keep = jnp.where(core == 0, upper, lower)
    got = swap(jnp.where(core == 0, lower, upper), plan.core_pairs())
    return jnp.where(core == 0, jnp.concatenate([keep, got], 1), jnp.concatenate([got, keep], 1))


def rotate(values_in, places, backward):
    half_dim = HD // 2
    frequency = 10000.0 ** (-(2.0 * jnp.arange(half_dim, dtype=F32)) / HD)
    angles = places.astype(F32)[:, None] * frequency[None, :]
    cosine = jnp.cos(angles)[:, None, :]
    sine_part = jnp.sin(angles)[:, None, :]
    if backward:
        sine_part = -sine_part
    shaped = values_in.reshape(values_in.shape[0], HEADS, half_dim, 2)
    even_part = shaped[..., 0]
    odd_part = shaped[..., 1]
    turned = jnp.stack(
        [even_part * cosine - odd_part * sine_part, even_part * sine_part + odd_part * cosine],
        axis=-1,
    )
    return turned.reshape(values_in.shape)


def normalize(row_data, norm_gain, offset):
    average = jnp.mean(row_data, axis=-1, keepdims=True)
    centered = row_data - average
    variance = jnp.mean(centered * centered, axis=-1, keepdims=True)
    inverse = lax.rsqrt(variance + 1e-05)
    standard = centered * inverse
    return (standard * norm_gain + offset, standard, inverse)


def normalize_back(grad_out, standard, inverse, norm_gain):
    grad_std = grad_out * norm_gain
    mean_grad = jnp.mean(grad_std, axis=-1, keepdims=True)
    mean_proj = jnp.mean(grad_std * standard, axis=-1, keepdims=True)
    grad_in = inverse * (grad_std - mean_grad - standard * mean_proj)
    return (grad_in, jnp.sum(grad_out * standard, axis=0), jnp.sum(grad_out, axis=0))


def gelu_slope(hidden):
    cumulative = 0.5 * (1.0 + lax.erf(hidden * (1.0 / math.sqrt(2.0))))
    return cumulative + hidden * jnp.exp(-0.5 * hidden * hidden) * (1.0 / math.sqrt(2.0 * math.pi))


def contract_rows(left, right):
    return lax.dot_general(left, right, (((0,), (0,)), ((), ())), preferred_element_type=F32)


def times_transposed(left, right):
    return lax.dot_general(left, right, (((1,), (1,)), ((), ())), preferred_element_type=F32)


def body(
    tokens,
    lengths,
    deal,
    w_qkv,
    b_qkv,
    w_out,
    b_out,
    norm1_gain,
    norm1_bias,
    w_up,
    b_up,
    w_down,
    b_down,
    norm2_gain,
    norm2_bias,
    cotangent,
):
    n_dp = lax.axis_size("dp")
    n_fsdp = lax.axis_size("fsdp")
    plan = Plan(n_dp, n_fsdp)
    n = plan.n
    dp_place = lax.axis_index("dp")
    fsdp_place = lax.axis_index("fsdp")
    me = dp_place * n_fsdp + fsdp_place
    core = me % 2
    batches, slot_count, home_rows, width = tokens.shape
    group = n_fsdp // batches
    part_rows = home_rows // group
    rows = n * part_rows
    local = fsdp_place % group
    batch_place = fsdp_place // group
    scale = 1.0 / math.sqrt(HD)
    mine = plan.order(me, core)
    other = plan.order(me, 1 - core)
    group_pairs = [
        [(i, i - i % group + (i + k) % group) for i in range(n)] for k in range(1, group)
    ]

    def spread(array):
        parts = array.reshape(batches, slot_count, group, part_rows, width)
        parts = parts.transpose(1, 0, 2, 3, 4).reshape(n, part_rows, width)
        moved = lax.all_to_all(parts, AXES, split_axis=0, concat_axis=0, tiled=True)
        return moved.reshape(rows, width)

    def collect(array):
        parts = array.reshape(n, part_rows, width)
        moved = lax.all_to_all(parts, AXES, split_axis=0, concat_axis=0, tiled=True)
        moved = moved.reshape(slot_count, batches, group, part_rows, width)
        return moved.transpose(1, 0, 2, 3, 4).reshape(batches, slot_count, home_rows, width)

    def fetch_split(shard, columns):
        piece = split_columns(plan, core, shard.reshape(-1, columns))
        own = gather_chips(plan, piece)
        par = swap(own, plan.core_pairs())
        own = own[mine_back].reshape(-1, columns // 2)
        par = par[other_back].reshape(-1, columns // 2)
        return jnp.where(
            core == 0, jnp.concatenate([own, par], 1), jnp.concatenate([par, own], 1)
        )

    def fetch_rows(shard, columns):
        own = gather_chips(plan, shard.reshape(-1, columns))
        par = swap(own, plan.core_pairs())
        own = own[mine_back]
        par = par[other_back]
        both = jnp.where(core == 0, jnp.stack([own, par], 1), jnp.stack([par, own], 1))
        return both.reshape(-1, columns)

    def return_split(grad):
        columns = grad.shape[1]
        blocks = grad.reshape(plan.chips, -1, columns)
        half = columns // 2
        left, right = blocks[..., :half], blocks[..., half:]
        own = jnp.where(core == 0, left, right)[mine].astype(BF16)
        par = jnp.where(core == 0, right, left)[other].astype(BF16)
        got = swap(par, plan.core_pairs())
        total = (own.astype(F32) + got.astype(F32)).astype(BF16)
        return unsplit_columns(plan, core, reduce_chips(plan, total)).reshape(-1)

    def return_rows(grad):
        columns = grad.shape[1]
        blocks = grad.reshape(plan.chips, 2, -1, columns)
        own = jnp.where(core == 0, blocks[:, 0], blocks[:, 1])[mine].astype(BF16)
        par = jnp.where(core == 0, blocks[:, 1], blocks[:, 0])[other].astype(BF16)
        got = swap(par, plan.core_pairs())
        total = (own.astype(F32) + got.astype(F32)).astype(BF16)
        return reduce_chips(plan, total).reshape(-1)

    chip_ids = jnp.arange(plan.chips, dtype=jnp.int32)
    mine_back = jnp.argmax(mine[None, :] == chip_ids[:, None], axis=1).astype(jnp.int32)
    other_back = jnp.argmax(other[None, :] == chip_ids[:, None], axis=1).astype(jnp.int32)

    small_shards = (
        b_qkv,
        b_out,
        norm1_gain,
        norm1_bias,
        b_up,
        b_down,
        norm2_gain,
        norm2_bias,
    )
    sizes = [piece.shape[0] for piece in small_shards]
    packed = jnp.concatenate(small_shards)
    everyone = lax.all_to_all(
        jnp.broadcast_to(packed[None], (n, packed.shape[0])),
        AXES,
        split_axis=0,
        concat_axis=0,
        tiled=True,
    )
    vectors = []
    start = 0
    for size in sizes:
        vectors.append(everyone[:, start : start + size].reshape(-1).astype(F32))
        start += size
    (qkv_bias, out_bias, gain_one, bias_one, up_bias, down_bias, gain_two, bias_two) = vectors

    block_in = spread(tokens)
    qkv_mat = fetch_split(w_qkv, 3 * D)
    out_mat = fetch_split(w_out, D)
    up_mat = fetch_split(w_up, FF)
    down_mat = fetch_rows(w_down, D)
    grad_top = spread(cotangent).astype(F32)

    home_len = jnp.zeros((batches, slot_count), jnp.int32)
    home_len = home_len.at[jnp.arange(batches, dtype=jnp.int32)[:, None], deal].set(lengths)
    seq_len = home_len[batch_place, dp_place]

    row_ids = jnp.arange(rows, dtype=jnp.int32)
    base_places = row_ids // part_rows * home_rows + row_ids % part_rows
    query_places = base_places + local * part_rows
    key_places = jnp.concatenate(
        [base_places + (local + k) % group * part_rows for k in range(group)]
    )
    visible = key_places < seq_len

    projected = jnp.dot(block_in, qkv_mat, preferred_element_type=F32) + qkv_bias
    queries = rotate(projected[:, :D], query_places, False).astype(BF16)
    keys_local = rotate(projected[:, D : 2 * D], query_places, False).astype(BF16)
    values_local = projected[:, 2 * D :].astype(BF16)
    key_value = jnp.concatenate([keys_local, values_local], axis=1)
    back_pairs = [[(b, a) for a, b in pairs] for pairs in group_pairs]
    all_kv = jnp.concatenate([key_value] + [swap(key_value, pairs) for pairs in back_pairs])
    query_heads = queries.reshape(rows, HEADS, HD)
    key_heads = all_kv[:, :D].reshape(-1, HEADS, HD)
    value_heads = all_kv[:, D:].reshape(-1, HEADS, HD)

    def scores_of():
        scores = (
            jnp.einsum("qhd,khd->hqk", query_heads, key_heads, preferred_element_type=F32) * scale
        )
        return jnp.where(visible[None, None, :], scores, -1000000000.0)

    scores = scores_of()
    peak = jnp.max(scores, axis=-1, keepdims=True)
    expanded = jnp.exp(scores - peak)
    row_total_exp = jnp.sum(expanded, axis=-1, keepdims=True)
    probabilities = expanded / row_total_exp
    log_total = peak + jnp.log(row_total_exp)
    attended = jnp.einsum(
        "hqk,khd->qhd", probabilities.astype(BF16), value_heads, preferred_element_type=F32
    )
    merged = attended.reshape(rows, D).astype(BF16)
    branch = jnp.dot(merged, out_mat, preferred_element_type=F32) + out_bias
    normed, standard_one, inverse_one = normalize(
        block_in.astype(F32) + branch, gain_one, bias_one
    )
    normed_low = normed.astype(BF16)
    hidden = jnp.dot(normed_low, up_mat, preferred_element_type=F32) + up_bias
    active_low = jax.nn.gelu(hidden, approximate=False).astype(BF16)
    down_out = jnp.dot(active_low, down_mat, preferred_element_type=F32) + down_bias
    result, standard_two, inverse_two = normalize(normed + down_out, gain_two, bias_two)
    home_out = collect(result.astype(BF16))

    grad_two, gain_two_grad, bias_two_grad = normalize_back(
        grad_top, standard_two, inverse_two, gain_two
    )
    down_grad = grad_two.astype(BF16)
    down_bias_grad = jnp.sum(down_grad.astype(F32), axis=0)
    down_mat_grad = return_rows(contract_rows(active_low, down_grad))
    hidden_grad = (times_transposed(down_grad, down_mat) * gelu_slope(hidden)).astype(BF16)
    up_bias_grad = jnp.sum(hidden_grad.astype(F32), axis=0)
    up_mat_grad = return_split(contract_rows(normed_low, hidden_grad))
    normed_grad = grad_two + times_transposed(hidden_grad, up_mat)
    grad_one, gain_one_grad, bias_one_grad = normalize_back(
        normed_grad, standard_one, inverse_one, gain_one
    )
    branch_grad = grad_one.astype(BF16)
    out_bias_grad = jnp.sum(branch_grad.astype(F32), axis=0)
    out_mat_grad = return_split(contract_rows(merged, branch_grad))
    merged_grad = times_transposed(branch_grad, out_mat).astype(BF16).reshape(rows, HEADS, HD)
    probabilities = jnp.exp(scores_of() - log_total)
    prob_grad = jnp.einsum("qhd,khd->hqk", merged_grad, value_heads, preferred_element_type=F32)
    row_dot = jnp.sum(prob_grad * probabilities, axis=-1, keepdims=True)
    score_grad = (probabilities * (prob_grad - row_dot)).astype(BF16)
    query_grad = (
        jnp.einsum("hqk,khd->qhd", score_grad, key_heads, preferred_element_type=F32) * scale
    )
    values_grad = jnp.einsum(
        "hqk,qhd->khd", probabilities.astype(BF16), merged_grad, preferred_element_type=F32
    )
    keys_grad = (
        jnp.einsum("hqk,qhd->khd", score_grad, query_heads, preferred_element_type=F32) * scale
    )
    both = jnp.concatenate([keys_grad.reshape(-1, D), values_grad.reshape(-1, D)], axis=1)
    kv_part = both[:rows]
    for k in range(1, group):
        kv_part = kv_part + swap(
            both[k * rows : (k + 1) * rows].astype(BF16), group_pairs[k - 1]
        ).astype(F32)
    qkv_grad = jnp.concatenate(
        [
            rotate(query_grad.reshape(rows, D), query_places, True),
            rotate(kv_part[:, :D], query_places, True),
            kv_part[:, D:],
        ],
        axis=-1,
    ).astype(BF16)
    qkv_bias_grad = jnp.sum(qkv_grad.astype(F32), axis=0)
    qkv_mat_grad = return_split(contract_rows(block_in, qkv_grad))
    input_grad = times_transposed(qkv_grad, qkv_mat) + grad_one
    home_grad = collect(input_grad.astype(BF16))

    small_grads = (
        qkv_bias_grad,
        out_bias_grad,
        gain_one_grad,
        bias_one_grad,
        up_bias_grad,
        down_bias_grad,
        gain_two_grad,
        bias_two_grad,
    )
    packed_grads = jnp.concatenate([piece.reshape(n, -1) for piece in small_grads], axis=1)
    got = lax.all_to_all(packed_grads, AXES, split_axis=0, concat_axis=0, tiled=True)
    summed = jnp.sum(got, axis=0)
    owned = []
    start = 0
    for size in sizes:
        owned.append(summed[start : start + size])
        start += size
    return (
        home_out,
        home_grad,
        qkv_mat_grad,
        owned[0],
        out_mat_grad,
        owned[1],
        owned[2],
        owned[3],
        up_mat_grad,
        owned[4],
        down_mat_grad,
        owned[5],
        owned[6],
        owned[7],
    )


def solution(mesh):
    rows = P(None, None, AXES, None)
    flat = P(AXES)
    in_specs = (rows, P(), P()) + (flat,) * 12 + (rows,)
    out_specs = (rows, rows) + (flat,) * 12
    return jax.shard_map(body, mesh=mesh, in_specs=in_specs, out_specs=out_specs, check_vma=False)
```

```python
import math

import jax
import jax.numpy as jnp
from jax import lax
from jax.experimental import pallas as pl
from jax.experimental.pallas import tpu as pltpu
from jax.sharding import PartitionSpec as P

D = 768
HEADS = 12
HD = 64
FF = 3072
AXES = ("dp", "fsdp")
BLOCK = 384
F32 = jnp.float32
BF16 = jnp.bfloat16


class Plan:
    def __init__(self, n_dp, n_fsdp):
        self.n = n_dp * n_fsdp
        self.chips = self.n // 2
        bits = [1 << k for k in range(1, self.n.bit_length() - 1)]
        near, far = bits[:2], bits[2:]
        first = [b | (b >> 1) if b >> 1 in far else b for b in reversed(far)]
        self.masks = [first + near[::-1], first + near]
        self.levels = len(bits)
        self.combos = []
        for masks in self.masks:
            row = []
            for rel in range(self.chips):
                total = 0
                for k in range(self.levels):
                    if rel >> k & 1:
                        total ^= masks[k]
                row.append(total)
            self.combos.append(row)

    def pairs(self, level):
        return [(i, i ^ self.masks[i & 1][level]) for i in range(self.n)]

    def core_pairs(self):
        return [(i, i ^ 1) for i in range(self.n)]

    def order(self, me, core):
        table = jnp.asarray(self.combos, jnp.int32)
        return (me ^ jnp.where(core == 0, table[0], table[1])) // 2

    def places(self, me, core):
        spots = [[0] * self.chips for _ in range(2)]
        for spot, row in zip(spots, self.combos):
            for rel, total in enumerate(row):
                spot[total // 2] = rel
        table = jnp.asarray(spots, jnp.int32)
        away = jnp.arange(self.chips, dtype=jnp.int32) ^ (me // 2)
        return jnp.where(core == 0, table[0], table[1])[away]


def swap(value, pairs):
    return lax.ppermute(value, AXES, pairs)


def after(value, *earlier):
    return lax.optimization_barrier((value,) + earlier)[0]


class Gather:
    def __init__(self, plan, piece):
        self.plan = plan
        self.held = piece[None]
        self.got = []

    def step(self, *earlier):
        level = len(self.got)
        if level > 0:
            self.held = jnp.concatenate([self.held, self.got[-1]], axis=0)
        if earlier:
            self.held = after(self.held, *earlier)
        self.got.append(swap(self.held, self.plan.pairs(level)))
        return self.held

    def finish(self, *earlier):
        self.own = [self.held, after(self.got[-1], *earlier) if earlier else self.got[-1]]
        self.par = [swap(part, self.plan.core_pairs()) for part in self.own]


class Reduction:
    def __init__(self, plan, par, own):
        self.plan = plan
        self.kept = own
        self.got = swap(par, plan.core_pairs())
        self.level = plan.levels

    def step(self, *earlier):
        self.level -= 1
        if earlier:
            self.got = after(self.got, *earlier)
        half = self.kept.shape[0] // 2
        kept, got = self.kept.astype(F32), self.got.astype(F32)
        away = (kept[half:] + got[half:]).astype(BF16)
        self.got = swap(away, self.plan.pairs(self.level))
        self.kept = kept[:half] + got[:half]
        if self.level > 0:
            self.kept = self.kept.astype(BF16)
        return away

    def steps_left(self, *earlier):
        return [self.step(*earlier) for _ in range(self.level)]

    def finish(self):
        self.steps_left()
        return (self.kept + self.got.astype(F32))[0]


def split_columns(plan, core, left, right):
    keep = jnp.where(core == 0, left, right)
    got = swap(jnp.where(core == 0, right, left), plan.core_pairs())
    return jnp.where(core == 0, jnp.concatenate([keep, got], 1), jnp.concatenate([got, keep], 1))


def unsplit_columns(plan, core, block):
    rows = block.shape[1] // 2
    upper, lower = block[:, :rows], block[:, rows:]
    keep = jnp.where(core == 0, upper, lower)
    got = swap(jnp.where(core == 0, lower, upper), plan.core_pairs())
    return jnp.where(core == 0, keep, got), jnp.where(core == 0, got, keep)


def vmem(array):
    return (array, pl.BlockSpec(memory_space=pltpu.VMEM))


def smem(array):
    return (array, pl.BlockSpec(memory_space=pltpu.SMEM))


def loose(array):
    return (array, pl.BlockSpec(memory_space=pl.ANY))


def lane_block(array, width, place):
    return (array, pl.BlockSpec((array.shape[0], width), lambda step: (0, place)))


def run_kernel(body, name, ins, outs, scratch, micros, grid=()):
    return pl.pallas_call(
        body,
        name=name,
        grid=grid,
        in_specs=[spec for _, spec in ins],
        out_specs=[
            pl.BlockSpec(memory_space=pltpu.VMEM if inside else pl.ANY) for _, _, inside in outs
        ],
        out_shape=[jax.ShapeDtypeStruct(shape, dtype) for shape, dtype, _ in outs],
        scratch_shapes=scratch,
        compiler_params=pltpu.CompilerParams(vmem_limit_bytes=32 * 2**20),
        cost_estimate=pl.CostEstimate(
            flops=int(micros * 1.1e9), bytes_accessed=2**20, transcendentals=0
        ),
    )(*[array for array, _ in ins])


def dot_nn(left, right):
    return jnp.dot(left, right, preferred_element_type=F32)


def dot_nt(left, right):
    return lax.dot_general(left, right, (((1,), (1,)), ((), ())), preferred_element_type=F32)


def dot_tn(left, right):
    return lax.dot_general(left, right, (((0,), (0,)), ((), ())), preferred_element_type=F32)


class Weight:
    def __init__(self, sources, places, blocks, height):
        self.sources = sources
        self.places = places
        self.blocks = blocks
        self.height = height

    def ins(self):
        return [smem(self.places)] + [loose(array) for array, _, _ in self.sources]

    def scratch(self):
        return [pltpu.VMEM((self.blocks, self.height, BLOCK), BF16), pltpu.SemaphoreType.DMA(())]

    def count(self):
        return 1 + len(self.sources)

    def start(self, refs, held, sem):
        places, at = refs[0], 0
        for (_, first, number), ref in zip(self.sources, refs[1:]):
            count, _, rows, _ = ref.shape
            for k in range(count):
                row = pl.multiple_of(places[2 * at + 1], 16)
                pltpu.make_async_copy(
                    ref.at[k, pl.ds(first, number)],
                    held.at[pl.ds(places[2 * at], number), pl.ds(row, rows)],
                    sem,
                ).start()
                at += 1


def wait_load(held, sem):
    pltpu.make_async_copy(held, held, sem).wait()


def turned(values, cosine, sine):
    lanes = lax.broadcasted_iota(jnp.int32, values.shape, 1)
    swapped = jnp.where(
        lanes % 2 == 0, pltpu.roll(values, 127, 1), pltpu.roll(values, 1, 1)
    )
    return values * cosine + swapped * sine


def qkv_forward(x, weight, bias, cosine, sine, ready):
    rows = x.shape[0]
    n_w = weight.count()

    def body(*refs):
        x_ref, b_ref, cos_ref, sin_ref = refs[:4]
        w_refs = refs[4 : 4 + n_w]
        q_ref, kv_ref, held, sem = refs[4 + n_w + len(ready) :]
        weight.start(w_refs, held, sem)
        wait_load(held, sem)
        cos, sin = cos_ref[...], sin_ref[...]
        for t in range(weight.blocks):
            y = dot_nn(x_ref[...], held[t]) + b_ref[:, t * BLOCK : (t + 1) * BLOCK]
            for g in range(BLOCK // 128):
                piece = y[:, g * 128 : (g + 1) * 128]
                at = t * BLOCK + g * 128
                if at < 2 * D:
                    piece = turned(piece, cos, sin)
                if at < D:
                    q_ref[:, at : at + 128] = (piece * (1.0 / math.sqrt(HD))).astype(BF16)
                else:
                    kv_ref[:, at - D : at - D + 128] = piece.astype(BF16)

    return run_kernel(
        body,
        "qkv_forward",
        [lane_block(x, D, 0), vmem(bias), vmem(cosine), vmem(sine)]
        + weight.ins()
        + [loose(array) for array in ready],
        [((rows, D), BF16, True), ((rows, 2 * D), BF16, True)],
        weight.scratch(),
        7,
        grid=(1,),
    )


def row_standard(values):
    average = jnp.mean(values, axis=-1, keepdims=True)
    centered = values - average
    variance = jnp.mean(centered * centered, axis=-1, keepdims=True)
    inverse = lax.rsqrt(variance + 1e-05)
    return centered * inverse, inverse


def row_standard_back(grad, standard, inverse):
    mean_grad = jnp.mean(grad, axis=-1, keepdims=True)
    mean_proj = jnp.mean(grad * standard, axis=-1, keepdims=True)
    return inverse * (grad - mean_grad - standard * mean_proj)


PART = 256


def attention_forward(queries, key_values, mask, part, ready):
    rows = queries.shape[0]
    n_kv = len(key_values)
    block = min(rows, 256)

    def body(*refs):
        q_ref, mask_ref = refs[:2]
        k_refs = refs[2 : 2 + n_kv]
        v_refs = refs[2 + n_kv : 2 + 2 * n_kv]
        a_ref, lse_ref, lse_acc = refs[2 + 2 * n_kv + len(ready) :]
        lse_acc[...] = jnp.zeros_like(lse_acc)
        lanes = lax.broadcasted_iota(jnp.int32, (block, 128), 1)
        for p in range(PART // 128):
            at = slice(p * 128, (p + 1) * 128)
            for r in range(rows // block):
                own = slice(r * block, (r + 1) * block)
                q_pair = q_ref[own, at].astype(F32)
                heads = []
                for head in range(2):
                    q_head = jnp.where(lanes // HD == head, q_pair, 0.0).astype(BF16)
                    scores = [
                        dot_nt(q_head, key[:, at]) + mask_ref[g : g + 1, :]
                        for g, key in enumerate(k_refs)
                    ]
                    peak = scores[0].max(axis=-1, keepdims=True)
                    for s in scores[1:]:
                        peak = jnp.maximum(peak, s.max(axis=-1, keepdims=True))
                    raised = [jnp.exp(s - peak) for s in scores]
                    total = raised[0].sum(axis=-1, keepdims=True)
                    for e in raised[1:]:
                        total = total + e.sum(axis=-1, keepdims=True)
                    mixed = dot_nn(raised[0].astype(BF16), v_refs[0][:, at])
                    for e, value in zip(raised[1:], v_refs[1:]):
                        mixed = mixed + dot_nn(e.astype(BF16), value[:, at])
                    heads.append(mixed / total)
                    lse_acc[own, :] = jnp.where(
                        lanes == 2 * p + head, peak + jnp.log(total), lse_acc[own, :]
                    )
                a_ref[own, at] = jnp.where(lanes < HD, heads[0], heads[1]).astype(BF16)
        lse_ref[...] = jnp.transpose(lse_acc[...])[:8]

    return run_kernel(
        body,
        "attention_forward",
        [lane_block(queries, PART, part), vmem(mask)]
        + [lane_block(kv, PART, part) for kv in key_values]
        + [lane_block(kv, PART, part + D // PART) for kv in key_values]
        + [loose(array) for array in ready],
        [((rows, PART), BF16, True), ((8, rows), F32, True)],
        [pltpu.VMEM((rows, 128), F32)],
        6,
        grid=(1,),
    )


def out_forward(x, attended, weight, vectors):
    rows = x.shape[0]
    n_a = len(attended)
    n_w = weight.count()
    block = min(rows, 128)

    def body(*refs):
        x_ref, ob_ref, g_ref, b_ref = refs[:4]
        part_refs = refs[4 : 4 + n_a]
        w_refs = refs[4 + n_a : 4 + n_a + n_w]
        a_ref, n_ref, s_ref, h_ref, held, sem, acc = refs[4 + n_a + n_w :]
        weight.start(w_refs, held, sem)
        for k, part in enumerate(part_refs):
            a_ref[:, k * PART : (k + 1) * PART] = part[...]
        wait_load(held, sem)
        for t in range(weight.blocks):
            acc[:, t * BLOCK : (t + 1) * BLOCK] = dot_nn(a_ref[...], held[t])

        def row(r, carry):
            own = pl.ds(pl.multiple_of(r * block, block), block)
            branch = acc[own, :] + ob_ref[...]
            standard, inverse = row_standard(x_ref[own, :].astype(F32) + branch)
            n_ref[own, :] = standard
            s_ref[own, :] = jnp.broadcast_to(inverse, (block, 128))
            h_ref[own, :] = (standard * g_ref[...] + b_ref[...]).astype(BF16)
            return carry

        lax.fori_loop(0, rows // block, row, 0)

    return run_kernel(
        body,
        "out_forward",
        [lane_block(x, D, 0)]
        + [vmem(v) for v in vectors]
        + [vmem(part) for part in attended]
        + weight.ins(),
        [
            ((rows, D), BF16, True),
            ((rows, D), F32, True),
            ((rows, 128), F32, True),
            ((rows, D), BF16, True),
        ],
        weight.scratch() + [pltpu.VMEM((rows, D), F32)],
        4,
        grid=(1,),
    )


def bell(u):
    size = jnp.abs(u)
    t = 1.0 / (1.0 + (0.3275911 / math.sqrt(2.0)) * size)
    raised = jnp.exp(-0.5 * u * u)
    poly = 0.5 * 1.061405429
    for c in (-1.453152027, 1.421413741, -0.284496736, 0.254829592):
        poly = poly * t + 0.5 * c
    tail = poly * t * raised
    return jnp.where(u >= 0.0, 1.0 - tail, tail), raised


def up_forward(h, weight, bias, ready):
    rows = h.shape[0]
    n_w = weight.count()

    def body(*refs):
        h_ref, b_ref = refs[:2]
        w_refs = refs[2 : 2 + n_w]
        g_ref, slope_ref, held, sem = refs[2 + n_w + len(ready) :]
        weight.start(w_refs, held, sem)
        wait_load(held, sem)

        def step(t, carry):
            at = pl.ds(pl.multiple_of(t * BLOCK, 128), BLOCK)
            u = dot_nn(h_ref[...], held[t]) + b_ref[:, at]
            share, raised = bell(u)
            g_ref[:, at] = (u * share).astype(BF16)
            slope_ref[:, at] = (share + u * raised * (1.0 / math.sqrt(2.0 * math.pi))).astype(BF16)
            return carry

        lax.fori_loop(0, weight.blocks, step, 0)

    return run_kernel(
        body,
        "up_forward",
        [vmem(h), vmem(bias)] + weight.ins() + [loose(array) for array in ready],
        [((rows, FF), BF16, True), ((rows, FF), BF16, True)],
        weight.scratch(),
        14,
    )


def down_both(active, weight, standard_one, cot, vectors):
    rows = active.shape[0]
    n_w = weight.count()
    block = min(rows, 128)

    def body(*refs):
        g_ref, n_ref, cot_ref, g1_ref, b1_ref, db_ref, g2_ref, b2_ref = refs[:8]
        w_refs = refs[8 : 8 + n_w]
        out_ref, dr_ref, dz_ref, sums_ref, held, sem, z_ref = refs[8 + n_w :]
        weight.start(w_refs, held, sem)
        wait_load(held, sem)

        for t in range(weight.blocks):
            z_ref[:, t * BLOCK : (t + 1) * BLOCK] = dot_nn(g_ref[...], held[t])
        sums_ref[...] = jnp.zeros_like(sums_ref)

        def row(r, carry):
            own = pl.ds(pl.multiple_of(r * block, block), block)
            h = n_ref[own, :] * g1_ref[...] + b1_ref[...]
            standard, inverse = row_standard(h + z_ref[own, :] + db_ref[...])
            out_ref[own, :] = (standard * g2_ref[...] + b2_ref[...]).astype(BF16)
            dy = cot_ref[own, :].astype(F32)
            dr = row_standard_back(dy * g2_ref[...], standard, inverse)
            dr_ref[own, :] = dr
            low = dr.astype(BF16)
            dz_ref[own, :] = low
            sums_ref[0:1, :] += jnp.sum(dy * standard, axis=0, keepdims=True)
            sums_ref[1:2, :] += jnp.sum(dy, axis=0, keepdims=True)
            sums_ref[2:3, :] += jnp.sum(low.astype(F32), axis=0, keepdims=True)
            return carry

        lax.fori_loop(0, rows // block, row, 0)

    return run_kernel(
        body,
        "down_both",
        [vmem(active), vmem(standard_one), vmem(cot)] + [vmem(v) for v in vectors] + weight.ins(),
        [
            ((rows, D), BF16, True),
            ((rows, D), F32, True),
            ((rows, D), BF16, True),
            ((8, D), F32, True),
        ],
        weight.scratch() + [pltpu.VMEM((rows, D), F32)],
        10,
    )


def up_back(dz, weight, slope, ready):
    rows = dz.shape[0]
    n_w = weight.count()
    tile = 512

    def body(*refs):
        dz_ref, slope_ref = refs[:2]
        w_refs = refs[2 : 2 + n_w]
        du_ref, sums_ref, held, sem = refs[2 + n_w + len(ready) :]
        weight.start(w_refs, held, sem)
        wait_load(held, sem)
        sums_ref[...] = jnp.zeros_like(sums_ref)

        def step(t, carry):
            at = pl.ds(pl.multiple_of(t * tile, tile), tile)
            grad = dot_nt(dz_ref[:, :BLOCK], held[0, at, :])
            for k in range(1, weight.blocks):
                grad = grad + dot_nt(dz_ref[:, k * BLOCK : (k + 1) * BLOCK], held[k, at, :])
            du = (grad * slope_ref[:, at].astype(F32)).astype(BF16)
            du_ref[:, at] = du
            sums_ref[0:1, at] = jnp.sum(du.astype(F32), axis=0, keepdims=True)
            return carry

        lax.fori_loop(0, FF // tile, step, 0)

    return run_kernel(
        body,
        "up_back",
        [vmem(dz), vmem(slope)] + weight.ins() + [loose(array) for array in ready],
        [((rows, FF), BF16, True), ((8, FF), F32, True)],
        weight.scratch(),
        9,
    )


def norm_back(du, weight_up, weight_out, dr2, standard, inverse, gain, ready):
    rows = du.shape[0]
    n_u, n_o = weight_up.count(), weight_out.count()
    block = min(rows, 128)

    def body(*refs):
        du_ref, dr2_ref, n_ref, s_ref, g_ref = refs[:5]
        u_refs = refs[5 : 5 + n_u]
        o_refs = refs[5 + n_u : 5 + n_u + n_o]
        dr_ref, do_ref, da_ref, sums_ref, up, up_sem, out, out_sem, acc = refs[
            5 + n_u + n_o + len(ready) :
        ]
        weight_up.start(u_refs, up, up_sem)
        weight_out.start(o_refs, out, out_sem)
        wait_load(up, up_sem)
        acc[...] = dr2_ref[...]

        def part(t, carry):
            at = pl.ds(pl.multiple_of(t * BLOCK, 128), BLOCK)
            acc[...] += dot_nt(du_ref[:, at], up[t])
            return carry

        lax.fori_loop(0, weight_up.blocks, part, 0)
        sums_ref[...] = jnp.zeros_like(sums_ref)

        def row(r, carry):
            own = pl.ds(pl.multiple_of(r * block, block), block)
            dh = acc[own, :]
            standard_own = n_ref[own, :]
            dr = row_standard_back(dh * g_ref[...], standard_own, s_ref[own, 0:1])
            dr_ref[own, :] = dr
            low = dr.astype(BF16)
            do_ref[own, :] = low
            sums_ref[0:1, :] += jnp.sum(dh * standard_own, axis=0, keepdims=True)
            sums_ref[1:2, :] += jnp.sum(dh, axis=0, keepdims=True)
            sums_ref[2:3, :] += jnp.sum(low.astype(F32), axis=0, keepdims=True)
            return carry

        lax.fori_loop(0, rows // block, row, 0)
        wait_load(out, out_sem)
        grad = dot_nt(do_ref[:, :BLOCK], out[0])
        for t in range(1, weight_out.blocks):
            grad = grad + dot_nt(do_ref[:, t * BLOCK : (t + 1) * BLOCK], out[t])
        da_ref[...] = grad.astype(BF16)

    return run_kernel(
        body,
        "norm_back",
        [vmem(du), vmem(dr2), vmem(standard), vmem(inverse), vmem(gain)]
        + weight_up.ins()
        + weight_out.ins()
        + [loose(array) for array in ready],
        [
            ((rows, D), F32, True),
            ((rows, D), BF16, True),
            ((rows, D), BF16, True),
            ((8, D), F32, True),
        ],
        weight_up.scratch() + weight_out.scratch() + [pltpu.VMEM((rows, D), F32)],
        11,
    )


def attention_back(
    queries, key_values, d_attended, attended, lse, mask, cosine, sine, part, ready
):
    rows = queries.shape[0]
    n_kv = len(key_values)
    block = min(rows, 256)
    scale = 1.0 / math.sqrt(HD)

    def body(*refs):
        q_ref, da_ref, a_ref, lse_ref, mask_ref, cos_ref, sin_ref = refs[:7]
        k_refs = refs[7 : 7 + n_kv]
        v_refs = refs[7 + n_kv : 7 + 2 * n_kv]
        dq_ref, *dkv_refs = refs[7 + 2 * n_kv + len(ready) :]
        lanes = lax.broadcasted_iota(jnp.int32, (rows, 128), 1)
        picks = lax.broadcasted_iota(jnp.int32, (8, 128), 1) // HD
        chosen = (picks == lax.broadcasted_iota(jnp.int32, (8, 128), 0)).astype(F32)
        for p in range(PART // 128):
            at = slice(p * 128, (p + 1) * 128)
            v_at = slice(PART + p * 128, PART + (p + 1) * 128)
            q_pair = q_ref[:, at].astype(F32)
            da_pair = da_ref[:, at].astype(F32)
            dots = lax.dot_general(
                chosen,
                da_pair * a_ref[:, at].astype(F32),
                (((1,), (1,)), ((), ())),
                precision=lax.Precision.HIGHEST,
                preferred_element_type=F32,
            )
            q_heads = [
                jnp.where(lanes // HD == head, q_pair, 0.0).astype(BF16) for head in range(2)
            ]
            da_heads = [
                jnp.where(lanes // HD == head, da_pair, 0.0).astype(BF16) for head in range(2)
            ]
            lse_rows = [lse_ref[2 * p + head : 2 * p + head + 1, :] for head in range(2)]
            dq_heads = [None, None]
            for g in range(n_kv):
                for b in range(rows // block):
                    own = slice(b * block, (b + 1) * block)
                    keys = k_refs[g][own, at]
                    values = v_refs[g][own, at]
                    hidden = mask_ref[g * rows + b * block : g * rows + (b + 1) * block, 0:1]
                    dk, dv = None, None
                    for head in range(2):
                        s = dot_nt(keys, q_heads[head]) + hidden
                        prob = jnp.exp(s - lse_rows[head])
                        dp = dot_nt(values, da_heads[head])
                        ds = (prob * (dp - dots[head : head + 1, :])).astype(BF16)
                        dv_part = dot_nn(prob.astype(BF16), da_heads[head])
                        dk_part = dot_nn(ds, q_heads[head])
                        dq_part = dot_tn(keys, ds)
                        dv = dv_part if dv is None else dv + dv_part
                        dk = dk_part if dk is None else dk + dk_part
                        dq_heads[head] = (
                            dq_part if dq_heads[head] is None else dq_heads[head] + dq_part
                        )
                    kind = F32 if g == 0 else BF16
                    dkv_refs[g][own, at] = dk.astype(kind)
                    dkv_refs[g][own, v_at] = dv.astype(kind)
            flipped = lax.broadcasted_iota(jnp.int32, (128, rows), 0)
            dq = jnp.transpose(jnp.where(flipped < HD, dq_heads[0], dq_heads[1])) * scale
            dq_ref[:, at] = turned(dq, cos_ref[...], -sin_ref[...]).astype(BF16)

    return run_kernel(
        body,
        "attention_back",
        [
            lane_block(queries, PART, part),
            lane_block(d_attended, PART, part),
            lane_block(attended, PART, part),
            vmem(lse),
            vmem(mask),
            vmem(cosine),
            vmem(sine),
        ]
        + [lane_block(kv, PART, part) for kv in key_values]
        + [lane_block(kv, PART, part + D // PART) for kv in key_values]
        + [loose(array) for array in ready],
        [((rows, PART), BF16, True)]
        + [((rows, 2 * PART), F32 if g == 0 else BF16, True) for g in range(n_kv)],
        [],
        8,
        grid=(1,),
    )


def join_qkv(parts, cosine, sine, ready):
    rows = parts[0][0].shape[0]
    n_each = len(parts[0])

    def body(*refs):
        cos_ref, sin_ref = refs[:2]
        part_refs = refs[2 : 2 + n_each * len(parts)]
        out_ref, sums_ref = refs[2 + n_each * len(parts) + len(ready) :]
        sums_ref[...] = jnp.zeros_like(sums_ref)
        cos, sin = cos_ref[...], -sin_ref[...]

        def put(at, low):
            out_ref[:, at : at + 128] = low
            sums_ref[0:1, at : at + 128] = jnp.sum(low.astype(F32), axis=0, keepdims=True)

        for k in range(len(parts)):
            dq_ref, dkv_ref, *got_refs = part_refs[k * n_each : (k + 1) * n_each]
            for at in range(0, PART, 128):
                put(k * PART + at, dq_ref[:, at : at + 128])
            for at in range(0, 2 * PART, 128):
                value = dkv_ref[:, at : at + 128]
                for got in got_refs:
                    value = value + got[:, at : at + 128].astype(F32)
                if at < PART:
                    put(D + k * PART + at, turned(value, cos, sin).astype(BF16))
                else:
                    put(2 * D + k * PART + at - PART, value.astype(BF16))

    return run_kernel(
        body,
        "join_qkv",
        [vmem(cosine), vmem(sine)]
        + [vmem(array) for part in parts for array in part]
        + [loose(array) for array in ready],
        [((rows, 3 * D), BF16, True), ((8, 3 * D), F32, True)],
        [],
        4,
    )


def input_back(dproj, weight, dr1, sums, width, part_rows, ready):
    rows = dproj.shape[0]
    n = rows // part_rows
    n_w = weight.count()
    n_s = len(sums)

    def body(*refs):
        dp_ref, dr_ref = refs[:2]
        sum_refs = refs[2 : 2 + n_s]
        w_refs = refs[2 + n_s : 2 + n_s + n_w]
        out_ref, held, sem, shares = refs[2 + n_s + n_w + len(ready) :]
        weight.start(w_refs, held, sem)
        shares[...] = jnp.zeros_like(shares)
        if n <= 64:
            for place, (_, line), ref in zip(range(n_s), sums, sum_refs):
                size = ref.shape[1] // n
                row, column = place % part_rows, place // part_rows * 128
                for k in range(n):
                    at = k * part_rows + row
                    shares[at : at + 1, column : column + size] = ref[
                        line : line + 1, k * size : (k + 1) * size
                    ]
        out_ref[:, D:] = shares[...].astype(BF16)
        wait_load(held, sem)
        grad = dr_ref[...]
        for t in range(weight.blocks):
            grad = grad + dot_nt(dp_ref[:, t * BLOCK : (t + 1) * BLOCK], held[t])
        out_ref[:, :D] = grad.astype(BF16)

    result = run_kernel(
        body,
        "input_back",
        [vmem(dproj), vmem(dr1)]
        + [vmem(array) for array, _ in sums]
        + weight.ins()
        + [loose(array) for array in ready],
        [((rows, width), BF16, True)],
        weight.scratch() + [pltpu.VMEM((rows, width - D), F32)],
        6,
    )[0]
    if n <= 64:
        return result
    shares = []
    for array, line in sums:
        size = array.shape[1] // n
        shares.append(jnp.pad(array[line].reshape(n, size), ((0, 0), (0, 128 - size))))
    spare = -len(shares) % part_rows
    shares = jnp.stack(shares + [jnp.zeros_like(shares[0])] * spare, axis=1)
    shares = shares.reshape(n, -1, part_rows, 128).transpose(0, 2, 1, 3).reshape(rows, -1)
    return jnp.concatenate([result[:, :D], shares.astype(BF16)], axis=1)


def unpack_vectors(moved, sizes, part_rows):
    rows = moved.shape[0]
    n = rows // part_rows
    if n > 64:
        shares = moved[:, D:].astype(F32).reshape(n, part_rows, -1, 128).transpose(0, 2, 1, 3)
        shares = shares.reshape(n, -1, 128)
        return [shares[:, k, :size].reshape(1, -1) for k, size in enumerate(sizes)]

    def body(moved_ref, *refs):
        shares = refs[-1]
        shares[...] = moved_ref[...].astype(F32)
        for place, (size, ref) in enumerate(zip(sizes, refs)):
            for k in range(n):
                at = k * part_rows + place
                ref[0:1, k * size : (k + 1) * size] = shares[at : at + 1, :size]

    return run_kernel(
        body,
        "unpack_vectors",
        [lane_block(moved, 128, D // 128)],
        [((1, n * size), F32, True) for size in sizes],
        [pltpu.VMEM((rows, 128), F32)],
        2,
        grid=(1,),
    )


def split_grad(products, table, chips, direct, name, micros, ready):
    height = D
    blocks = [right.shape[1] // 2 // BLOCK for _, right in products]
    count = chips if direct else 1
    size = height // count
    total = sum(blocks)
    shape = (count, total, size, BLOCK)

    def body(*refs):
        pair_refs = refs[: 2 * len(products)]
        table_ref = refs[2 * len(products)]
        par_ref, own_ref, held, par_sem, own_sem = refs[2 * len(products) + 1 + len(ready) :]
        core = table_ref[2 * count]
        for turn, (out, sem) in enumerate(((par_ref, par_sem), (own_ref, own_sem))):
            half = 1 - core if turn == 0 else core
            done = 0
            for k, number in enumerate(blocks):
                left_ref, right_ref = pair_refs[2 * k : 2 * k + 2]

                def step(t, carry, left_ref=left_ref, right_ref=right_ref, number=number, done=done):
                    at = pl.ds(pl.multiple_of((half * number + t) * BLOCK, 128), BLOCK)
                    held[turn, done + t] = dot_tn(left_ref[...], right_ref[:, at]).astype(BF16)
                    return carry

                lax.fori_loop(0, number, step, 0)
                done += number
            for k in range(count):
                pltpu.make_async_copy(
                    held.at[turn, :, pl.ds(k * size, size)],
                    out.at[table_ref[turn * count + k]],
                    sem,
                ).start()
        pltpu.make_async_copy(par_ref, par_ref, par_sem).wait()
        pltpu.make_async_copy(own_ref, own_ref, own_sem).wait()

    return run_kernel(
        body,
        name,
        [
            spec
            for left, right in products
            for spec in (lane_block(left, D, 0), vmem(right))
        ]
        + [smem(table)]
        + [loose(array) for array in ready],
        [(shape, BF16, False), (shape, BF16, False)],
        [
            pltpu.VMEM((2, total, height, BLOCK), BF16),
            pltpu.SemaphoreType.DMA(()),
            pltpu.SemaphoreType.DMA(()),
        ],
        micros,
        grid=(1,),
    )


def row_grad(left, right, table, chips, direct, name):
    height = left.shape[1]
    blocks = right.shape[1] // BLOCK
    tile = 768
    size = height // chips // 2
    shape = (chips, blocks, size, BLOCK)
    per_tile = tile // (2 * size)

    def body(left_ref, right_ref, table_ref, par_ref, own_ref, held, par_sem, own_sem):
        core = table_ref[2 * chips]

        def step(t, carry):
            at = pl.ds(pl.multiple_of(t * tile, tile), tile)
            grad = dot_tn(left_ref[:, at], right_ref[...]).astype(BF16)
            for k in range(blocks):
                held[k, at, :] = grad[:, k * BLOCK : (k + 1) * BLOCK]
            for k in range(per_tile):
                chip = t * per_tile + k
                for turn, (out, sem) in enumerate(((par_ref, par_sem), (own_ref, own_sem))):
                    part = 1 - core if turn == 0 else core
                    start = pl.multiple_of((2 * chip + part) * size, 16)
                    pltpu.make_async_copy(
                        held.at[:, pl.ds(start, size)],
                        out.at[table_ref[turn * chips + chip]],
                        sem,
                    ).start()
            return carry

        lax.fori_loop(0, height // tile, step, 0)
        pltpu.make_async_copy(par_ref, par_ref, par_sem).wait()
        pltpu.make_async_copy(own_ref, own_ref, own_sem).wait()

    def whole(left_ref, right_ref, table_ref, out_ref):
        for t in range(height // tile):
            at = slice(t * tile, (t + 1) * tile)
            out_ref[at, :] = dot_tn(left_ref[:, at], right_ref[...]).astype(BF16)

    if not direct:
        return run_kernel(
            whole,
            name,
            [vmem(left), vmem(right), smem(table)],
            [((height, right.shape[1]), BF16, True)],
            [],
            6,
        )
    return run_kernel(
        body,
        name,
        [vmem(left), vmem(right), smem(table)],
        [(shape, BF16, False), (shape, BF16, False)],
        [
            pltpu.VMEM((blocks, height, BLOCK), BF16),
            pltpu.SemaphoreType.DMA(()),
            pltpu.SemaphoreType.DMA(()),
        ],
        6,
    )


def body(
    tokens,
    lengths,
    deal,
    w_qkv,
    b_qkv,
    w_out,
    b_out,
    norm1_gain,
    norm1_bias,
    w_up,
    b_up,
    w_down,
    b_down,
    norm2_gain,
    norm2_bias,
    cotangent,
):
    n_dp = lax.axis_size("dp")
    n_fsdp = lax.axis_size("fsdp")
    plan = Plan(n_dp, n_fsdp)
    n, chips = plan.n, plan.chips
    dp_place = lax.axis_index("dp")
    fsdp_place = lax.axis_index("fsdp")
    me = dp_place * n_fsdp + fsdp_place
    core = me % 2
    batches, slot_count, home_rows, width = tokens.shape
    group = n_fsdp // batches
    part_rows = home_rows // group
    rows = n * part_rows
    local = fsdp_place % group
    batch_place = fsdp_place // group
    mine = plan.order(me, core)
    other = plan.order(me, 1 - core)
    mine_place = plan.places(me, core)
    other_place = plan.places(me, 1 - core)
    stores = jnp.concatenate([other_place, mine_place, core[None]]).astype(jnp.int32)
    group_pairs = [
        [(i, i - i % group + (i + k) % group) for i in range(n)] for k in range(1, group)
    ]
    back_pairs = [[(b, a) for a, b in pairs] for pairs in group_pairs]

    def to_parts(array):
        parts = array.reshape(batches, slot_count, group, part_rows, width)
        return parts.transpose(1, 0, 2, 3, 4).reshape(n, part_rows, width)

    def exchange(parts):
        moved = lax.all_to_all(parts, AXES, split_axis=0, concat_axis=0, tiled=True)
        return moved.reshape(rows, -1)

    def from_parts(moved):
        moved = moved.reshape(slot_count, batches, group, part_rows, width)
        return moved.transpose(1, 0, 2, 3, 4).reshape(batches, slot_count, home_rows, width)

    def by_blocks(shard, columns):
        return shard.reshape(-1, columns // BLOCK, BLOCK).transpose(1, 0, 2)

    def whole(parts, place):
        joined = jnp.concatenate(parts)[place].transpose(1, 0, 2, 3)
        return joined.reshape(1, joined.shape[0], -1, BLOCK)

    def split_parts(gather):
        if gather.own[0].shape[2] % 16 == 0:
            return gather.own + gather.par
        return [whole(gather.own, mine_place), whole(gather.par, other_place)]

    def split_weight(parts, first, number):
        count = sum(part.shape[0] for part in parts) // 2
        size = parts[0].shape[2]
        spots = [mine, other] if count == chips else [jnp.zeros((1,), jnp.int32)] * 2
        tables = []
        for half, spot in zip((core, 1 - core), spots):
            tables.append(jnp.stack([jnp.full((count,), half * number), spot * size], axis=1))
        places = jnp.concatenate(tables).reshape(-1).astype(jnp.int32)
        return Weight([(part, first, number) for part in parts], places, 2 * number, D)

    def row_weight(gather):
        own, par = gather.own, gather.par
        _, number, size, _ = own[0].shape
        if size % 16 == 0:
            starts = jnp.concatenate([mine * 2 + core, other * 2 + 1 - core]) * size
            places = jnp.stack([jnp.zeros_like(starts), starts], axis=1).reshape(-1)
            sources = [(part, 0, number) for part in own + par]
        else:
            own = jnp.concatenate(own)[mine_place]
            par = jnp.concatenate(par)[other_place]
            both = jnp.where(core == 0, jnp.stack([own, par], 2), jnp.stack([par, own], 2))
            both = both.transpose(1, 0, 2, 3, 4).reshape(1, number, -1, BLOCK)
            places = jnp.zeros((2,), jnp.int32)
            sources = [(both, 0, number)]
        return Weight(sources, places.astype(jnp.int32), number, n * size)

    def split_pieces(products, name, micros, ready=()):
        size = D // chips
        if size % 16 == 0:
            return split_grad(products, stores, chips, True, name, micros, ready)
        table = jnp.concatenate([jnp.zeros((2,), jnp.int32), core[None].astype(jnp.int32)])
        par, own = split_grad(products, table, chips, False, name, micros, ready)

        def cut(array, order):
            return array.reshape(-1, chips, size, BLOCK).transpose(1, 0, 2, 3)[order]

        return cut(par, other), cut(own, mine)

    def split_result(block, numbers):
        halves = unsplit_columns(plan, core, block)
        results, at = [], 0
        for number in numbers:
            both = jnp.concatenate([half[at : at + number] for half in halves])
            results.append(both.transpose(1, 0, 2).reshape(-1))
            at += number
        return results

    def row_pieces(left, right, name):
        size = FF // n
        if size % 16 == 0:
            return row_grad(left, right, stores, chips, True, name)
        both = row_grad(left, right, stores, chips, False, name)[0]
        blocks = both.reshape(chips, 2, size, -1, BLOCK).transpose(0, 1, 3, 2, 4)
        par = jnp.where(core == 0, blocks[:, 1], blocks[:, 0])[other]
        own = jnp.where(core == 0, blocks[:, 0], blocks[:, 1])[mine]
        return par, own

    small_shards = (
        b_qkv,
        b_out,
        norm1_gain,
        norm1_bias,
        b_up,
        b_down,
        norm2_gain,
        norm2_bias,
    )
    sizes = [piece.shape[0] for piece in small_shards]
    spare = -len(sizes) % part_rows
    shares = [jnp.pad(piece[None], ((0, 0), (0, 128 - piece.shape[0]))) for piece in small_shards]
    shares = jnp.concatenate(shares + [jnp.zeros((1, 128), BF16)] * (max(spare, 0)))
    shares = shares.reshape(-1, part_rows, 128).transpose(1, 0, 2).reshape(1, part_rows, -1)
    wide = width + shares.shape[2]
    parts = jnp.concatenate(
        [to_parts(tokens), jnp.broadcast_to(shares, (n,) + shares.shape[1:])], axis=2
    )
    cuts = [by_blocks(w_qkv, 3 * D), by_blocks(w_out, D), by_blocks(w_up, FF)]
    left = jnp.concatenate([cut[: cut.shape[0] // 2] for cut in cuts])
    right = jnp.concatenate([cut[cut.shape[0] // 2 :] for cut in cuts])
    piece = split_columns(plan, core, left, right)
    n_qkv, n_out, n_up = [cut.shape[0] // 2 for cut in cuts]
    first = Gather(plan, piece[:n_qkv])
    second = Gather(plan, piece[n_qkv:])
    third = Gather(plan, by_blocks(w_down, D))
    last = plan.levels - 1
    first.step()
    parts = after(parts, first.got[0])
    block_in = exchange(parts)
    first.step()
    second.step(first.got[0])
    first.step(parts)
    for level in range(3, last):
        second.step()
        first.step()
    second.step(first.got[1])
    first.step()
    third.step(second.got[-1])
    for _ in range(1, last - 1):
        third.step()
    sent_second = second.step(first.got[-1])
    first.finish()
    qkv_weight = split_weight(split_parts(first), 0, n_qkv)
    vectors = unpack_vectors(block_in, sizes, part_rows)
    cot_parts = to_parts(cotangent)
    (qkv_bias, out_bias, gain_one, bias_one, up_bias, down_bias, gain_two, bias_two) = vectors

    own_deal = jnp.where(batch_place == 0, deal[0], deal[1])
    own_lengths = jnp.where(batch_place == 0, lengths[0], lengths[1])
    for m in range(2, batches):
        own_deal = jnp.where(batch_place == m, deal[m], own_deal)
        own_lengths = jnp.where(batch_place == m, lengths[m], own_lengths)
    seq_len = jnp.sum(jnp.where(own_deal == dp_place, own_lengths, 0))

    row_ids = jnp.arange(rows, dtype=jnp.int32)
    base_places = row_ids // part_rows * home_rows + row_ids % part_rows
    query_places = base_places + local * part_rows
    key_places = jnp.stack([base_places + (local + k) % group * part_rows for k in range(group)])
    mask = jnp.where(key_places < seq_len, 0.0, -1000000000.0).astype(F32)
    mask_columns = jnp.broadcast_to(mask.reshape(-1, 1), (group * rows, 128))
    half_lane = (jnp.arange(128) % HD // 2).astype(F32)
    frequency = 10000.0 ** (-(2.0 * half_lane) / HD)
    angles = query_places.astype(F32)[:, None] * frequency[None, :]
    cosine = jnp.cos(angles)
    sine = jnp.sin(angles) * jnp.where(jnp.arange(128) % 2 == 0, -1.0, 1.0)

    queries, key_value = qkv_forward(
        block_in, qkv_weight, qkv_bias, cosine, sine, [sent_second, cot_parts]
    )
    key_values = [key_value] + [swap(key_value, pairs) for pairs in back_pairs]
    sent = second.step(key_value)
    heads, lses = [], []
    n_parts = D // PART
    ready = [sent]
    for part in range(n_parts):
        head, lse = attention_forward(queries, key_values, mask, part, ready)
        heads.append(head)
        lses.append(lse)
        ready = []
        if part == n_parts - 2:
            second.finish(head)
            ready = [third.step(head, second.got[-1])]
    rest = split_parts(second)
    out_weight = split_weight(rest, 0, n_out)
    up_weight = split_weight(rest, n_out, n_up)
    attended, standard_one, inverse_one, normed_low = out_forward(
        block_in, heads, out_weight, [out_bias, gain_one, bias_one]
    )
    sent = third.step(normed_low)
    active, slope = up_forward(normed_low, up_weight, up_bias, [sent])
    third.finish(active)
    down_weight = row_weight(third)
    grad_top = exchange(after(cot_parts, queries))
    result, grad_two, down_grad, sums_two = down_both(
        active,
        down_weight,
        standard_one,
        grad_top,
        [gain_one, bias_one, down_bias, gain_two, bias_two],
    )
    par, own = row_pieces(active, down_grad, "down_grad")
    down_sum = Reduction(plan, par, own)
    home_out = from_parts(exchange(result.reshape(n, part_rows, width)).reshape(n, part_rows, width))
    hidden_grad, sums_up = up_back(down_grad, down_weight, slope, [par])
    sent = down_sum.step(hidden_grad)
    grad_one, branch_grad, d_attended, sums_one = norm_back(
        hidden_grad, up_weight, out_weight, grad_two, standard_one, inverse_one, gain_one, [sent]
    )
    sent = down_sum.step(grad_one)
    par, own = split_pieces(
        [(normed_low, hidden_grad), (attended, branch_grad)], "up_out_grad", 9, [sent]
    )
    up_sum = Reduction(plan, par, own)
    ready = [par, down_sum.step(own)]
    parts = []
    for part in range(n_parts):
        query_grad, *kv_grads = attention_back(
            queries,
            key_values,
            d_attended,
            attended,
            lses[part],
            mask_columns,
            cosine,
            sine,
            part,
            ready,
        )
        received = [swap(grad, pairs) for grad, pairs in zip(kv_grads[1:], group_pairs)]
        parts.append([query_grad, kv_grads[0]] + received)
        ready = []
        if part == 0:
            ready = [up_sum.step(query_grad)] + down_sum.steps_left(query_grad)
    qkv_grad, sums_qkv = join_qkv(parts, cosine, sine, [up_sum.step(query_grad)])
    par, own = split_pieces([(block_in, qkv_grad)], "qkv_grad", 5, [up_sum.step(qkv_grad)])
    qkv_sum = Reduction(plan, par, own)
    up_sum.steps_left(own)
    small_sums = [
        (sums_qkv, 0),
        (sums_one, 2),
        (sums_one, 0),
        (sums_one, 1),
        (sums_up, 0),
        (sums_two, 2),
        (sums_two, 0),
        (sums_two, 1),
    ]
    input_grad = input_back(qkv_grad, qkv_weight, grad_one, small_sums, wide, part_rows, [par])
    moved = exchange(input_grad.reshape(n, part_rows, wide)).reshape(n, part_rows, wide)
    qkv_sum.step(input_grad)
    home_grad = from_parts(moved[:, :, :width])
    summed = jnp.sum(moved[:, :, width:].astype(F32), axis=0)
    summed = summed.reshape(part_rows, -1, 128).transpose(1, 0, 2).reshape(-1, 128)
    owned = [summed[k, :size] for k, size in enumerate(sizes)]
    down_mat_grad = down_sum.finish().transpose(1, 0, 2).reshape(-1)
    up_mat_grad, out_mat_grad = split_result(up_sum.finish(), [n_up, n_out])
    (qkv_mat_grad,) = split_result(qkv_sum.finish(), [n_qkv])
    return (
        home_out,
        home_grad,
        qkv_mat_grad,
        owned[0],
        out_mat_grad,
        owned[1],
        owned[2],
        owned[3],
        up_mat_grad,
        owned[4],
        down_mat_grad,
        owned[5],
        owned[6],
        owned[7],
    )


def solution(mesh):
    rows = P(None, None, AXES, None)
    flat = P(AXES)
    in_specs = (rows, P(), P()) + (flat,) * 12 + (rows,)
    out_specs = (rows, rows) + (flat,) * 12
    return jax.shard_map(body, mesh=mesh, in_specs=in_specs, out_specs=out_specs, check_vma=False)
```

```python
import math

import jax
import jax.numpy as jnp
from jax import lax
from jax.experimental import pallas as pl
from jax.experimental.pallas import tpu as pltpu
from jax.sharding import PartitionSpec as P

D = 768
HEADS = 12
HD = 64
FF = 3072
AXES = ("dp", "fsdp")
BLOCK = 384
F32 = jnp.float32
BF16 = jnp.bfloat16


class Plan:
    def __init__(self, n_dp, n_fsdp):
        self.n = n_dp * n_fsdp
        self.chips = self.n // 2
        bits = [1 << k for k in range(1, self.n.bit_length() - 1)]
        near, far = bits[:2], bits[2:]
        first = [b | (b >> 1) if b >> 1 in far else b for b in reversed(far)]
        self.masks = [first + near[::-1], first + near]
        self.levels = len(bits)
        self.combos = []
        for masks in self.masks:
            row = []
            for rel in range(self.chips):
                total = 0
                for k in range(self.levels):
                    if rel >> k & 1:
                        total ^= masks[k]
                row.append(total)
            self.combos.append(row)

    def pairs(self, level):
        return [(i, i ^ self.masks[i & 1][level]) for i in range(self.n)]

    def core_pairs(self):
        return [(i, i ^ 1) for i in range(self.n)]

    def order(self, me, core):
        table = jnp.asarray(self.combos, jnp.int32)
        return (me ^ jnp.where(core == 0, table[0], table[1])) // 2

    def places(self, me, core):
        spots = [[0] * self.chips for _ in range(2)]
        for spot, row in zip(spots, self.combos):
            for rel, total in enumerate(row):
                spot[total // 2] = rel
        table = jnp.asarray(spots, jnp.int32)
        away = jnp.arange(self.chips, dtype=jnp.int32) ^ (me // 2)
        return jnp.where(core == 0, table[0], table[1])[away]


def swap(value, pairs):
    return lax.ppermute(value, AXES, pairs)


def after(value, *earlier):
    return lax.optimization_barrier((value,) + earlier)[0]


class Gather:
    def __init__(self, plan, piece):
        self.plan = plan
        self.held = piece[None]
        self.got = []
        self.merged = 0

    def merge(self):
        if self.merged < len(self.got):
            self.held = jnp.concatenate([self.held, self.got[-1]], axis=0)
            self.merged = len(self.got)
        return self.held

    def step(self, *earlier, late=False):
        level = len(self.got)
        if late:
            self.got[-1] = after(self.got[-1], *earlier)
        self.merge()
        if earlier and not late:
            self.held = after(self.held, *earlier)
        self.got.append(swap(self.held, self.plan.pairs(level)))
        return self.held

    def finish(self, *earlier):
        self.own = [self.held, self.got[-1]]
        if earlier:
            self.own = [after(part, *earlier) for part in self.own]
        self.par = [swap(part, self.plan.core_pairs()) for part in self.own]


class Reduction:
    def __init__(self, plan, kept, away):
        self.plan = plan
        self.kept = kept
        self.level = plan.levels - 1
        self.got = swap(away, plan.pairs(self.level))

    def step(self, *earlier):
        self.level -= 1
        if earlier:
            self.got = after(self.got, *earlier)
        half = self.kept.shape[0] // 2
        kept, got = self.kept.astype(F32), self.got.astype(F32)
        away = (kept[half:] + got[half:]).astype(BF16)
        self.got = swap(away, self.plan.pairs(self.level))
        self.kept = kept[:half] + got[:half]
        if self.level > 0:
            self.kept = after(self.kept.astype(BF16))
        return away

    def steps_left(self, *earlier):
        return [self.step(*earlier) for _ in range(self.level)]

    def finish(self, *earlier):
        self.steps_left()
        if earlier:
            self.got = after(self.got, *earlier)
        return (self.kept + self.got.astype(F32))[0]


def split_columns(plan, core, left, right):
    keep = jnp.where(core == 0, left, right)
    got = swap(jnp.where(core == 0, right, left), plan.core_pairs())
    return jnp.where(core == 0, jnp.concatenate([keep, got], 1), jnp.concatenate([got, keep], 1))


def unsplit_columns(plan, core, block):
    rows = block.shape[1] // 2
    upper, lower = block[:, :rows], block[:, rows:]
    keep = jnp.where(core == 0, upper, lower)
    got = swap(jnp.where(core == 0, lower, upper), plan.core_pairs())
    return jnp.where(core == 0, keep, got), jnp.where(core == 0, got, keep)


def vmem(array):
    return (array, pl.BlockSpec(memory_space=pltpu.VMEM))


def smem(array):
    return (array, pl.BlockSpec(memory_space=pltpu.SMEM))


def loose(array):
    return (array, pl.BlockSpec(memory_space=pltpu.HBM))


def lane_block(array, width, place):
    return (array, pl.BlockSpec((array.shape[0], width), lambda step: (0, place)))


def run_kernel(body, name, ins, outs, scratch, micros, grid=()):
    return pl.pallas_call(
        body,
        name=name,
        grid=grid,
        in_specs=[spec for _, spec in ins],
        out_specs=[
            pl.BlockSpec(memory_space=pltpu.VMEM if inside else pl.ANY) for _, _, inside in outs
        ],
        out_shape=[jax.ShapeDtypeStruct(shape, dtype) for shape, dtype, _ in outs],
        scratch_shapes=scratch,
        compiler_params=pltpu.CompilerParams(vmem_limit_bytes=44 * 2**20),
        cost_estimate=pl.CostEstimate(
            flops=int(micros * 2.2e9), bytes_accessed=2**20, transcendentals=0
        ),
    )(*[array for array, _ in ins])


def dot_nn(left, right):
    return jnp.dot(left, right, preferred_element_type=F32)


def dot_nt(left, right):
    return lax.dot_general(left, right, (((1,), (1,)), ((), ())), preferred_element_type=F32)


def dot_tn(left, right):
    return lax.dot_general(left, right, (((0,), (0,)), ((), ())), preferred_element_type=F32)


def buffer(array):
    return [pltpu.VMEM(array.shape, array.dtype), pltpu.SemaphoreType.DMA(())]


def fetch(ref, held, sem):
    copy = pltpu.make_async_copy(ref, held, sem)
    copy.start()
    return copy


class Weight:
    def __init__(self, sources, places, blocks, height, per_column=1):
        self.sources = sources
        self.places = places
        self.blocks = blocks
        self.height = height
        self.per_column = per_column

    def ins(self):
        return [smem(self.places)] + [loose(array) for array, _, _ in self.sources]

    def scratch(self):
        return [pltpu.VMEM((self.blocks, self.height, BLOCK), BF16), pltpu.SemaphoreType.DMA((2,))]

    def count(self):
        return 1 + len(self.sources)

    def start(self, refs, held, sem):
        places, at = refs[0], 0
        for k, ((_, first, number), ref) in enumerate(zip(self.sources, refs[1:])):
            count, _, rows, _ = ref.shape
            for j in range(count):
                for turn in range(self.per_column):
                    row = pl.multiple_of(places[2 * at + 1] + turn * rows, 16)
                    share = number // self.per_column
                    pltpu.make_async_copy(
                        ref.at[j, pl.ds(first + turn * share, share)],
                        held.at[pl.ds(places[2 * at], share), pl.ds(row, rows)],
                        sem.at[2 * k // len(self.sources)],
                    ).start()
                at += 1

    def halves(self, refs, held, sem):
        number = self.blocks // 2
        total = sum(ref.shape[0] for ref in refs[1:])
        for k in range(2):
            part = held.at[pl.ds(0, number)]
            pltpu.make_async_copy(part, part, sem.at[k]).wait()
            yield refs[0][k * total]

    def wait(self, refs, held, sem):
        if len(self.sources) == 1:
            pltpu.make_async_copy(held, held, sem.at[0]).wait()
        else:
            part = held.at[:, pl.ds(0, self.height // 2)]
            for k in range(2):
                pltpu.make_async_copy(part, part, sem.at[k]).wait()


class Whole:
    def __init__(self, array):
        self.array = array

    def scratch(self, steps):
        return [pltpu.VMEM(self.array.shape, BF16), pltpu.SemaphoreType.DMA((steps,))]


def turned(values, cosine, sine):
    lanes = lax.broadcasted_iota(jnp.int32, values.shape, 1)
    swapped = jnp.where(
        lanes % 2 == 0, pltpu.roll(values, 127, 1), pltpu.roll(values, 1, 1)
    )
    return values * cosine + swapped * sine


def qkv_forward(x, weight, bias, cosine, sine, ready):
    rows = x.shape[0]
    n_w = weight.count()

    def body(*refs):
        x_ref, b_ref, cos_ref, sin_ref = refs[:4]
        w_refs = refs[4 : 4 + n_w]
        q_ref, kv_ref, whole, held, sem, whole_sem = refs[4 + n_w + len(ready) :]
        weight.start(w_refs, held, sem)
        weight.wait(w_refs, held, sem)
        whole_there = fetch(held, whole, whole_sem)
        cos, sin = cos_ref[...], sin_ref[...]
        for t in range(weight.blocks):
            y = dot_nn(x_ref[...], held[t]) + b_ref[:, t * BLOCK : (t + 1) * BLOCK]
            for g in range(BLOCK // 128):
                piece = y[:, g * 128 : (g + 1) * 128]
                at = t * BLOCK + g * 128
                if at < 2 * D:
                    piece = turned(piece, cos, sin)
                if at < D:
                    q_ref[:, at : at + 128] = (piece * (1.0 / math.sqrt(HD))).astype(BF16)
                else:
                    kv_ref[:, at - D : at - D + 128] = piece.astype(BF16)
        whole_there.wait()

    return run_kernel(
        body,
        "qkv_forward",
        [lane_block(x, D, 0), vmem(bias), vmem(cosine), vmem(sine)]
        + weight.ins()
        + [loose(array) for array in ready],
        [
            ((rows, D), BF16, True),
            ((rows, 2 * D), BF16, True),
            ((weight.blocks, D, BLOCK), BF16, False),
        ],
        weight.scratch() + [pltpu.SemaphoreType.DMA(())],
        7,
        grid=(1,),
    )


def row_standard(values):
    average = jnp.mean(values, axis=-1, keepdims=True)
    centered = values - average
    variance = jnp.mean(centered * centered, axis=-1, keepdims=True)
    inverse = lax.rsqrt(variance + 1e-05)
    return centered * inverse, inverse


def row_standard_back(grad, standard, inverse):
    mean_grad = jnp.mean(grad, axis=-1, keepdims=True)
    mean_proj = jnp.mean(grad * standard, axis=-1, keepdims=True)
    return inverse * (grad - mean_grad - standard * mean_proj)


PART = 384


def attention_forward(queries, key_values, mask, part, ready):
    rows = queries.shape[0]
    n_kv = len(key_values)
    block = min(rows, 256)

    def body(*refs):
        q_ref, mask_ref = refs[:2]
        k_refs = refs[2 : 2 + n_kv]
        v_refs = refs[2 + n_kv : 2 + 2 * n_kv]
        a_ref, lse_ref, lse_acc = refs[2 + 2 * n_kv + len(ready) :]
        lse_acc[...] = jnp.zeros_like(lse_acc)
        lanes = lax.broadcasted_iota(jnp.int32, (block, 128), 1)
        def pair(p, carry):
            at = pl.ds(pl.multiple_of(p * 128, 128), 128)
            for r in range(rows // block):
                own = slice(r * block, (r + 1) * block)
                q_pair = q_ref[own, at].astype(F32)
                heads = []
                for head in range(2):
                    q_head = jnp.where(lanes // HD == head, q_pair, 0.0).astype(BF16)
                    scores = [
                        dot_nt(q_head, key[:, at]) + mask_ref[g : g + 1, :]
                        for g, key in enumerate(k_refs)
                    ]
                    peak = scores[0].max(axis=-1, keepdims=True)
                    for s in scores[1:]:
                        peak = jnp.maximum(peak, s.max(axis=-1, keepdims=True))
                    raised = [jnp.exp(s - peak) for s in scores]
                    total = raised[0].sum(axis=-1, keepdims=True)
                    for e in raised[1:]:
                        total = total + e.sum(axis=-1, keepdims=True)
                    mixed = dot_nn(raised[0].astype(BF16), v_refs[0][:, at])
                    for e, value in zip(raised[1:], v_refs[1:]):
                        mixed = mixed + dot_nn(e.astype(BF16), value[:, at])
                    heads.append(mixed / total)
                    lse_acc[own, :] = jnp.where(
                        lanes == 2 * p + head, peak + jnp.log(total), lse_acc[own, :]
                    )
                a_ref[own, at] = jnp.where(lanes < HD, heads[0], heads[1]).astype(BF16)
            return carry

        lax.fori_loop(0, PART // 128, pair, 0)
        lse_ref[...] = jnp.transpose(lse_acc[...])[:8]

    return run_kernel(
        body,
        "attention_forward",
        [lane_block(queries, PART, part), vmem(mask)]
        + [lane_block(kv, PART, part) for kv in key_values]
        + [lane_block(kv, PART, part + D // PART) for kv in key_values]
        + [loose(array) for array in ready],
        [((rows, PART), BF16, True), ((8, rows), F32, True)],
        [pltpu.VMEM((rows, 128), F32)],
        6,
        grid=(1,),
    )


def out_forward(x, attended, weight, vectors, ready):
    rows = x.shape[0]
    n_a = len(attended)
    n_w = weight.count()
    block = min(rows, 128)

    def body(*refs):
        x_ref, ob_ref, g_ref, b_ref = refs[:4]
        part_refs = refs[4 : 4 + n_a]
        w_refs = refs[4 + n_a : 4 + n_a + n_w]
        a_ref, n_ref, s_ref, h_ref, whole, held, sem, acc, whole_sem = refs[
            4 + n_a + n_w + len(ready) :
        ]
        weight.start(w_refs, held, sem)
        for k, part in enumerate(part_refs):
            a_ref[:, k * PART : (k + 1) * PART] = part[...]
        weight.wait(w_refs, held, sem)
        whole_there = fetch(held, whole, whole_sem)
        for t in range(weight.blocks):
            acc[:, t * BLOCK : (t + 1) * BLOCK] = dot_nn(a_ref[...], held[t])

        def row(r, carry):
            own = pl.ds(pl.multiple_of(r * block, block), block)
            branch = acc[own, :] + ob_ref[...]
            standard, inverse = row_standard(x_ref[own, :].astype(F32) + branch)
            n_ref[own, :] = standard
            s_ref[own, :] = jnp.broadcast_to(inverse, (block, 128))
            h_ref[own, :] = (standard * g_ref[...] + b_ref[...]).astype(BF16)
            return carry

        lax.fori_loop(0, rows // block, row, 0)
        whole_there.wait()

    return run_kernel(
        body,
        "out_forward",
        [lane_block(x, D, 0)]
        + [vmem(v) for v in vectors]
        + [vmem(part) for part in attended]
        + weight.ins()
        + [loose(array) for array in ready],
        [
            ((rows, D), BF16, True),
            ((rows, D), F32, True),
            ((rows, 128), F32, True),
            ((rows, D), BF16, True),
            ((weight.blocks, D, BLOCK), BF16, False),
        ],
        weight.scratch() + [pltpu.VMEM((rows, D), F32), pltpu.SemaphoreType.DMA(())],
        4,
        grid=(1,),
    )


def bell(u):
    size = jnp.abs(u)
    t = 1.0 / (1.0 + (0.3275911 / math.sqrt(2.0)) * size)
    raised = jnp.exp(-0.5 * u * u)
    poly = 0.5 * 1.061405429
    for c in (-1.453152027, 1.421413741, -0.284496736, 0.254829592):
        poly = poly * t + 0.5 * c
    tail = poly * t * raised
    return jnp.where(u >= 0.0, 1.0 - tail, tail), raised


def up_forward(h, weight, bias, ready):
    rows = h.shape[0]
    n_w = weight.count()

    def body(*refs):
        h_ref, b_ref = refs[:2]
        w_refs = refs[2 : 2 + n_w]
        g_out, slope_out, whole, *scratch = refs[2 + n_w + len(ready) :]
        held, sem, g_ref, g_sem, slope_ref, slope_sem, whole_sem = scratch
        weight.start(w_refs, held, sem)
        for first in weight.halves(w_refs, held, sem):
            part = pl.ds(first, weight.blocks // 2)
            pltpu.make_async_copy(held.at[part], whole.at[part], whole_sem).start()

            def step(t, carry, first=first):
                at = pl.ds(pl.multiple_of((first + t) * BLOCK, 128), BLOCK)
                u = dot_nn(h_ref[...], held[first + t]) + b_ref[:, at]
                share, raised = bell(u)
                g_ref[:, at] = (u * share).astype(BF16)
                slope_ref[:, at] = (
                    share + u * raised * (1.0 / math.sqrt(2.0 * math.pi))
                ).astype(BF16)
                pltpu.make_async_copy(g_ref.at[:, at], g_out.at[:, at], g_sem).start()
                pltpu.make_async_copy(slope_ref.at[:, at], slope_out.at[:, at], slope_sem).start()
                return carry

            lax.fori_loop(0, weight.blocks // 2, step, 0)
        pltpu.make_async_copy(held, whole, whole_sem).wait()
        pltpu.make_async_copy(g_ref, g_out, g_sem).wait()
        pltpu.make_async_copy(slope_ref, slope_out, slope_sem).wait()

    wide = jax.ShapeDtypeStruct((rows, FF), BF16)
    return run_kernel(
        body,
        "up_forward",
        [vmem(h), vmem(bias)] + weight.ins() + [loose(array) for array in ready],
        [
            ((rows, FF), BF16, False),
            ((rows, FF), BF16, False),
            ((weight.blocks, D, BLOCK), BF16, False),
        ],
        weight.scratch() + buffer(wide) + buffer(wide) + [pltpu.SemaphoreType.DMA(())],
        12,
    )


def down_both(active, weight, standard_one, cot, vectors):
    rows = active.shape[0]
    n_w = weight.count()
    block = min(rows, 128)

    def body(*refs):
        g_in, n_in, cot_in, g1_ref, b1_ref, db_ref, g2_ref, b2_ref = refs[:8]
        w_refs = refs[8 : 8 + n_w]
        out_ref, dr_ref, dz_ref, sums_ref, whole, held, sem, z_ref = refs[8 + n_w : 16 + n_w]
        g_ref, g_sem, n_ref, n_sem, cot_ref, cot_sem, whole_sem = refs[16 + n_w :]
        active_there = fetch(g_in, g_ref, g_sem)
        weight.start(w_refs, held, sem)
        others_there = [fetch(n_in, n_ref, n_sem), fetch(cot_in, cot_ref, cot_sem)]
        active_there.wait()
        weight.wait(w_refs, held, sem)
        whole_there = fetch(held, whole, whole_sem)
        for t in range(weight.blocks):
            z_ref[:, t * BLOCK : (t + 1) * BLOCK] = dot_nn(g_ref[...], held[t])
        for there in others_there:
            there.wait()
        sums_ref[...] = jnp.zeros_like(sums_ref)

        def row(r, carry):
            own = pl.ds(pl.multiple_of(r * block, block), block)
            h = n_ref[own, :] * g1_ref[...] + b1_ref[...]
            standard, inverse = row_standard(h + z_ref[own, :] + db_ref[...])
            out_ref[own, :] = (standard * g2_ref[...] + b2_ref[...]).astype(BF16)
            dy = cot_ref[own, :].astype(F32)
            dr = row_standard_back(dy * g2_ref[...], standard, inverse)
            dr_ref[own, :] = dr
            low = dr.astype(BF16)
            dz_ref[own, :] = low
            sums_ref[0:1, :] += jnp.sum(dy * standard, axis=0, keepdims=True)
            sums_ref[1:2, :] += jnp.sum(dy, axis=0, keepdims=True)
            sums_ref[2:3, :] += jnp.sum(low.astype(F32), axis=0, keepdims=True)
            return carry

        lax.fori_loop(0, rows // block, row, 0)
        whole_there.wait()

    return run_kernel(
        body,
        "down_both",
        [loose(active), loose(standard_one), loose(cot)]
        + [vmem(v) for v in vectors]
        + weight.ins(),
        [
            ((rows, D), BF16, True),
            ((rows, D), F32, True),
            ((rows, D), BF16, True),
            ((8, D), F32, True),
            ((weight.blocks, FF, BLOCK), BF16, False),
        ],
        weight.scratch()
        + [pltpu.VMEM((rows, D), F32)]
        + buffer(active)
        + buffer(standard_one)
        + buffer(cot)
        + [pltpu.SemaphoreType.DMA(())],
        10,
    )


def middle_back(dz, slope, down, up, out, dr2, standard, inverse, gain, ready):
    rows = dz.shape[0]
    block = min(rows, 128)
    steps = FF // BLOCK

    def body(*refs):
        dz_ref, slope_in, down_in, up_in, out_in, dr2_in, n_in, s_in, g_ref = refs[:9]
        rest = refs[9 + len(ready) :]
        du_out, up_sums_ref, dr_ref, do_ref, da_ref, sums_ref = rest[:6]
        down_w, down_sem, up_w, up_sem, out_w, out_sem = rest[6:12]
        slope_ref, slope_sem, du_ref, du_sem = rest[12:16]
        acc, acc_sem, n_ref, n_sem, s_ref, s_sem, slope_sems = rest[16:]
        del slope_sem
        for t in range(steps):
            at = slice(t * BLOCK, (t + 1) * BLOCK)
            fetch(down_in.at[:, at], down_w.at[:, at], down_sem.at[t])
            fetch(slope_in.at[:, at], slope_ref.at[:, at], slope_sems.at[t])
            fetch(up_in.at[t], up_w.at[t], up_sem.at[t])
            if t == 0:
                acc_there = fetch(dr2_in, acc, acc_sem)
        others_there = [
            fetch(n_in, n_ref, n_sem),
            fetch(s_in, s_ref, s_sem),
            fetch(out_in, out_w, out_sem.at[0]),
        ]
        up_sums_ref[...] = jnp.zeros_like(up_sums_ref)
        sums_ref[...] = jnp.zeros_like(sums_ref)
        acc_there.wait()

        def step(t, carry):
            at = pl.ds(pl.multiple_of(t * BLOCK, 128), BLOCK)
            pltpu.make_async_copy(down_in.at[:, at], down_w.at[:, at], down_sem.at[t]).wait()
            pltpu.make_async_copy(slope_in.at[:, at], slope_ref.at[:, at], slope_sems.at[t]).wait()
            grad = dot_nt(dz_ref[:, :BLOCK], down_w[0, at, :])
            for k in range(1, D // BLOCK):
                grad = grad + dot_nt(dz_ref[:, k * BLOCK : (k + 1) * BLOCK], down_w[k, at, :])
            du = (grad * slope_ref[:, at].astype(F32)).astype(BF16)
            du_ref[:, at] = du
            pltpu.make_async_copy(du_ref.at[:, at], du_out.at[:, at], du_sem).start()
            up_sums_ref[0:1, at] = jnp.sum(du.astype(F32), axis=0, keepdims=True)
            pltpu.make_async_copy(up_in.at[t], up_w.at[t], up_sem.at[t]).wait()
            acc[...] += dot_nt(du, up_w[t])
            return carry

        lax.fori_loop(0, steps, step, 0)
        for there in others_there:
            there.wait()

        def row(r, carry):
            own = pl.ds(pl.multiple_of(r * block, block), block)
            dh = acc[own, :]
            standard_own = n_ref[own, :]
            dr = row_standard_back(dh * g_ref[...], standard_own, s_ref[own, 0:1])
            dr_ref[own, :] = dr
            low = dr.astype(BF16)
            do_ref[own, :] = low
            sums_ref[0:1, :] += jnp.sum(dh * standard_own, axis=0, keepdims=True)
            sums_ref[1:2, :] += jnp.sum(dh, axis=0, keepdims=True)
            sums_ref[2:3, :] += jnp.sum(low.astype(F32), axis=0, keepdims=True)
            return carry

        lax.fori_loop(0, rows // block, row, 0)
        grad = dot_nt(do_ref[:, :BLOCK], out_w[0])
        for t in range(1, D // BLOCK):
            grad = grad + dot_nt(do_ref[:, t * BLOCK : (t + 1) * BLOCK], out_w[t])
        da_ref[...] = grad.astype(BF16)
        pltpu.make_async_copy(du_ref, du_out, du_sem).wait()

    return run_kernel(
        body,
        "middle_back",
        [vmem(dz), loose(slope), loose(down.array), loose(up.array), loose(out.array)]
        + [loose(dr2), loose(standard), loose(inverse), vmem(gain)]
        + [loose(array) for array in ready],
        [
            ((rows, FF), BF16, False),
            ((8, FF), F32, True),
            ((rows, D), F32, True),
            ((rows, D), BF16, True),
            ((rows, D), BF16, True),
            ((8, D), F32, True),
        ],
        down.scratch(steps)
        + up.scratch(steps)
        + out.scratch(1)
        + buffer(slope)
        + buffer(slope)
        + buffer(dr2)
        + buffer(standard)
        + buffer(inverse)
        + [pltpu.SemaphoreType.DMA((steps,))],
        14,
    )


def attention_back(
    queries, key_values, d_attended, attended, lse, mask, cosine, sine, part, ready
):
    rows = queries.shape[0]
    n_kv = len(key_values)
    block = min(rows, 256)
    scale = 1.0 / math.sqrt(HD)

    def body(*refs):
        q_ref, da_ref, a_ref, lse_ref, mask_ref, cos_ref, sin_ref = refs[:7]
        k_refs = refs[7 : 7 + n_kv]
        v_refs = refs[7 + n_kv : 7 + 2 * n_kv]
        dq_ref, *dkv_refs = refs[7 + 2 * n_kv + len(ready) :]
        lanes = lax.broadcasted_iota(jnp.int32, (rows, 128), 1)
        picks = lax.broadcasted_iota(jnp.int32, (8, 128), 1) // HD
        chosen = (picks == lax.broadcasted_iota(jnp.int32, (8, 128), 0)).astype(F32)

        def pair(p, carry):
            at = pl.ds(pl.multiple_of(p * 128, 128), 128)
            v_at = pl.ds(pl.multiple_of(PART + p * 128, 128), 128)
            q_pair = q_ref[:, at].astype(F32)
            da_pair = da_ref[:, at].astype(F32)
            dots = lax.dot_general(
                chosen,
                da_pair * a_ref[:, at].astype(F32),
                (((1,), (1,)), ((), ())),
                precision=lax.Precision.HIGHEST,
                preferred_element_type=F32,
            )
            q_heads = [
                jnp.where(lanes // HD == head, q_pair, 0.0).astype(BF16) for head in range(2)
            ]
            da_heads = [
                jnp.where(lanes // HD == head, da_pair, 0.0).astype(BF16) for head in range(2)
            ]
            lse_rows = [lse_ref[pl.ds(2 * p + head, 1), :] for head in range(2)]
            dq_heads = [None, None]
            for g in range(n_kv):
                for b in range(rows // block):
                    own = slice(b * block, (b + 1) * block)
                    keys = k_refs[g][own, at]
                    values = v_refs[g][own, at]
                    hidden = mask_ref[g * rows + b * block : g * rows + (b + 1) * block, 0:1]
                    dk, dv = None, None
                    for head in range(2):
                        s = dot_nt(keys, q_heads[head]) + hidden
                        prob = jnp.exp(s - lse_rows[head])
                        dp = dot_nt(values, da_heads[head])
                        ds = (prob * (dp - dots[head : head + 1, :])).astype(BF16)
                        dv_part = dot_nn(prob.astype(BF16), da_heads[head])
                        dk_part = dot_nn(ds, q_heads[head])
                        dq_part = dot_tn(keys, ds)
                        dv = dv_part if dv is None else dv + dv_part
                        dk = dk_part if dk is None else dk + dk_part
                        dq_heads[head] = (
                            dq_part if dq_heads[head] is None else dq_heads[head] + dq_part
                        )
                    kind = F32 if g == 0 else BF16
                    dkv_refs[g][own, at] = dk.astype(kind)
                    dkv_refs[g][own, v_at] = dv.astype(kind)
            flipped = lax.broadcasted_iota(jnp.int32, (128, rows), 0)
            dq = jnp.transpose(jnp.where(flipped < HD, dq_heads[0], dq_heads[1])) * scale
            dq_ref[:, at] = turned(dq, cos_ref[...], -sin_ref[...]).astype(BF16)
            return carry

        lax.fori_loop(0, PART // 128, pair, 0)

    return run_kernel(
        body,
        "attention_back",
        [
            lane_block(queries, PART, part),
            lane_block(d_attended, PART, part),
            lane_block(attended, PART, part),
            vmem(lse),
            vmem(mask),
            vmem(cosine),
            vmem(sine),
        ]
        + [lane_block(kv, PART, part) for kv in key_values]
        + [lane_block(kv, PART, part + D // PART) for kv in key_values]
        + [loose(array) for array in ready],
        [((rows, PART), BF16, True)]
        + [((rows, 2 * PART), F32 if g == 0 else BF16, True) for g in range(n_kv)],
        [],
        8,
        grid=(1,),
    )


def join_qkv(parts, cosine, sine, ready):
    rows = parts[0][0].shape[0]
    n_each = len(parts[0])

    def body(*refs):
        cos_ref, sin_ref = refs[:2]
        part_refs = refs[2 : 2 + n_each * len(parts)]
        out_ref, sums_ref = refs[2 + n_each * len(parts) + len(ready) :]
        sums_ref[...] = jnp.zeros_like(sums_ref)
        cos, sin = cos_ref[...], -sin_ref[...]

        def put(at, low):
            out_ref[:, at : at + 128] = low
            sums_ref[0:1, at : at + 128] = jnp.sum(low.astype(F32), axis=0, keepdims=True)

        for k in range(len(parts)):
            dq_ref, dkv_ref, *got_refs = part_refs[k * n_each : (k + 1) * n_each]
            for at in range(0, PART, 128):
                put(k * PART + at, dq_ref[:, at : at + 128])
            for at in range(0, 2 * PART, 128):
                value = dkv_ref[:, at : at + 128]
                for got in got_refs:
                    value = value + got[:, at : at + 128].astype(F32)
                if at < PART:
                    put(D + k * PART + at, turned(value, cos, sin).astype(BF16))
                else:
                    put(2 * D + k * PART + at - PART, value.astype(BF16))

    return run_kernel(
        body,
        "join_qkv",
        [vmem(cosine), vmem(sine)]
        + [vmem(array) for part in parts for array in part]
        + [loose(array) for array in ready],
        [((rows, 3 * D), BF16, True), ((8, 3 * D), F32, True)],
        [],
        4,
    )


def input_back(dproj, weight, dr1, sums, width, part_rows, ready):
    rows = dproj.shape[0]
    n = rows // part_rows
    blocks = weight.array.shape[0]
    n_s = len(sums)

    def body(*refs):
        dp_ref, dr_in = refs[:2]
        sum_refs = refs[2 : 2 + n_s]
        w_in = refs[2 + n_s]
        out_ref, held, sem, shares, dr_ref, dr_sem = refs[3 + n_s + len(ready) :]
        there = [fetch(w_in.at[t], held.at[t], sem.at[t]) for t in range(blocks)]
        dr_there = fetch(dr_in, dr_ref, dr_sem)
        shares[...] = jnp.zeros_like(shares)
        if n <= 64:
            for place, (_, line), ref in zip(range(n_s), sums, sum_refs):
                size = ref.shape[1] // n
                row, column = place % part_rows, place // part_rows * 128
                for k in range(n):
                    at = k * part_rows + row
                    shares[at : at + 1, column : column + size] = ref[
                        line : line + 1, k * size : (k + 1) * size
                    ]
        out_ref[:, D:] = shares[...].astype(BF16)
        dr_there.wait()
        grad = dr_ref[...]
        for t in range(blocks):
            there[t].wait()
            grad = grad + dot_nt(dp_ref[:, t * BLOCK : (t + 1) * BLOCK], held[t])
        out_ref[:, :D] = grad.astype(BF16)

    result = run_kernel(
        body,
        "input_back",
        [vmem(dproj), loose(dr1)]
        + [vmem(array) for array, _ in sums]
        + [loose(weight.array)]
        + [loose(array) for array in ready],
        [((rows, width), BF16, True)],
        weight.scratch(blocks) + [pltpu.VMEM((rows, width - D), F32)] + buffer(dr1),
        6,
    )[0]
    if n <= 64:
        return result
    shares = []
    for array, line in sums:
        size = array.shape[1] // n
        shares.append(jnp.pad(array[line].reshape(n, size), ((0, 0), (0, 128 - size))))
    spare = -len(shares) % part_rows
    shares = jnp.stack(shares + [jnp.zeros_like(shares[0])] * spare, axis=1)
    shares = shares.reshape(n, -1, part_rows, 128).transpose(0, 2, 1, 3).reshape(rows, -1)
    return jnp.concatenate([result[:, :D], shares.astype(BF16)], axis=1)


def unpack_vectors(moved, sizes, part_rows):
    rows = moved.shape[0]
    n = rows // part_rows
    if n > 64:
        shares = moved[:, D:].astype(F32).reshape(n, part_rows, -1, 128).transpose(0, 2, 1, 3)
        shares = shares.reshape(n, -1, 128)
        return [shares[:, k, :size].reshape(1, -1) for k, size in enumerate(sizes)]

    def body(moved_ref, *refs):
        shares = refs[-1]
        shares[...] = moved_ref[...].astype(F32)
        for place, (size, ref) in enumerate(zip(sizes, refs)):
            for k in range(n):
                at = k * part_rows + place
                ref[0:1, k * size : (k + 1) * size] = shares[at : at + 1, :size]

    return run_kernel(
        body,
        "unpack_vectors",
        [lane_block(moved, 128, D // 128)],
        [((1, n * size), F32, True) for size in sizes],
        [pltpu.VMEM((rows, 128), F32)],
        2,
        grid=(1,),
    )


def split_grad(products, table, turn, got, chips, direct, name, micros, ready):
    height = D
    rows = products[0][0].shape[0]
    blocks = [right.shape[1] // 2 // BLOCK for _, right in products]
    count = chips if direct else 1
    size = height // count
    total = sum(blocks)
    extra = [] if got is None else [loose(got)]
    parts = 2 if direct and got is not None else 1

    def body(*refs):
        pair_refs = refs[: 2 * len(products)]
        table_ref = refs[2 * len(products)]
        got_refs = refs[2 * len(products) + 1 :][: len(extra)]
        rest = refs[2 * len(products) + 1 + len(extra) + len(ready) :]
        outs, (held, sem, other, other_sem, columns, column_sems) = rest[:parts], rest[parts:]
        core = table_ref[2 * count]
        half = 1 - core if turn == 0 else core
        column_there = []
        for k, number in enumerate(blocks):
            for t in range(number):
                at = pl.ds(pl.multiple_of((half * number + t) * BLOCK, 128), BLOCK)
                spot = len(column_there)
                column_there.append(
                    fetch(
                        pair_refs[2 * k + 1].at[:, at], columns.at[spot], column_sems.at[spot]
                    )
                )
        for got_ref in got_refs:
            for k in range(count):
                pltpu.make_async_copy(
                    got_ref.at[table_ref[turn * count + k]],
                    other.at[:, pl.ds(k * size, size)],
                    other_sem,
                ).start()
        done = 0
        for k, number in enumerate(blocks):
            left_ref = pair_refs[2 * k]
            for t in range(number):
                column_there[done].wait()
                grad = dot_tn(left_ref[...], columns[done])
                if got_refs:
                    if done == 0:
                        pltpu.make_async_copy(other, other, other_sem).wait()
                    grad = grad + other[done].astype(F32)
                held[done] = grad.astype(BF16)
                done += 1
        for k in range(count):
            place = table_ref[turn * count + k]
            source = held.at[:, pl.ds(k * size, size)]
            if parts == 1:
                pltpu.make_async_copy(source, outs[0].at[place], sem).start()
            else:
                for part, out in enumerate(outs):

                    @pl.when(place // (count // 2) == part)
                    def _(source=source, out=out, place=place, part=part):
                        spot = place - part * (count // 2)
                        pltpu.make_async_copy(source, out.at[spot], sem).start()

        for out in outs:
            pltpu.make_async_copy(out, out, sem).wait()

    kept = pltpu.VMEM((total, height, BLOCK), BF16)
    return run_kernel(
        body,
        name,
        [spec for left, right in products for spec in (lane_block(left, D, 0), loose(right))]
        + [smem(table)]
        + extra
        + [loose(array) for array in ready],
        [((count // parts, total, size, BLOCK), BF16, False)] * parts,
        [
            kept,
            pltpu.SemaphoreType.DMA(()),
            kept if extra else pltpu.VMEM((1, 16, BLOCK), BF16),
            pltpu.SemaphoreType.DMA(()),
            pltpu.VMEM((total, rows, BLOCK), BF16),
            pltpu.SemaphoreType.DMA((total,)),
        ],
        micros,
        grid=(1,),
    )


def row_grad(left, right, table, chips, direct, name):
    height = left.shape[1]
    blocks = right.shape[1] // BLOCK
    tile = 768
    size = height // chips // 2
    shape = (chips, blocks, size, BLOCK)
    per_tile = tile // (2 * size)

    def body(left_in, right_ref, table_ref, par_ref, own_ref, *scratch):
        held, par_sem, own_sem, left_ref, left_sems = scratch
        core = table_ref[2 * chips]
        for t in range(height // tile):
            at = slice(t * tile, (t + 1) * tile)
            fetch(left_in.at[:, at], left_ref.at[:, at], left_sems.at[t])

        def step(t, carry):
            at = pl.ds(pl.multiple_of(t * tile, tile), tile)
            pltpu.make_async_copy(left_in.at[:, at], left_ref.at[:, at], left_sems.at[t]).wait()
            grad = dot_tn(left_ref[:, at], right_ref[...]).astype(BF16)
            for k in range(blocks):
                held[k, at, :] = grad[:, k * BLOCK : (k + 1) * BLOCK]
            for k in range(per_tile):
                chip = t * per_tile + k
                for turn, (out, sem) in enumerate(((par_ref, par_sem), (own_ref, own_sem))):
                    part = 1 - core if turn == 0 else core
                    start = pl.multiple_of((2 * chip + part) * size, 16)
                    pltpu.make_async_copy(
                        held.at[:, pl.ds(start, size)],
                        out.at[table_ref[turn * chips + chip]],
                        sem,
                    ).start()
            return carry

        lax.fori_loop(0, height // tile, step, 0)
        pltpu.make_async_copy(par_ref, par_ref, par_sem).wait()
        pltpu.make_async_copy(own_ref, own_ref, own_sem).wait()

    def whole(left_ref, right_ref, table_ref, out_ref):
        for t in range(height // tile):
            at = slice(t * tile, (t + 1) * tile)
            out_ref[at, :] = dot_tn(left_ref[:, at], right_ref[...]).astype(BF16)

    if not direct:
        return run_kernel(
            whole,
            name,
            [vmem(left), vmem(right), smem(table)],
            [((height, right.shape[1]), BF16, True)],
            [],
            6,
        )
    return run_kernel(
        body,
        name,
        [loose(left), vmem(right), smem(table)],
        [(shape, BF16, False), (shape, BF16, False)],
        [
            pltpu.VMEM((blocks, height, BLOCK), BF16),
            pltpu.SemaphoreType.DMA(()),
            pltpu.SemaphoreType.DMA(()),
            pltpu.VMEM(left.shape, left.dtype),
            pltpu.SemaphoreType.DMA((height // tile,)),
        ],
        6,
    )


def body(
    tokens,
    lengths,
    deal,
    w_qkv,
    b_qkv,
    w_out,
    b_out,
    norm1_gain,
    norm1_bias,
    w_up,
    b_up,
    w_down,
    b_down,
    norm2_gain,
    norm2_bias,
    cotangent,
):
    n_dp = lax.axis_size("dp")
    n_fsdp = lax.axis_size("fsdp")
    plan = Plan(n_dp, n_fsdp)
    n, chips = plan.n, plan.chips
    dp_place = lax.axis_index("dp")
    fsdp_place = lax.axis_index("fsdp")
    me = dp_place * n_fsdp + fsdp_place
    core = me % 2
    batches, slot_count, home_rows, width = tokens.shape
    group = n_fsdp // batches
    part_rows = home_rows // group
    rows = n * part_rows
    local = fsdp_place % group
    batch_place = fsdp_place // group
    mine = plan.order(me, core)
    other = plan.order(me, 1 - core)
    mine_place = plan.places(me, core)
    other_place = plan.places(me, 1 - core)
    stores = jnp.concatenate([other_place, mine_place, core[None]]).astype(jnp.int32)
    group_pairs = [
        [(i, i - i % group + (i + k) % group) for i in range(n)] for k in range(1, group)
    ]
    back_pairs = [[(b, a) for a, b in pairs] for pairs in group_pairs]

    def to_parts(array):
        parts = array.reshape(batches, slot_count, group, part_rows, width)
        return parts.transpose(1, 0, 2, 3, 4).reshape(n, part_rows, width)

    def exchange(parts):
        moved = lax.all_to_all(parts, AXES, split_axis=0, concat_axis=0, tiled=True)
        return moved.reshape(rows, -1)

    def from_parts(moved):
        moved = moved.reshape(slot_count, batches, group, part_rows, width)
        return moved.transpose(1, 0, 2, 3, 4).reshape(batches, slot_count, home_rows, width)

    def by_blocks(shard, columns):
        return shard.reshape(-1, columns // BLOCK, BLOCK).transpose(1, 0, 2)

    def whole(parts, place):
        joined = jnp.concatenate(parts)[place].transpose(1, 0, 2, 3)
        return joined.reshape(1, joined.shape[0], -1, BLOCK)

    def split_parts(gather, number):
        if gather.own[0].shape[2] % 16 == 0:
            return gather.own + gather.par
        own, par = [[part[:, :number] for part in parts] for parts in (gather.own, gather.par)]
        return [whole(own, mine_place), whole(par, other_place)]

    def split_places(number):
        size = D // chips
        spots = [mine, other] if size % 16 == 0 else [jnp.zeros((1,), jnp.int32)] * 2
        tables = []
        for half, spot in zip((core, 1 - core), spots):
            starts = jnp.full(spot.shape, half * number)
            tables.append(jnp.stack([starts, spot * size], axis=1))
        return jnp.concatenate(tables).reshape(-1).astype(jnp.int32)

    def row_places():
        size = FF // n
        if size % 16 != 0:
            return jnp.zeros((2,), jnp.int32)
        starts = jnp.concatenate([mine * 2 + core, other * 2 + 1 - core]) * size
        return jnp.stack([jnp.zeros_like(starts), starts], axis=1).reshape(-1).astype(jnp.int32)

    def split_weight(parts, places, first, number):
        return Weight([(part, first, number) for part in parts], places, 2 * number, D)

    def row_weight(gather, places, first, number, chunks):
        own, par = gather.own, gather.par
        size = own[0].shape[2]
        if size % 16 == 0:
            sources = [(part, first, number * chunks) for part in own + par]
            return Weight(sources, places, number, n * size * chunks, chunks)

        def joined(parts, place):
            parts = jnp.concatenate(parts)[place][:, first:]
            parts = parts.reshape(chips, chunks, number, size, BLOCK).transpose(0, 2, 1, 3, 4)
            return parts.reshape(chips, number, chunks * size, BLOCK)

        own, par = joined(own, mine_place), joined(par, other_place)
        both = jnp.where(core == 0, jnp.stack([own, par], 2), jnp.stack([par, own], 2))
        both = both.transpose(1, 0, 2, 3, 4).reshape(1, number, -1, BLOCK)
        return Weight([(both, 0, number)], jnp.zeros((2,), jnp.int32), number, FF)

    size = D // chips
    direct = size % 16 == 0
    no_table = jnp.concatenate([jnp.zeros((2,), jnp.int32), core[None].astype(jnp.int32)])

    def split_order(array, order):
        return array.reshape(-1, chips, size, BLOCK).transpose(1, 0, 2, 3)[order]

    def split_other(products, name, micros, ready=()):
        table = stores if direct else no_table
        (par,) = split_grad(products, table, 0, None, chips, direct, name, micros, ready)
        return par if direct else split_order(par, other)

    def split_own(products, got, name, micros, ready=()):
        if direct:
            return split_grad(products, stores, 1, got, chips, True, name, micros, ready)
        got = got[mine_place].transpose(1, 0, 2, 3).reshape(1, -1, D, BLOCK)
        (own,) = split_grad(products, no_table, 1, got, chips, False, name, micros, ready)
        own = split_order(own, mine)
        return own[: chips // 2], own[chips // 2 :]

    def split_result(block, numbers):
        halves = unsplit_columns(plan, core, block)
        results, at = [], 0
        for number in numbers:
            both = jnp.concatenate([half[at : at + number] for half in halves])
            results.append(both.transpose(1, 0, 2).reshape(-1))
            at += number
        return results

    def row_pieces(left, right, name):
        size = FF // n
        if size % 16 == 0:
            return row_grad(left, right, stores, chips, True, name)
        both = row_grad(left, right, stores, chips, False, name)[0]
        blocks = both.reshape(chips, 2, size, -1, BLOCK).transpose(0, 1, 3, 2, 4)
        par = jnp.where(core == 0, blocks[:, 1], blocks[:, 0])[other]
        own = jnp.where(core == 0, blocks[:, 0], blocks[:, 1])[mine]
        return par, own

    small_shards = (
        b_qkv,
        b_out,
        norm1_gain,
        norm1_bias,
        b_up,
        b_down,
        norm2_gain,
        norm2_bias,
    )
    sizes = [piece.shape[0] for piece in small_shards]
    spare = -len(sizes) % part_rows
    shares = [jnp.pad(piece[None], ((0, 0), (0, 128 - piece.shape[0]))) for piece in small_shards]
    shares = jnp.concatenate(shares + [jnp.zeros((1, 128), BF16)] * (max(spare, 0)))
    shares = shares.reshape(-1, part_rows, 128).transpose(1, 0, 2).reshape(1, part_rows, -1)
    wide = width + shares.shape[2]
    parts = jnp.concatenate(
        [to_parts(tokens), jnp.broadcast_to(shares, (n,) + shares.shape[1:])], axis=2
    )
    def in_halves(cuts):
        left = jnp.concatenate([cut[: cut.shape[0] // 2] for cut in cuts])
        right = jnp.concatenate([cut[cut.shape[0] // 2 :] for cut in cuts])
        return split_columns(plan, core, left, right)

    n_qkv, n_out, n_up = 3 * D // BLOCK // 2, D // BLOCK // 2, FF // BLOCK // 2
    first = Gather(plan, in_halves([by_blocks(w_qkv, 3 * D)]))
    second = Gather(plan, in_halves([by_blocks(w_out, D), by_blocks(w_up, FF)]))
    third = Gather(plan, by_blocks(w_down, D))
    last = plan.levels - 1
    own_deal = jnp.where(batch_place == 0, deal[0], deal[1])
    own_lengths = jnp.where(batch_place == 0, lengths[0], lengths[1])
    for m in range(2, batches):
        own_deal = jnp.where(batch_place == m, deal[m], own_deal)
        own_lengths = jnp.where(batch_place == m, lengths[m], own_lengths)
    seq_len = jnp.sum(jnp.where(own_deal == dp_place, own_lengths, 0))

    row_ids = jnp.arange(rows, dtype=jnp.int32)
    base_places = row_ids // part_rows * home_rows + row_ids % part_rows
    query_places = base_places + local * part_rows
    key_places = jnp.stack([base_places + (local + k) % group * part_rows for k in range(group)])
    mask = jnp.where(key_places < seq_len, 0.0, -1000000000.0).astype(F32)
    mask_columns = jnp.broadcast_to(mask.reshape(-1, 1), (group * rows, 128))
    half_lane = (jnp.arange(128) % HD // 2).astype(F32)
    frequency = 10000.0 ** (-(2.0 * half_lane) / HD)
    angles = query_places.astype(F32)[:, None] * frequency[None, :]
    cosine = jnp.cos(angles)
    sine = jnp.sin(angles) * jnp.where(jnp.arange(128) % 2 == 0, -1.0, 1.0)

    first.step()
    first.step()
    second.step(first.got[0])
    sent = second.step(first.got[1])
    parts = after(parts, sent)
    block_in = exchange(parts)
    first.step()
    for level in range(3, last):
        second.step()
        first.step()
    first.step(parts)
    cot_parts = to_parts(cotangent)
    qkv_places, out_places, up_places, down_places = (
        split_places(n_qkv),
        split_places(n_out),
        split_places(n_up),
        row_places(),
    )
    (
        first.got[-1],
        qkv_places,
        out_places,
        up_places,
        down_places,
        stores,
        cot_parts,
        mask,
        mask_columns,
        cosine,
        sine,
    ) = lax.optimization_barrier(
        (
            first.got[-1],
            qkv_places,
            out_places,
            up_places,
            down_places,
            stores,
            cot_parts,
            mask,
            mask_columns,
            cosine,
            sine,
        )
    )
    sent = second.step(first.got[-1])
    first.finish(sent)
    early = third.step(sent)
    qkv_weight = split_weight(split_parts(first, n_qkv), qkv_places, 0, n_qkv)
    vectors = unpack_vectors(block_in, sizes, part_rows)
    (qkv_bias, out_bias, gain_one, bias_one, up_bias, down_bias, gain_two, bias_two) = vectors

    queries, key_value, qkv_whole = qkv_forward(
        block_in, qkv_weight, qkv_bias, cosine, sine, [early, cot_parts]
    )
    key_values = [key_value] + [swap(key_value, pairs) for pairs in back_pairs]
    ready = [second.step(key_value)]
    heads, lses = [], []
    n_parts = D // PART
    for part in range(n_parts):
        head, lse = attention_forward(queries, key_values, mask, part, ready)
        heads.append(head)
        lses.append(lse)
        ready = [head]
        while part == 0 and len(third.got) < last - 1:
            ready.append(third.step(head))
    third.merge()
    cot_parts = after(cot_parts, *heads)
    grad_top = exchange(cot_parts)
    second.finish(head)
    rest = split_parts(second, n_out + n_up)
    out_weight = split_weight(rest, out_places, 0, n_out)
    up_weight = split_weight(rest, up_places, n_out, n_up)
    sent = third.step(head, second.got[-1])
    attended, standard_one, inverse_one, normed_low, out_whole = out_forward(
        block_in, heads, out_weight, [out_bias, gain_one, bias_one], [sent]
    )
    sent = third.step(normed_low, late=True)
    active, slope, up_whole = up_forward(normed_low, up_weight, up_bias, [sent])
    third.finish(active)
    down_weight = row_weight(third, down_places, 0, D // BLOCK, 1)
    result, grad_two, down_grad, sums_two, down_whole = down_both(
        active,
        down_weight,
        standard_one,
        grad_top,
        [gain_one, bias_one, down_bias, gain_two, bias_two],
    )
    par, own = row_pieces(active, down_grad, "down_grad")
    got = swap(par, plan.core_pairs())
    got = swap(par, plan.core_pairs())
    home_out = from_parts(exchange(result.reshape(n, part_rows, width)).reshape(n, part_rows, width))
    hidden_grad, sums_up, grad_one, branch_grad, d_attended, sums_one = middle_back(
        down_grad,
        slope,
        Whole(down_whole),
        Whole(up_whole),
        Whole(out_whole),
        grad_two,
        standard_one,
        inverse_one,
        gain_one,
        [par],
    )
    got = after(got, hidden_grad)
    half = chips // 2
    sent = (own[half:].astype(F32) + got[half:].astype(F32)).astype(BF16)
    kept = after((own[:half].astype(F32) + got[:half].astype(F32)).astype(BF16))
    down_sum = Reduction(plan, kept, sent)
    products = [(normed_low, hidden_grad), (attended, branch_grad)]
    par = split_other(products, "up_out_other", 5, [sent, home_out])
    got = swap(par, plan.core_pairs())
    kept, away = split_own(products, after(got, down_sum.kept), "up_out_own", 6)
    up_sum = Reduction(plan, kept, away)
    ready = [away]
    parts = []
    for part in range(n_parts):
        query_grad, *kv_grads = attention_back(
            queries,
            key_values,
            d_attended,
            attended,
            lses[part],
            mask_columns,
            cosine,
            sine,
            part,
            ready,
        )
        received = [swap(grad, pairs) for grad, pairs in zip(kv_grads[1:], group_pairs)]
        parts.append([query_grad, kv_grads[0]] + received)
        ready = [query_grad, down_sum.step(query_grad)]
    ready.append(up_sum.step(query_grad))
    qkv_grad, sums_qkv = join_qkv(parts, cosine, sine, ready)
    products = [(block_in, qkv_grad)]
    ready = down_sum.steps_left(qkv_grad)
    par = split_other(products, "qkv_other", 3, ready)
    got = swap(par, plan.core_pairs())
    sent = up_sum.step(par)
    down_mat_grad = down_sum.finish(par).transpose(1, 0, 2).reshape(-1)
    small_sums = [
        (sums_qkv, 0),
        (sums_one, 2),
        (sums_one, 0),
        (sums_one, 1),
        (sums_up, 0),
        (sums_two, 2),
        (sums_two, 0),
        (sums_two, 1),
    ]
    input_grad = input_back(qkv_grad, Whole(qkv_whole), grad_one, small_sums, wide, part_rows, [sent, down_mat_grad])
    ready = up_sum.steps_left(input_grad)
    input_grad = after(input_grad, *ready)
    moved = exchange(input_grad.reshape(n, part_rows, wide)).reshape(n, part_rows, wide)
    kept, away = split_own(products, after(got, input_grad), "qkv_own", 4)
    qkv_sum = Reduction(plan, kept, away)
    qkv_sum.step()
    up_total = up_sum.finish(qkv_sum.step())
    home_grad = from_parts(moved[:, :, :width])
    summed = jnp.sum(moved[:, :, width:].astype(F32), axis=0)
    summed = summed.reshape(part_rows, -1, 128).transpose(1, 0, 2).reshape(-1, 128)
    owned = [summed[k, :size] for k, size in enumerate(sizes)]
    up_mat_grad, out_mat_grad = split_result(up_total, [n_up, n_out])
    (qkv_mat_grad,) = split_result(qkv_sum.finish(), [n_qkv])
    return (
        home_out,
        home_grad,
        qkv_mat_grad,
        owned[0],
        out_mat_grad,
        owned[1],
        owned[2],
        owned[3],
        up_mat_grad,
        owned[4],
        down_mat_grad,
        owned[5],
        owned[6],
        owned[7],
    )


def solution(mesh):
    rows = P(None, None, AXES, None)
    flat = P(AXES)
    in_specs = (rows, P(), P()) + (flat,) * 12 + (rows,)
    out_specs = (rows, rows) + (flat,) * 12
    return jax.shard_map(body, mesh=mesh, in_specs=in_specs, out_specs=out_specs, check_vma=False)
```

```python
import math

import jax
import jax.numpy as jnp
from jax import lax
from jax.experimental import pallas as pl
from jax.experimental.pallas import tpu as pltpu
from jax.sharding import PartitionSpec as P

D = 768
HEADS = 12
HD = 64
FF = 3072
AXES = ("dp", "fsdp")
BLOCK = 384
F32 = jnp.float32
BF16 = jnp.bfloat16


class Plan:
    def __init__(self, n_dp, n_fsdp):
        self.n = n_dp * n_fsdp
        self.chips = self.n // 2
        bits = [1 << k for k in range(1, self.n.bit_length() - 1)]
        near, far = bits[:2], bits[2:]
        first = [b | (b >> 1) if b >> 1 in far else b for b in reversed(far)]
        self.masks = [first + near[::-1], first + near]
        self.levels = len(bits)
        self.combos = []
        for masks in self.masks:
            row = []
            for rel in range(self.chips):
                total = 0
                for k in range(self.levels):
                    if rel >> k & 1:
                        total ^= masks[k]
                row.append(total)
            self.combos.append(row)

    def pairs(self, level):
        return [(i, i ^ self.masks[i & 1][level]) for i in range(self.n)]

    def core_pairs(self):
        return [(i, i ^ 1) for i in range(self.n)]

    def order(self, me, core):
        table = jnp.asarray(self.combos, jnp.int32)
        return (me ^ jnp.where(core == 0, table[0], table[1])) // 2

    def places(self, me, core):
        spots = [[0] * self.chips for _ in range(2)]
        for spot, row in zip(spots, self.combos):
            for rel, total in enumerate(row):
                spot[total // 2] = rel
        table = jnp.asarray(spots, jnp.int32)
        away = jnp.arange(self.chips, dtype=jnp.int32) ^ (me // 2)
        return jnp.where(core == 0, table[0], table[1])[away]


def swap(value, pairs):
    return lax.ppermute(value, AXES, pairs)


def after(value, *earlier):
    return lax.optimization_barrier((value,) + earlier)[0]


class Gather:
    def __init__(self, plan, piece):
        self.plan = plan
        self.held = piece[None]
        self.got = []
        self.merged = 0

    def merge(self, *earlier):
        if self.merged < len(self.got):
            if earlier:
                self.got[-1] = after(self.got[-1], *earlier)
            self.held = jnp.concatenate([self.held, self.got[-1]], axis=0)
            self.merged = len(self.got)
        return self.held

    def step(self, *earlier, late=False):
        level = len(self.got)
        if late:
            self.got[-1] = after(self.got[-1], *earlier)
        self.merge()
        if earlier and not late:
            self.held = after(self.held, *earlier)
        self.got.append(swap(self.held, self.plan.pairs(level)))
        return self.held

    def finish(self, *earlier):
        self.own = [self.held, self.got[-1]]
        if earlier:
            self.own = [after(part, *earlier) for part in self.own]
        self.par = [swap(part, self.plan.core_pairs()) for part in self.own]


class Reduction:
    def __init__(self, plan, kept, away):
        self.plan = plan
        self.kept = kept
        self.level = plan.levels - 1
        self.got = swap(away, plan.pairs(self.level))

    def step(self, *earlier):
        self.level -= 1
        if earlier:
            self.got = after(self.got, *earlier)
        half = self.kept.shape[0] // 2
        kept, got = self.kept.astype(F32), self.got.astype(F32)
        away = (kept[half:] + got[half:]).astype(BF16)
        self.got = swap(away, self.plan.pairs(self.level))
        self.kept = kept[:half] + got[:half]
        if self.level > 0:
            self.kept = after(self.kept.astype(BF16))
        return away

    def steps_left(self, *earlier):
        return [self.step(*earlier) for _ in range(self.level)]

    def finish(self, *earlier):
        self.steps_left()
        if earlier:
            self.got = after(self.got, *earlier)
        return (self.kept + self.got.astype(F32))[0]


def split_columns(plan, core, left, right):
    keep = jnp.where(core == 0, left, right)
    got = swap(jnp.where(core == 0, right, left), plan.core_pairs())
    return jnp.where(core == 0, jnp.concatenate([keep, got], 1), jnp.concatenate([got, keep], 1))


def unsplit_columns(plan, core, block):
    rows = block.shape[1] // 2
    upper, lower = block[:, :rows], block[:, rows:]
    keep = jnp.where(core == 0, upper, lower)
    got = swap(jnp.where(core == 0, lower, upper), plan.core_pairs())
    return jnp.where(core == 0, keep, got), jnp.where(core == 0, got, keep)


def vmem(array):
    return (array, pl.BlockSpec(memory_space=pltpu.VMEM))


def smem(array):
    return (array, pl.BlockSpec(memory_space=pltpu.SMEM))


def loose(array):
    return (array, pl.BlockSpec(memory_space=pltpu.HBM))


def lane_block(array, width, place):
    return (array, pl.BlockSpec((array.shape[0], width), lambda step: (0, place)))


def run_kernel(body, name, ins, outs, scratch, micros, grid=()):
    return pl.pallas_call(
        body,
        name=name,
        grid=grid,
        in_specs=[spec for _, spec in ins],
        out_specs=[
            pl.BlockSpec(memory_space=pltpu.VMEM if inside else pl.ANY) for _, _, inside in outs
        ],
        out_shape=[jax.ShapeDtypeStruct(shape, dtype) for shape, dtype, _ in outs],
        scratch_shapes=scratch,
        compiler_params=pltpu.CompilerParams(vmem_limit_bytes=44 * 2**20),
        cost_estimate=pl.CostEstimate(
            flops=int(micros * 2.2e9), bytes_accessed=2**20, transcendentals=0
        ),
    )(*[array for array, _ in ins])


def dot_nn(left, right):
    return jnp.dot(left, right, preferred_element_type=F32)


def dot_nt(left, right):
    return lax.dot_general(left, right, (((1,), (1,)), ((), ())), preferred_element_type=F32)


def dot_tn(left, right):
    return lax.dot_general(left, right, (((0,), (0,)), ((), ())), preferred_element_type=F32)


def buffer(array):
    return [pltpu.VMEM(array.shape, array.dtype), pltpu.SemaphoreType.DMA(())]


def fetch(ref, held, sem):
    copy = pltpu.make_async_copy(ref, held, sem)
    copy.start()
    return copy


class Weight:
    def __init__(self, sources, places, blocks, height, per_column=1):
        self.sources = sources
        self.places = places
        self.blocks = blocks
        self.height = height
        self.per_column = per_column

    def ins(self):
        return [smem(self.places)] + [loose(array) for array, _, _ in self.sources]

    def scratch(self):
        return [pltpu.VMEM((self.blocks, self.height, BLOCK), BF16), pltpu.SemaphoreType.DMA((2,))]

    def count(self):
        return 1 + len(self.sources)

    def start(self, refs, held, sem):
        places, at = refs[0], 0
        for k, ((_, first, number), ref) in enumerate(zip(self.sources, refs[1:])):
            count, _, rows, _ = ref.shape
            for j in range(count):
                for turn in range(self.per_column):
                    row = pl.multiple_of(places[2 * at + 1] + turn * rows, 16)
                    share = number // self.per_column
                    pltpu.make_async_copy(
                        ref.at[j, pl.ds(first + turn * share, share)],
                        held.at[pl.ds(places[2 * at], share), pl.ds(row, rows)],
                        sem.at[2 * k // len(self.sources)],
                    ).start()
                at += 1

    def halves(self, refs, held, sem):
        number = self.blocks // 2
        total = sum(ref.shape[0] for ref in refs[1:])
        for k in range(2):
            part = held.at[pl.ds(0, number)]
            pltpu.make_async_copy(part, part, sem.at[k]).wait()
            yield refs[0][k * total]

    def wait(self, refs, held, sem):
        if len(self.sources) == 1:
            pltpu.make_async_copy(held, held, sem.at[0]).wait()
        else:
            part = held.at[:, pl.ds(0, self.height // 2)]
            for k in range(2):
                pltpu.make_async_copy(part, part, sem.at[k]).wait()


class Whole:
    def __init__(self, array):
        self.array = array

    def scratch(self, steps):
        return [pltpu.VMEM(self.array.shape, BF16), pltpu.SemaphoreType.DMA((steps,))]


def turned(values, cosine, sine):
    lanes = lax.broadcasted_iota(jnp.int32, values.shape, 1)
    swapped = jnp.where(
        lanes % 2 == 0, pltpu.roll(values, 127, 1), pltpu.roll(values, 1, 1)
    )
    return values * cosine + swapped * sine


def qkv_forward(x, weight, bias, cosine, sine, ready):
    rows = x.shape[0]
    n_w = weight.count()

    def body(*refs):
        x_ref, b_ref, cos_ref, sin_ref = refs[:4]
        w_refs = refs[4 : 4 + n_w]
        q_ref, kv_ref, whole, held, sem, whole_sem = refs[4 + n_w + len(ready) :]
        weight.start(w_refs, held, sem)
        weight.wait(w_refs, held, sem)
        whole_there = fetch(held, whole, whole_sem)
        cos, sin = cos_ref[...], sin_ref[...]
        for t in range(weight.blocks):
            y = dot_nn(x_ref[...], held[t]) + b_ref[:, t * BLOCK : (t + 1) * BLOCK]
            for g in range(BLOCK // 128):
                piece = y[:, g * 128 : (g + 1) * 128]
                at = t * BLOCK + g * 128
                if at < 2 * D:
                    piece = turned(piece, cos, sin)
                if at < D:
                    q_ref[:, at : at + 128] = (piece * (1.0 / math.sqrt(HD))).astype(BF16)
                else:
                    kv_ref[:, at - D : at - D + 128] = piece.astype(BF16)
        whole_there.wait()

    return run_kernel(
        body,
        "qkv_forward",
        [lane_block(x, D, 0), vmem(bias), vmem(cosine), vmem(sine)]
        + weight.ins()
        + [loose(array) for array in ready],
        [
            ((rows, D), BF16, True),
            ((rows, 2 * D), BF16, True),
            ((weight.blocks, D, BLOCK), BF16, False),
        ],
        weight.scratch() + [pltpu.SemaphoreType.DMA(())],
        7,
        grid=(1,),
    )


def row_standard(values):
    average = jnp.mean(values, axis=-1, keepdims=True)
    centered = values - average
    variance = jnp.mean(centered * centered, axis=-1, keepdims=True)
    inverse = lax.rsqrt(variance + 1e-05)
    return centered * inverse, inverse


def row_standard_back(grad, standard, inverse):
    mean_grad = jnp.mean(grad, axis=-1, keepdims=True)
    mean_proj = jnp.mean(grad * standard, axis=-1, keepdims=True)
    return inverse * (grad - mean_grad - standard * mean_proj)


PART = 384


def attention_forward(queries, key_values, mask, part, ready):
    rows = queries.shape[0]
    n_kv = len(key_values)
    block = min(rows, 256)

    def body(*refs):
        q_ref, mask_ref = refs[:2]
        k_refs = refs[2 : 2 + n_kv]
        v_refs = refs[2 + n_kv : 2 + 2 * n_kv]
        a_ref, lse_ref, lse_acc = refs[2 + 2 * n_kv + len(ready) :]
        lse_acc[...] = jnp.zeros_like(lse_acc)
        lanes = lax.broadcasted_iota(jnp.int32, (block, 128), 1)
        def pair(p, carry):
            at = pl.ds(pl.multiple_of(p * 128, 128), 128)
            for r in range(rows // block):
                own = slice(r * block, (r + 1) * block)
                q_pair = q_ref[own, at].astype(F32)
                heads = []
                for head in range(2):
                    q_head = jnp.where(lanes // HD == head, q_pair, 0.0).astype(BF16)
                    scores = [
                        dot_nt(q_head, key[:, at]) + mask_ref[g : g + 1, :]
                        for g, key in enumerate(k_refs)
                    ]
                    peak = scores[0].max(axis=-1, keepdims=True)
                    for s in scores[1:]:
                        peak = jnp.maximum(peak, s.max(axis=-1, keepdims=True))
                    raised = [jnp.exp(s - peak) for s in scores]
                    total = raised[0].sum(axis=-1, keepdims=True)
                    for e in raised[1:]:
                        total = total + e.sum(axis=-1, keepdims=True)
                    mixed = dot_nn(raised[0].astype(BF16), v_refs[0][:, at])
                    for e, value in zip(raised[1:], v_refs[1:]):
                        mixed = mixed + dot_nn(e.astype(BF16), value[:, at])
                    heads.append(mixed / total)
                    lse_acc[own, :] = jnp.where(
                        lanes == 2 * p + head, peak + jnp.log(total), lse_acc[own, :]
                    )
                a_ref[own, at] = jnp.where(lanes < HD, heads[0], heads[1]).astype(BF16)
            return carry

        lax.fori_loop(0, PART // 128, pair, 0)
        lse_ref[...] = jnp.transpose(lse_acc[...])[:8]

    return run_kernel(
        body,
        "attention_forward",
        [lane_block(queries, PART, part), vmem(mask)]
        + [lane_block(kv, PART, part) for kv in key_values]
        + [lane_block(kv, PART, part + D // PART) for kv in key_values]
        + [loose(array) for array in ready],
        [((rows, PART), BF16, True), ((8, rows), F32, True)],
        [pltpu.VMEM((rows, 128), F32)],
        6,
        grid=(1,),
    )


def out_forward(x, attended, weight, vectors, ready):
    rows = x.shape[0]
    n_a = len(attended)
    n_w = weight.count()
    block = min(rows, 128)

    def body(*refs):
        x_ref, ob_ref, g_ref, b_ref = refs[:4]
        part_refs = refs[4 : 4 + n_a]
        w_refs = refs[4 + n_a : 4 + n_a + n_w]
        a_ref, n_ref, s_ref, h_ref, whole, held, sem, acc, whole_sem = refs[
            4 + n_a + n_w + len(ready) :
        ]
        weight.start(w_refs, held, sem)
        for k, part in enumerate(part_refs):
            a_ref[:, k * PART : (k + 1) * PART] = part[...]
        weight.wait(w_refs, held, sem)
        whole_there = fetch(held, whole, whole_sem)
        for t in range(weight.blocks):
            acc[:, t * BLOCK : (t + 1) * BLOCK] = dot_nn(a_ref[...], held[t])

        def row(r, carry):
            own = pl.ds(pl.multiple_of(r * block, block), block)
            branch = acc[own, :] + ob_ref[...]
            standard, inverse = row_standard(x_ref[own, :].astype(F32) + branch)
            n_ref[own, :] = standard
            s_ref[own, :] = jnp.broadcast_to(inverse, (block, 128))
            h_ref[own, :] = (standard * g_ref[...] + b_ref[...]).astype(BF16)
            return carry

        lax.fori_loop(0, rows // block, row, 0)
        whole_there.wait()

    return run_kernel(
        body,
        "out_forward",
        [lane_block(x, D, 0)]
        + [vmem(v) for v in vectors]
        + [vmem(part) for part in attended]
        + weight.ins()
        + [loose(array) for array in ready],
        [
            ((rows, D), BF16, True),
            ((rows, D), F32, True),
            ((rows, 128), F32, True),
            ((rows, D), BF16, True),
            ((weight.blocks, D, BLOCK), BF16, False),
        ],
        weight.scratch() + [pltpu.VMEM((rows, D), F32), pltpu.SemaphoreType.DMA(())],
        4,
        grid=(1,),
    )


def bell(u):
    size = jnp.abs(u)
    t = 1.0 / (1.0 + (0.3275911 / math.sqrt(2.0)) * size)
    raised = jnp.exp(-0.5 * u * u)
    poly = 0.5 * 1.061405429
    for c in (-1.453152027, 1.421413741, -0.284496736, 0.254829592):
        poly = poly * t + 0.5 * c
    tail = poly * t * raised
    return jnp.where(u >= 0.0, 1.0 - tail, tail), raised


def up_forward(h, weight, bias, ready):
    rows = h.shape[0]
    n_w = weight.count()

    def body(*refs):
        h_ref, b_ref = refs[:2]
        w_refs = refs[2 : 2 + n_w]
        g_out, slope_out, whole, *scratch = refs[2 + n_w + len(ready) :]
        held, sem, g_ref, g_sem, slope_ref, slope_sem, whole_sem = scratch
        weight.start(w_refs, held, sem)
        for first in weight.halves(w_refs, held, sem):
            part = pl.ds(first, weight.blocks // 2)
            pltpu.make_async_copy(held.at[part], whole.at[part], whole_sem).start()

            def step(t, carry, first=first):
                at = pl.ds(pl.multiple_of((first + t) * BLOCK, 128), BLOCK)
                u = dot_nn(h_ref[...], held[first + t]) + b_ref[:, at]
                share, raised = bell(u)
                g_ref[:, at] = (u * share).astype(BF16)
                slope_ref[:, at] = (
                    share + u * raised * (1.0 / math.sqrt(2.0 * math.pi))
                ).astype(BF16)
                pltpu.make_async_copy(g_ref.at[:, at], g_out.at[:, at], g_sem).start()
                pltpu.make_async_copy(slope_ref.at[:, at], slope_out.at[:, at], slope_sem).start()
                return carry

            lax.fori_loop(0, weight.blocks // 2, step, 0)
        pltpu.make_async_copy(held, whole, whole_sem).wait()
        pltpu.make_async_copy(g_ref, g_out, g_sem).wait()
        pltpu.make_async_copy(slope_ref, slope_out, slope_sem).wait()

    wide = jax.ShapeDtypeStruct((rows, FF), BF16)
    return run_kernel(
        body,
        "up_forward",
        [vmem(h), vmem(bias)] + weight.ins() + [loose(array) for array in ready],
        [
            ((rows, FF), BF16, False),
            ((rows, FF), BF16, False),
            ((weight.blocks, D, BLOCK), BF16, False),
        ],
        weight.scratch() + buffer(wide) + buffer(wide) + [pltpu.SemaphoreType.DMA(())],
        12,
    )


def down_both(active, weight, standard_one, cot, vectors):
    rows = active.shape[0]
    n_w = weight.count()
    block = min(rows, 128)

    def body(*refs):
        g_in, n_in, cot_in, g1_ref, b1_ref, db_ref, g2_ref, b2_ref = refs[:8]
        w_refs = refs[8 : 8 + n_w]
        out_ref, dr_ref, dz_ref, sums_ref, whole, held, sem, z_ref = refs[8 + n_w : 16 + n_w]
        g_ref, g_sem, n_ref, n_sem, cot_ref, cot_sem, whole_sem = refs[16 + n_w :]
        active_there = fetch(g_in, g_ref, g_sem)
        weight.start(w_refs, held, sem)
        others_there = [fetch(n_in, n_ref, n_sem), fetch(cot_in, cot_ref, cot_sem)]
        active_there.wait()
        weight.wait(w_refs, held, sem)
        whole_there = fetch(held, whole, whole_sem)
        for t in range(weight.blocks):
            z_ref[:, t * BLOCK : (t + 1) * BLOCK] = dot_nn(g_ref[...], held[t])
        for there in others_there:
            there.wait()
        sums_ref[...] = jnp.zeros_like(sums_ref)

        def row(r, carry):
            own = pl.ds(pl.multiple_of(r * block, block), block)
            h = n_ref[own, :] * g1_ref[...] + b1_ref[...]
            standard, inverse = row_standard(h + z_ref[own, :] + db_ref[...])
            out_ref[own, :] = (standard * g2_ref[...] + b2_ref[...]).astype(BF16)
            dy = cot_ref[own, :].astype(F32)
            dr = row_standard_back(dy * g2_ref[...], standard, inverse)
            dr_ref[own, :] = dr
            low = dr.astype(BF16)
            dz_ref[own, :] = low
            sums_ref[0:1, :] += jnp.sum(dy * standard, axis=0, keepdims=True)
            sums_ref[1:2, :] += jnp.sum(dy, axis=0, keepdims=True)
            sums_ref[2:3, :] += jnp.sum(low.astype(F32), axis=0, keepdims=True)
            return carry

        lax.fori_loop(0, rows // block, row, 0)
        whole_there.wait()

    return run_kernel(
        body,
        "down_both",
        [loose(active), loose(standard_one), loose(cot)]
        + [vmem(v) for v in vectors]
        + weight.ins(),
        [
            ((rows, D), BF16, True),
            ((rows, D), F32, True),
            ((rows, D), BF16, True),
            ((8, D), F32, True),
            ((weight.blocks, FF, BLOCK), BF16, False),
        ],
        weight.scratch()
        + [pltpu.VMEM((rows, D), F32)]
        + buffer(active)
        + buffer(standard_one)
        + buffer(cot)
        + [pltpu.SemaphoreType.DMA(())],
        10,
    )


def middle_back(dz, slope, down, up, out, dr2, standard, inverse, gain, ready):
    rows = dz.shape[0]
    block = min(rows, 128)
    steps = FF // BLOCK

    def body(*refs):
        dz_ref, slope_in, down_in, up_in, out_in, dr2_in, n_in, s_in, g_ref = refs[:9]
        rest = refs[9 + len(ready) :]
        du_out, up_sums_ref, dr_ref, do_ref, da_ref, sums_ref = rest[:6]
        down_w, down_sem, up_w, up_sem, out_w, out_sem = rest[6:12]
        slope_ref, slope_sem, du_ref, du_sem = rest[12:16]
        acc, acc_sem, n_ref, n_sem, s_ref, s_sem, slope_sems = rest[16:]
        del slope_sem
        for t in range(steps):
            at = slice(t * BLOCK, (t + 1) * BLOCK)
            fetch(down_in.at[:, at], down_w.at[:, at], down_sem.at[t])
            fetch(slope_in.at[:, at], slope_ref.at[:, at], slope_sems.at[t])
            fetch(up_in.at[t], up_w.at[t], up_sem.at[t])
            if t == 0:
                acc_there = fetch(dr2_in, acc, acc_sem)
        others_there = [
            fetch(n_in, n_ref, n_sem),
            fetch(s_in, s_ref, s_sem),
            fetch(out_in, out_w, out_sem.at[0]),
        ]
        up_sums_ref[...] = jnp.zeros_like(up_sums_ref)
        sums_ref[...] = jnp.zeros_like(sums_ref)
        acc_there.wait()

        def step(t, carry):
            at = pl.ds(pl.multiple_of(t * BLOCK, 128), BLOCK)
            pltpu.make_async_copy(down_in.at[:, at], down_w.at[:, at], down_sem.at[t]).wait()
            pltpu.make_async_copy(slope_in.at[:, at], slope_ref.at[:, at], slope_sems.at[t]).wait()
            grad = dot_nt(dz_ref[:, :BLOCK], down_w[0, at, :])
            for k in range(1, D // BLOCK):
                grad = grad + dot_nt(dz_ref[:, k * BLOCK : (k + 1) * BLOCK], down_w[k, at, :])
            du = (grad * slope_ref[:, at].astype(F32)).astype(BF16)
            du_ref[:, at] = du
            pltpu.make_async_copy(du_ref.at[:, at], du_out.at[:, at], du_sem).start()
            up_sums_ref[0:1, at] = jnp.sum(du.astype(F32), axis=0, keepdims=True)
            pltpu.make_async_copy(up_in.at[t], up_w.at[t], up_sem.at[t]).wait()
            acc[...] += dot_nt(du, up_w[t])
            return carry

        lax.fori_loop(0, steps, step, 0)
        for there in others_there:
            there.wait()

        def row(r, carry):
            own = pl.ds(pl.multiple_of(r * block, block), block)
            dh = acc[own, :]
            standard_own = n_ref[own, :]
            dr = row_standard_back(dh * g_ref[...], standard_own, s_ref[own, 0:1])
            dr_ref[own, :] = dr
            low = dr.astype(BF16)
            do_ref[own, :] = low
            sums_ref[0:1, :] += jnp.sum(dh * standard_own, axis=0, keepdims=True)
            sums_ref[1:2, :] += jnp.sum(dh, axis=0, keepdims=True)
            sums_ref[2:3, :] += jnp.sum(low.astype(F32), axis=0, keepdims=True)
            return carry

        lax.fori_loop(0, rows // block, row, 0)
        grad = dot_nt(do_ref[:, :BLOCK], out_w[0])
        for t in range(1, D // BLOCK):
            grad = grad + dot_nt(do_ref[:, t * BLOCK : (t + 1) * BLOCK], out_w[t])
        da_ref[...] = grad.astype(BF16)
        pltpu.make_async_copy(du_ref, du_out, du_sem).wait()

    return run_kernel(
        body,
        "middle_back",
        [vmem(dz), loose(slope), loose(down.array), loose(up.array), loose(out.array)]
        + [loose(dr2), loose(standard), loose(inverse), vmem(gain)]
        + [loose(array) for array in ready],
        [
            ((rows, FF), BF16, False),
            ((8, FF), F32, True),
            ((rows, D), F32, True),
            ((rows, D), BF16, True),
            ((rows, D), BF16, True),
            ((8, D), F32, True),
        ],
        down.scratch(steps)
        + up.scratch(steps)
        + out.scratch(1)
        + buffer(slope)
        + buffer(slope)
        + buffer(dr2)
        + buffer(standard)
        + buffer(inverse)
        + [pltpu.SemaphoreType.DMA((steps,))],
        14,
    )


def attention_back(
    queries, key_values, d_attended, attended, lse, mask, cosine, sine, part, ready
):
    rows = queries.shape[0]
    n_kv = len(key_values)
    block = min(rows, 256)
    scale = 1.0 / math.sqrt(HD)

    def body(*refs):
        q_ref, da_ref, a_ref, lse_ref, mask_ref, cos_ref, sin_ref = refs[:7]
        k_refs = refs[7 : 7 + n_kv]
        v_refs = refs[7 + n_kv : 7 + 2 * n_kv]
        dq_ref, *dkv_refs = refs[7 + 2 * n_kv + len(ready) :]
        lanes = lax.broadcasted_iota(jnp.int32, (rows, 128), 1)
        picks = lax.broadcasted_iota(jnp.int32, (8, 128), 1) // HD
        chosen = (picks == lax.broadcasted_iota(jnp.int32, (8, 128), 0)).astype(F32)

        def pair(p, carry):
            at = pl.ds(pl.multiple_of(p * 128, 128), 128)
            v_at = pl.ds(pl.multiple_of(PART + p * 128, 128), 128)
            q_pair = q_ref[:, at].astype(F32)
            da_pair = da_ref[:, at].astype(F32)
            dots = lax.dot_general(
                chosen,
                da_pair * a_ref[:, at].astype(F32),
                (((1,), (1,)), ((), ())),
                precision=lax.Precision.HIGHEST,
                preferred_element_type=F32,
            )
            q_heads = [
                jnp.where(lanes // HD == head, q_pair, 0.0).astype(BF16) for head in range(2)
            ]
            da_heads = [
                jnp.where(lanes // HD == head, da_pair, 0.0).astype(BF16) for head in range(2)
            ]
            lse_rows = [lse_ref[pl.ds(2 * p + head, 1), :] for head in range(2)]
            dq_heads = [None, None]
            for g in range(n_kv):
                for b in range(rows // block):
                    own = slice(b * block, (b + 1) * block)
                    keys = k_refs[g][own, at]
                    values = v_refs[g][own, at]
                    hidden = mask_ref[g * rows + b * block : g * rows + (b + 1) * block, 0:1]
                    dk, dv = None, None
                    for head in range(2):
                        s = dot_nt(keys, q_heads[head]) + hidden
                        prob = jnp.exp(s - lse_rows[head])
                        dp = dot_nt(values, da_heads[head])
                        ds = (prob * (dp - dots[head : head + 1, :])).astype(BF16)
                        dv_part = dot_nn(prob.astype(BF16), da_heads[head])
                        dk_part = dot_nn(ds, q_heads[head])
                        dq_part = dot_tn(keys, ds)
                        dv = dv_part if dv is None else dv + dv_part
                        dk = dk_part if dk is None else dk + dk_part
                        dq_heads[head] = (
                            dq_part if dq_heads[head] is None else dq_heads[head] + dq_part
                        )
                    kind = F32 if g == 0 else BF16
                    dkv_refs[g][own, at] = dk.astype(kind)
                    dkv_refs[g][own, v_at] = dv.astype(kind)
            flipped = lax.broadcasted_iota(jnp.int32, (128, rows), 0)
            dq = jnp.transpose(jnp.where(flipped < HD, dq_heads[0], dq_heads[1])) * scale
            dq_ref[:, at] = turned(dq, cos_ref[...], -sin_ref[...]).astype(BF16)
            return carry

        lax.fori_loop(0, PART // 128, pair, 0)

    return run_kernel(
        body,
        "attention_back",
        [
            lane_block(queries, PART, part),
            lane_block(d_attended, PART, part),
            lane_block(attended, PART, part),
            vmem(lse),
            vmem(mask),
            vmem(cosine),
            vmem(sine),
        ]
        + [lane_block(kv, PART, part) for kv in key_values]
        + [lane_block(kv, PART, part + D // PART) for kv in key_values]
        + [loose(array) for array in ready],
        [((rows, PART), BF16, True)]
        + [((rows, 2 * PART), F32 if g == 0 else BF16, True) for g in range(n_kv)],
        [],
        8,
        grid=(1,),
    )


def join_qkv(parts, cosine, sine, ready):
    rows = parts[0][0].shape[0]
    n_each = len(parts[0])

    def body(*refs):
        cos_ref, sin_ref = refs[:2]
        part_refs = refs[2 : 2 + n_each * len(parts)]
        out_ref, sums_ref = refs[2 + n_each * len(parts) + len(ready) :]
        sums_ref[...] = jnp.zeros_like(sums_ref)
        cos, sin = cos_ref[...], -sin_ref[...]

        def put(at, low):
            out_ref[:, at : at + 128] = low
            sums_ref[0:1, at : at + 128] = jnp.sum(low.astype(F32), axis=0, keepdims=True)

        for k in range(len(parts)):
            dq_ref, dkv_ref, *got_refs = part_refs[k * n_each : (k + 1) * n_each]
            for at in range(0, PART, 128):
                put(k * PART + at, dq_ref[:, at : at + 128])
            for at in range(0, 2 * PART, 128):
                value = dkv_ref[:, at : at + 128]
                for got in got_refs:
                    value = value + got[:, at : at + 128].astype(F32)
                if at < PART:
                    put(D + k * PART + at, turned(value, cos, sin).astype(BF16))
                else:
                    put(2 * D + k * PART + at - PART, value.astype(BF16))

    return run_kernel(
        body,
        "join_qkv",
        [vmem(cosine), vmem(sine)]
        + [vmem(array) for part in parts for array in part]
        + [loose(array) for array in ready],
        [((rows, 3 * D), BF16, True), ((8, 3 * D), F32, True)],
        [],
        4,
    )


def input_back(dproj, weight, dr1, sums, width, part_rows, ready):
    rows = dproj.shape[0]
    n = rows // part_rows
    blocks = weight.array.shape[0]
    n_s = len(sums)

    def body(*refs):
        dp_ref, dr_in = refs[:2]
        sum_refs = refs[2 : 2 + n_s]
        w_in = refs[2 + n_s]
        out_ref, held, sem, shares, dr_ref, dr_sem = refs[3 + n_s + len(ready) :]
        there = [fetch(w_in.at[t], held.at[t], sem.at[t]) for t in range(blocks)]
        dr_there = fetch(dr_in, dr_ref, dr_sem)
        shares[...] = jnp.zeros_like(shares)
        if n <= 64:
            for place, (_, line), ref in zip(range(n_s), sums, sum_refs):
                size = ref.shape[1] // n
                row, column = place % part_rows, place // part_rows * 128
                for k in range(n):
                    at = k * part_rows + row
                    shares[at : at + 1, column : column + size] = ref[
                        line : line + 1, k * size : (k + 1) * size
                    ]
        out_ref[:, D:] = shares[...].astype(BF16)
        dr_there.wait()
        grad = dr_ref[...]
        for t in range(blocks):
            there[t].wait()
            grad = grad + dot_nt(dp_ref[:, t * BLOCK : (t + 1) * BLOCK], held[t])
        out_ref[:, :D] = grad.astype(BF16)

    result = run_kernel(
        body,
        "input_back",
        [vmem(dproj), loose(dr1)]
        + [vmem(array) for array, _ in sums]
        + [loose(weight.array)]
        + [loose(array) for array in ready],
        [((rows, width), BF16, True)],
        weight.scratch(blocks) + [pltpu.VMEM((rows, width - D), F32)] + buffer(dr1),
        6,
    )[0]
    if n <= 64:
        return result
    shares = []
    for array, line in sums:
        size = array.shape[1] // n
        shares.append(jnp.pad(array[line].reshape(n, size), ((0, 0), (0, 128 - size))))
    spare = -len(shares) % part_rows
    shares = jnp.stack(shares + [jnp.zeros_like(shares[0])] * spare, axis=1)
    shares = shares.reshape(n, -1, part_rows, 128).transpose(0, 2, 1, 3).reshape(rows, -1)
    return jnp.concatenate([result[:, :D], shares.astype(BF16)], axis=1)


def unpack_vectors(moved, sizes, part_rows):
    rows = moved.shape[0]
    n = rows // part_rows
    if n > 64:
        shares = moved[:, D:].astype(F32).reshape(n, part_rows, -1, 128).transpose(0, 2, 1, 3)
        shares = shares.reshape(n, -1, 128)
        return [shares[:, k, :size].reshape(1, -1) for k, size in enumerate(sizes)]

    def body(moved_ref, *refs):
        shares = refs[-1]
        shares[...] = moved_ref[...].astype(F32)
        for place, (size, ref) in enumerate(zip(sizes, refs)):
            for k in range(n):
                at = k * part_rows + place
                ref[0:1, k * size : (k + 1) * size] = shares[at : at + 1, :size]

    return run_kernel(
        body,
        "unpack_vectors",
        [lane_block(moved, 128, D // 128)],
        [((1, n * size), F32, True) for size in sizes],
        [pltpu.VMEM((rows, 128), F32)],
        2,
        grid=(1,),
    )


def split_grad(products, table, turn, got, chips, direct, name, micros, ready):
    height = D
    rows = products[0][0].shape[0]
    blocks = [right.shape[1] // 2 // BLOCK for _, right in products]
    count = chips if direct else 1
    size = height // count
    total = sum(blocks)
    extra = [] if got is None else [loose(got)]
    parts = 2 if direct and got is not None else 1

    def body(*refs):
        pair_refs = refs[: 2 * len(products)]
        table_ref = refs[2 * len(products)]
        got_refs = refs[2 * len(products) + 1 :][: len(extra)]
        rest = refs[2 * len(products) + 1 + len(extra) + len(ready) :]
        outs, (held, sem, other, other_sem, columns, column_sems) = rest[:parts], rest[parts:]
        core = table_ref[2 * count]
        half = 1 - core if turn == 0 else core
        column_there = []
        for k, number in enumerate(blocks):
            for t in range(number):
                at = pl.ds(pl.multiple_of((half * number + t) * BLOCK, 128), BLOCK)
                spot = len(column_there)
                column_there.append(
                    fetch(
                        pair_refs[2 * k + 1].at[:, at], columns.at[spot], column_sems.at[spot]
                    )
                )
        for got_ref in got_refs:
            for k in range(count):
                pltpu.make_async_copy(
                    got_ref.at[table_ref[turn * count + k]],
                    other.at[:, pl.ds(k * size, size)],
                    other_sem,
                ).start()
        done = 0
        for k, number in enumerate(blocks):
            left_ref = pair_refs[2 * k]
            for t in range(number):
                column_there[done].wait()
                grad = dot_tn(left_ref[...], columns[done])
                if got_refs:
                    if done == 0:
                        pltpu.make_async_copy(other, other, other_sem).wait()
                    grad = grad + other[done].astype(F32)
                held[done] = grad.astype(BF16)
                done += 1
        for k in range(count):
            place = table_ref[turn * count + k]
            source = held.at[:, pl.ds(k * size, size)]
            if parts == 1:
                pltpu.make_async_copy(source, outs[0].at[place], sem).start()
            else:
                for part, out in enumerate(outs):

                    @pl.when(place // (count // 2) == part)
                    def _(source=source, out=out, place=place, part=part):
                        spot = place - part * (count // 2)
                        pltpu.make_async_copy(source, out.at[spot], sem).start()

        for out in outs:
            pltpu.make_async_copy(out, out, sem).wait()

    kept = pltpu.VMEM((total, height, BLOCK), BF16)
    return run_kernel(
        body,
        name,
        [spec for left, right in products for spec in (lane_block(left, D, 0), loose(right))]
        + [smem(table)]
        + extra
        + [loose(array) for array in ready],
        [((count // parts, total, size, BLOCK), BF16, False)] * parts,
        [
            kept,
            pltpu.SemaphoreType.DMA(()),
            kept if extra else pltpu.VMEM((1, 16, BLOCK), BF16),
            pltpu.SemaphoreType.DMA(()),
            pltpu.VMEM((total, rows, BLOCK), BF16),
            pltpu.SemaphoreType.DMA((total,)),
        ],
        micros,
        grid=(1,),
    )


def row_grad(left, right, table, chips, direct, name):
    height = left.shape[1]
    blocks = right.shape[1] // BLOCK
    tile = 768
    size = height // chips // 2
    shape = (chips, blocks, size, BLOCK)
    per_tile = tile // (2 * size)

    def body(left_in, right_ref, table_ref, par_ref, own_ref, *scratch):
        held, par_sem, own_sem, left_ref, left_sems = scratch
        core = table_ref[2 * chips]
        for t in range(height // tile):
            at = slice(t * tile, (t + 1) * tile)
            fetch(left_in.at[:, at], left_ref.at[:, at], left_sems.at[t])

        def step(t, carry):
            at = pl.ds(pl.multiple_of(t * tile, tile), tile)
            pltpu.make_async_copy(left_in.at[:, at], left_ref.at[:, at], left_sems.at[t]).wait()
            grad = dot_tn(left_ref[:, at], right_ref[...]).astype(BF16)
            for k in range(blocks):
                held[k, at, :] = grad[:, k * BLOCK : (k + 1) * BLOCK]
            for k in range(per_tile):
                chip = t * per_tile + k
                for turn, (out, sem) in enumerate(((par_ref, par_sem), (own_ref, own_sem))):
                    part = 1 - core if turn == 0 else core
                    start = pl.multiple_of((2 * chip + part) * size, 16)
                    pltpu.make_async_copy(
                        held.at[:, pl.ds(start, size)],
                        out.at[table_ref[turn * chips + chip]],
                        sem,
                    ).start()
            return carry

        lax.fori_loop(0, height // tile, step, 0)
        pltpu.make_async_copy(par_ref, par_ref, par_sem).wait()
        pltpu.make_async_copy(own_ref, own_ref, own_sem).wait()

    def whole(left_ref, right_ref, table_ref, out_ref):
        for t in range(height // tile):
            at = slice(t * tile, (t + 1) * tile)
            out_ref[at, :] = dot_tn(left_ref[:, at], right_ref[...]).astype(BF16)

    if not direct:
        return run_kernel(
            whole,
            name,
            [vmem(left), vmem(right), smem(table)],
            [((height, right.shape[1]), BF16, True)],
            [],
            6,
        )
    return run_kernel(
        body,
        name,
        [loose(left), vmem(right), smem(table)],
        [(shape, BF16, False), (shape, BF16, False)],
        [
            pltpu.VMEM((blocks, height, BLOCK), BF16),
            pltpu.SemaphoreType.DMA(()),
            pltpu.SemaphoreType.DMA(()),
            pltpu.VMEM(left.shape, left.dtype),
            pltpu.SemaphoreType.DMA((height // tile,)),
        ],
        6,
    )


def body(
    tokens,
    lengths,
    deal,
    w_qkv,
    b_qkv,
    w_out,
    b_out,
    norm1_gain,
    norm1_bias,
    w_up,
    b_up,
    w_down,
    b_down,
    norm2_gain,
    norm2_bias,
    cotangent,
):
    n_dp = lax.axis_size("dp")
    n_fsdp = lax.axis_size("fsdp")
    plan = Plan(n_dp, n_fsdp)
    n, chips = plan.n, plan.chips
    dp_place = lax.axis_index("dp")
    fsdp_place = lax.axis_index("fsdp")
    me = dp_place * n_fsdp + fsdp_place
    core = me % 2
    batches, slot_count, home_rows, width = tokens.shape
    group = n_fsdp // batches
    part_rows = home_rows // group
    rows = n * part_rows
    local = fsdp_place % group
    batch_place = fsdp_place // group
    mine = plan.order(me, core)
    other = plan.order(me, 1 - core)
    mine_place = plan.places(me, core)
    other_place = plan.places(me, 1 - core)
    stores = jnp.concatenate([other_place, mine_place, core[None]]).astype(jnp.int32)
    group_pairs = [
        [(i, i - i % group + (i + k) % group) for i in range(n)] for k in range(1, group)
    ]
    back_pairs = [[(b, a) for a, b in pairs] for pairs in group_pairs]

    def to_parts(array):
        parts = array.reshape(batches, slot_count, group, part_rows, width)
        return parts.transpose(1, 0, 2, 3, 4).reshape(n, part_rows, width)

    def exchange(parts):
        moved = lax.all_to_all(parts, AXES, split_axis=0, concat_axis=0, tiled=True)
        return moved.reshape(rows, -1)

    def from_parts(moved):
        moved = moved.reshape(slot_count, batches, group, part_rows, width)
        return moved.transpose(1, 0, 2, 3, 4).reshape(batches, slot_count, home_rows, width)

    def by_blocks(shard, columns):
        return shard.reshape(-1, columns // BLOCK, BLOCK).transpose(1, 0, 2)

    def whole(parts, place):
        joined = jnp.concatenate(parts)[place].transpose(1, 0, 2, 3)
        return joined.reshape(1, joined.shape[0], -1, BLOCK)

    def split_parts(gather, number):
        if gather.own[0].shape[2] % 16 == 0:
            return gather.own + gather.par
        own, par = [[part[:, :number] for part in parts] for parts in (gather.own, gather.par)]
        return [whole(own, mine_place), whole(par, other_place)]

    def split_places(number):
        size = D // chips
        spots = [mine, other] if size % 16 == 0 else [jnp.zeros((1,), jnp.int32)] * 2
        tables = []
        for half, spot in zip((core, 1 - core), spots):
            starts = jnp.full(spot.shape, half * number)
            tables.append(jnp.stack([starts, spot * size], axis=1))
        return jnp.concatenate(tables).reshape(-1).astype(jnp.int32)

    def row_places():
        size = FF // n
        if size % 16 != 0:
            return jnp.zeros((2,), jnp.int32)
        starts = jnp.concatenate([mine * 2 + core, other * 2 + 1 - core]) * size
        return jnp.stack([jnp.zeros_like(starts), starts], axis=1).reshape(-1).astype(jnp.int32)

    def split_weight(parts, places, first, number):
        return Weight([(part, first, number) for part in parts], places, 2 * number, D)

    def row_weight(gather, places, first, number, chunks):
        own, par = gather.own, gather.par
        size = own[0].shape[2]
        if size % 16 == 0:
            sources = [(part, first, number * chunks) for part in own + par]
            return Weight(sources, places, number, n * size * chunks, chunks)

        def joined(parts, place):
            parts = jnp.concatenate(parts)[place][:, first:]
            parts = parts.reshape(chips, chunks, number, size, BLOCK).transpose(0, 2, 1, 3, 4)
            return parts.reshape(chips, number, chunks * size, BLOCK)

        own, par = joined(own, mine_place), joined(par, other_place)
        both = jnp.where(core == 0, jnp.stack([own, par], 2), jnp.stack([par, own], 2))
        both = both.transpose(1, 0, 2, 3, 4).reshape(1, number, -1, BLOCK)
        return Weight([(both, 0, number)], jnp.zeros((2,), jnp.int32), number, FF)

    size = D // chips
    direct = size % 16 == 0
    no_table = jnp.concatenate([jnp.zeros((2,), jnp.int32), core[None].astype(jnp.int32)])

    def split_order(array, order):
        return array.reshape(-1, chips, size, BLOCK).transpose(1, 0, 2, 3)[order]

    def split_other(products, name, micros, ready=()):
        table = stores if direct else no_table
        (par,) = split_grad(products, table, 0, None, chips, direct, name, micros, ready)
        return par if direct else split_order(par, other)

    def split_own(products, got, name, micros, ready=()):
        if direct:
            return split_grad(products, stores, 1, got, chips, True, name, micros, ready)
        got = got[mine_place].transpose(1, 0, 2, 3).reshape(1, -1, D, BLOCK)
        (own,) = split_grad(products, no_table, 1, got, chips, False, name, micros, ready)
        own = split_order(own, mine)
        return own[: chips // 2], own[chips // 2 :]

    def split_result(block, numbers):
        halves = unsplit_columns(plan, core, block)
        results, at = [], 0
        for number in numbers:
            both = jnp.concatenate([half[at : at + number] for half in halves])
            results.append(both.transpose(1, 0, 2).reshape(-1))
            at += number
        return results

    def row_pieces(left, right, name):
        size = FF // n
        if size % 16 == 0:
            return row_grad(left, right, stores, chips, True, name)
        both = row_grad(left, right, stores, chips, False, name)[0]
        blocks = both.reshape(chips, 2, size, -1, BLOCK).transpose(0, 1, 3, 2, 4)
        par = jnp.where(core == 0, blocks[:, 1], blocks[:, 0])[other]
        own = jnp.where(core == 0, blocks[:, 0], blocks[:, 1])[mine]
        return par, own

    small_shards = (
        b_qkv,
        b_out,
        norm1_gain,
        norm1_bias,
        b_up,
        b_down,
        norm2_gain,
        norm2_bias,
    )
    sizes = [piece.shape[0] for piece in small_shards]
    spare = -len(sizes) % part_rows
    shares = [jnp.pad(piece[None], ((0, 0), (0, 128 - piece.shape[0]))) for piece in small_shards]
    shares = jnp.concatenate(shares + [jnp.zeros((1, 128), BF16)] * (max(spare, 0)))
    shares = shares.reshape(-1, part_rows, 128).transpose(1, 0, 2).reshape(1, part_rows, -1)
    wide = width + shares.shape[2]
    parts = jnp.concatenate(
        [to_parts(tokens), jnp.broadcast_to(shares, (n,) + shares.shape[1:])], axis=2
    )
    def in_halves(cuts):
        left = jnp.concatenate([cut[: cut.shape[0] // 2] for cut in cuts])
        right = jnp.concatenate([cut[cut.shape[0] // 2 :] for cut in cuts])
        return split_columns(plan, core, left, right)

    n_qkv, n_out, n_up = 3 * D // BLOCK // 2, D // BLOCK // 2, FF // BLOCK // 2
    first = Gather(plan, in_halves([by_blocks(w_qkv, 3 * D)]))
    second = Gather(plan, in_halves([by_blocks(w_out, D), by_blocks(w_up, FF)]))
    third = Gather(plan, by_blocks(w_down, D))
    last = plan.levels - 1
    own_deal = jnp.where(batch_place == 0, deal[0], deal[1])
    own_lengths = jnp.where(batch_place == 0, lengths[0], lengths[1])
    for m in range(2, batches):
        own_deal = jnp.where(batch_place == m, deal[m], own_deal)
        own_lengths = jnp.where(batch_place == m, lengths[m], own_lengths)
    seq_len = jnp.sum(jnp.where(own_deal == dp_place, own_lengths, 0))

    row_ids = jnp.arange(rows, dtype=jnp.int32)
    base_places = row_ids // part_rows * home_rows + row_ids % part_rows
    query_places = base_places + local * part_rows
    key_places = jnp.stack([base_places + (local + k) % group * part_rows for k in range(group)])
    mask = jnp.where(key_places < seq_len, 0.0, -1000000000.0).astype(F32)
    mask_columns = jnp.broadcast_to(mask.reshape(-1, 1), (group * rows, 128))
    half_lane = (jnp.arange(128) % HD // 2).astype(F32)
    frequency = 10000.0 ** (-(2.0 * half_lane) / HD)
    angles = query_places.astype(F32)[:, None] * frequency[None, :]
    cosine = jnp.cos(angles)
    sine = jnp.sin(angles) * jnp.where(jnp.arange(128) % 2 == 0, -1.0, 1.0)

    first.step()
    first.step()
    second.step(first.got[0])
    sent = second.step(first.got[1])
    parts = after(parts, sent)
    block_in = exchange(parts)
    first.step()
    for level in range(3, last):
        second.step()
        first.step()
    first.step(parts)
    cot_parts = to_parts(cotangent)
    qkv_places, out_places, up_places, down_places = (
        split_places(n_qkv),
        split_places(n_out),
        split_places(n_up),
        row_places(),
    )
    (
        first.got[-1],
        qkv_places,
        out_places,
        up_places,
        down_places,
        stores,
        cot_parts,
        mask,
        mask_columns,
        cosine,
        sine,
    ) = lax.optimization_barrier(
        (
            first.got[-1],
            qkv_places,
            out_places,
            up_places,
            down_places,
            stores,
            cot_parts,
            mask,
            mask_columns,
            cosine,
            sine,
        )
    )
    sent = second.step(first.got[-1])
    first.finish(sent)
    early = third.step(sent)
    qkv_weight = split_weight(split_parts(first, n_qkv), qkv_places, 0, n_qkv)
    vectors = unpack_vectors(block_in, sizes, part_rows)
    (qkv_bias, out_bias, gain_one, bias_one, up_bias, down_bias, gain_two, bias_two) = vectors

    queries, key_value, qkv_whole = qkv_forward(
        block_in, qkv_weight, qkv_bias, cosine, sine, [early, cot_parts]
    )
    key_values = [key_value] + [swap(key_value, pairs) for pairs in back_pairs]
    ready = [second.step(key_value)]
    while len(third.got) < last - 1:
        ready.append(third.step(key_value))
    heads, lses = [], []
    n_parts = D // PART
    for part in range(n_parts):
        head, lse = attention_forward(queries, key_values, mask, part, ready)
        heads.append(head)
        lses.append(lse)
        ready = [head]
        ready.append(third.merge(head))
    cot_parts = after(cot_parts, *heads)
    grad_top = exchange(cot_parts)
    second.finish(head)
    rest = split_parts(second, n_out + n_up)
    out_weight = split_weight(rest, out_places, 0, n_out)
    up_weight = split_weight(rest, up_places, n_out, n_up)
    sent = third.step(head, second.got[-1])
    attended, standard_one, inverse_one, normed_low, out_whole = out_forward(
        block_in, heads, out_weight, [out_bias, gain_one, bias_one], [sent]
    )
    sent = third.step(normed_low, late=True)
    active, slope, up_whole = up_forward(normed_low, up_weight, up_bias, [sent])
    third.finish(active)
    down_weight = row_weight(third, down_places, 0, D // BLOCK, 1)
    result, grad_two, down_grad, sums_two, down_whole = down_both(
        active,
        down_weight,
        standard_one,
        grad_top,
        [gain_one, bias_one, down_bias, gain_two, bias_two],
    )
    par, own = row_pieces(active, down_grad, "down_grad")
    got = swap(par, plan.core_pairs())
    got = swap(par, plan.core_pairs())
    home_out = from_parts(exchange(result.reshape(n, part_rows, width)).reshape(n, part_rows, width))
    hidden_grad, sums_up, grad_one, branch_grad, d_attended, sums_one = middle_back(
        down_grad,
        slope,
        Whole(down_whole),
        Whole(up_whole),
        Whole(out_whole),
        grad_two,
        standard_one,
        inverse_one,
        gain_one,
        [par],
    )
    got = after(got, hidden_grad)
    half = chips // 2
    sent = (own[half:].astype(F32) + got[half:].astype(F32)).astype(BF16)
    kept = after((own[:half].astype(F32) + got[:half].astype(F32)).astype(BF16))
    down_sum = Reduction(plan, kept, sent)
    products = [(normed_low, hidden_grad), (attended, branch_grad)]
    par = split_other(products, "up_out_other", 5, [sent, home_out])
    got = swap(par, plan.core_pairs())
    kept, away = split_own(products, after(got, down_sum.kept), "up_out_own", 6)
    up_sum = Reduction(plan, kept, away)
    ready = [away]
    parts = []
    for part in range(n_parts):
        query_grad, *kv_grads = attention_back(
            queries,
            key_values,
            d_attended,
            attended,
            lses[part],
            mask_columns,
            cosine,
            sine,
            part,
            ready,
        )
        received = [swap(grad, pairs) for grad, pairs in zip(kv_grads[1:], group_pairs)]
        parts.append([query_grad, kv_grads[0]] + received)
        ready = [query_grad, down_sum.step(query_grad)]
    ready = [query_grad, up_sum.step(query_grad)]
    qkv_grad, sums_qkv = join_qkv(parts, cosine, sine, ready)
    products = [(block_in, qkv_grad)]
    small_sums = [
        (sums_qkv, 0),
        (sums_one, 2),
        (sums_one, 0),
        (sums_one, 1),
        (sums_up, 0),
        (sums_two, 2),
        (sums_two, 0),
        (sums_two, 1),
    ]
    input_grad = input_back(
        qkv_grad, Whole(qkv_whole), grad_one, small_sums, wide, part_rows, []
    )
    ready = down_sum.steps_left(input_grad) + [up_sum.step(input_grad)]
    moved = exchange(after(input_grad, *ready).reshape(n, part_rows, wide))
    moved = moved.reshape(n, part_rows, wide)
    par = split_other(products, "qkv_other", 3, [input_grad] + ready)
    got = swap(par, plan.core_pairs())
    kept, away = split_own(products, after(got, par), "qkv_own", 4)
    qkv_sum = Reduction(plan, kept, away)
    moved = after(moved, qkv_sum.step())
    sent = qkv_sum.step()
    up_sum.steps_left(sent)
    sent = qkv_sum.step()
    down_mat_grad = down_sum.finish(sent).transpose(1, 0, 2).reshape(-1)
    up_total = up_sum.finish(sent)
    home_grad = from_parts(moved[:, :, :width])
    summed = jnp.sum(moved[:, :, width:].astype(F32), axis=0)
    summed = summed.reshape(part_rows, -1, 128).transpose(1, 0, 2).reshape(-1, 128)
    owned = [summed[k, :size] for k, size in enumerate(sizes)]
    up_mat_grad, out_mat_grad = split_result(up_total, [n_up, n_out])
    (qkv_mat_grad,) = split_result(qkv_sum.finish(), [n_qkv])
    return (
        home_out,
        home_grad,
        qkv_mat_grad,
        owned[0],
        out_mat_grad,
        owned[1],
        owned[2],
        owned[3],
        up_mat_grad,
        owned[4],
        down_mat_grad,
        owned[5],
        owned[6],
        owned[7],
    )


def solution(mesh):
    rows = P(None, None, AXES, None)
    flat = P(AXES)
    in_specs = (rows, P(), P()) + (flat,) * 12 + (rows,)
    out_specs = (rows, rows) + (flat,) * 12
    return jax.shard_map(body, mesh=mesh, in_specs=in_specs, out_specs=out_specs, check_vma=False)
```

```python
import math

import jax
import jax.numpy as jnp
from jax import lax
from jax.experimental import pallas as pl
from jax.experimental.pallas import tpu as pltpu
from jax.sharding import PartitionSpec as P

D = 768
HEADS = 12
HD = 64
FF = 3072
AXES = ("dp", "fsdp")
BLOCK = 384
F32 = jnp.float32
BF16 = jnp.bfloat16


class Plan:
    def __init__(self, n_dp, n_fsdp):
        self.n = n_dp * n_fsdp
        self.chips = self.n // 2
        bits = [1 << k for k in range(1, self.n.bit_length() - 1)]
        near, far = bits[:2], bits[2:]
        first = [b | (b >> 1) if b >> 1 in far else b for b in reversed(far)]
        self.masks = [first + near[::-1], first + near]
        self.levels = len(bits)
        self.combos = []
        for masks in self.masks:
            row = []
            for rel in range(self.chips):
                total = 0
                for k in range(self.levels):
                    if rel >> k & 1:
                        total ^= masks[k]
                row.append(total)
            self.combos.append(row)

    def pairs(self, level):
        return [(i, i ^ self.masks[i & 1][level]) for i in range(self.n)]

    def core_pairs(self):
        return [(i, i ^ 1) for i in range(self.n)]

    def order(self, me, core):
        table = jnp.asarray(self.combos, jnp.int32)
        return (me ^ jnp.where(core == 0, table[0], table[1])) // 2

    def places(self, me, core):
        spots = [[0] * self.chips for _ in range(2)]
        for spot, row in zip(spots, self.combos):
            for rel, total in enumerate(row):
                spot[total // 2] = rel
        table = jnp.asarray(spots, jnp.int32)
        away = jnp.arange(self.chips, dtype=jnp.int32) ^ (me // 2)
        return jnp.where(core == 0, table[0], table[1])[away]


def swap(value, pairs):
    return lax.ppermute(value, AXES, pairs)


def after(value, *earlier):
    return lax.optimization_barrier((value,) + earlier)[0]


class Gather:
    def __init__(self, plan, piece):
        self.plan = plan
        self.held = piece[None]
        self.got = []
        self.merged = 0

    def merge(self, *earlier):
        if self.merged < len(self.got):
            if earlier:
                self.got[-1] = after(self.got[-1], *earlier)
            self.held = jnp.concatenate([self.held, self.got[-1]], axis=0)
            self.merged = len(self.got)
        return self.held

    def step(self, *earlier, late=False):
        level = len(self.got)
        if late:
            self.got[-1] = after(self.got[-1], *earlier)
        self.merge()
        if earlier and not late:
            self.held = after(self.held, *earlier)
        self.got.append(swap(self.held, self.plan.pairs(level)))
        return self.held

    def finish(self, *earlier):
        self.own = [self.held, self.got[-1]]
        if earlier:
            self.own = [after(part, *earlier) for part in self.own]
        self.par = [swap(part, self.plan.core_pairs()) for part in self.own]


class Reduction:
    def __init__(self, plan, kept, away):
        self.plan = plan
        self.kept = kept
        self.level = plan.levels - 1
        self.got = swap(away, plan.pairs(self.level))

    def step(self, *earlier):
        self.level -= 1
        if earlier:
            self.got = after(self.got, *earlier)
        half = self.kept.shape[0] // 2
        kept, got = self.kept.astype(F32), self.got.astype(F32)
        away = (kept[half:] + got[half:]).astype(BF16)
        self.got = swap(away, self.plan.pairs(self.level))
        self.kept = kept[:half] + got[:half]
        if self.level > 0:
            self.kept = self.kept.astype(BF16)
        return away

    def steps_left(self, *earlier):
        return [self.step(*earlier) for _ in range(self.level)]

    def finish(self, *earlier):
        self.steps_left()
        if earlier:
            self.got = after(self.got, *earlier)
        return (self.kept + self.got.astype(F32))[0]


def split_columns(plan, core, left, right):
    keep = jnp.where(core == 0, left, right)
    got = swap(jnp.where(core == 0, right, left), plan.core_pairs())
    return jnp.where(core == 0, jnp.concatenate([keep, got], 1), jnp.concatenate([got, keep], 1))


def unsplit_columns(plan, core, block):
    rows = block.shape[1] // 2
    upper, lower = block[:, :rows], block[:, rows:]
    keep = jnp.where(core == 0, upper, lower)
    got = swap(jnp.where(core == 0, lower, upper), plan.core_pairs())
    return jnp.where(core == 0, keep, got), jnp.where(core == 0, got, keep)


def vmem(array):
    return (array, pl.BlockSpec(memory_space=pltpu.VMEM))


def smem(array):
    return (array, pl.BlockSpec(memory_space=pltpu.SMEM))


def loose(array):
    return (array, pl.BlockSpec(memory_space=pltpu.HBM))


def lane_block(array, width, place):
    return (array, pl.BlockSpec((array.shape[0], width), lambda step: (0, place)))


def run_kernel(body, name, ins, outs, scratch, micros, grid=()):
    return pl.pallas_call(
        body,
        name=name,
        grid=grid,
        in_specs=[spec for _, spec in ins],
        out_specs=[
            pl.BlockSpec(memory_space=pltpu.VMEM if inside else pl.ANY) for _, _, inside in outs
        ],
        out_shape=[jax.ShapeDtypeStruct(shape, dtype) for shape, dtype, _ in outs],
        scratch_shapes=scratch,
        compiler_params=pltpu.CompilerParams(vmem_limit_bytes=44 * 2**20),
        cost_estimate=pl.CostEstimate(
            flops=int(micros * 2.2e9), bytes_accessed=2**20, transcendentals=0
        ),
    )(*[array for array, _ in ins])


def dot_nn(left, right):
    return jnp.dot(left, right, preferred_element_type=F32)


def dot_nt(left, right):
    return lax.dot_general(left, right, (((1,), (1,)), ((), ())), preferred_element_type=F32)


def dot_tn(left, right):
    return lax.dot_general(left, right, (((0,), (0,)), ((), ())), preferred_element_type=F32)


def buffer(array):
    return [pltpu.VMEM(array.shape, array.dtype), pltpu.SemaphoreType.DMA(())]


def fetch(ref, held, sem):
    copy = pltpu.make_async_copy(ref, held, sem)
    copy.start()
    return copy


class Weight:
    def __init__(self, sources, places, blocks, height, per_column=1):
        self.sources = sources
        self.places = places
        self.blocks = blocks
        self.height = height
        self.per_column = per_column

    def ins(self):
        return [smem(self.places)] + [loose(array) for array, _, _ in self.sources]

    def scratch(self):
        return [pltpu.VMEM((self.blocks, self.height, BLOCK), BF16), pltpu.SemaphoreType.DMA((2,))]

    def count(self):
        return 1 + len(self.sources)

    def start(self, refs, held, sem):
        places, at = refs[0], 0
        for k, ((_, first, number), ref) in enumerate(zip(self.sources, refs[1:])):
            count, _, rows, _ = ref.shape
            for j in range(count):
                for turn in range(self.per_column):
                    row = pl.multiple_of(places[2 * at + 1] + turn * rows, 16)
                    share = number // self.per_column
                    pltpu.make_async_copy(
                        ref.at[j, pl.ds(first + turn * share, share)],
                        held.at[pl.ds(places[2 * at], share), pl.ds(row, rows)],
                        sem.at[2 * k // len(self.sources)],
                    ).start()
                at += 1

    def halves(self, refs, held, sem):
        number = self.blocks // 2
        total = sum(ref.shape[0] for ref in refs[1:])
        for k in range(2):
            part = held.at[pl.ds(0, number)]
            pltpu.make_async_copy(part, part, sem.at[k]).wait()
            yield refs[0][k * total]

    def wait(self, refs, held, sem):
        if len(self.sources) == 1:
            pltpu.make_async_copy(held, held, sem.at[0]).wait()
        else:
            part = held.at[:, pl.ds(0, self.height // 2)]
            for k in range(2):
                pltpu.make_async_copy(part, part, sem.at[k]).wait()


class Whole:
    def __init__(self, array):
        self.array = array

    def scratch(self, steps):
        return [pltpu.VMEM(self.array.shape, BF16), pltpu.SemaphoreType.DMA((steps,))]


def turned(values, cosine, sine):
    lanes = lax.broadcasted_iota(jnp.int32, values.shape, 1)
    swapped = jnp.where(
        lanes % 2 == 0, pltpu.roll(values, 127, 1), pltpu.roll(values, 1, 1)
    )
    return values * cosine + swapped * sine


def qkv_forward(x, weight, bias, cosine, sine, ready):
    rows = x.shape[0]
    n_w = weight.count()

    def body(*refs):
        x_ref, b_ref, cos_ref, sin_ref = refs[:4]
        w_refs = refs[4 : 4 + n_w]
        q_ref, kv_ref, whole, held, sem, whole_sem = refs[4 + n_w + len(ready) :]
        weight.start(w_refs, held, sem)
        weight.wait(w_refs, held, sem)
        whole_there = fetch(held, whole, whole_sem)
        cos, sin = cos_ref[...], sin_ref[...]
        for t in range(weight.blocks):
            y = dot_nn(x_ref[...], held[t]) + b_ref[:, t * BLOCK : (t + 1) * BLOCK]
            for g in range(BLOCK // 128):
                piece = y[:, g * 128 : (g + 1) * 128]
                at = t * BLOCK + g * 128
                if at < 2 * D:
                    piece = turned(piece, cos, sin)
                if at < D:
                    q_ref[:, at : at + 128] = (piece * (1.0 / math.sqrt(HD))).astype(BF16)
                else:
                    kv_ref[:, at - D : at - D + 128] = piece.astype(BF16)
        whole_there.wait()

    return run_kernel(
        body,
        "qkv_forward",
        [lane_block(x, D, 0), vmem(bias), vmem(cosine), vmem(sine)]
        + weight.ins()
        + [loose(array) for array in ready],
        [
            ((rows, D), BF16, True),
            ((rows, 2 * D), BF16, True),
            ((weight.blocks, D, BLOCK), BF16, False),
        ],
        weight.scratch() + [pltpu.SemaphoreType.DMA(())],
        7,
        grid=(1,),
    )


def row_standard(values):
    average = jnp.mean(values, axis=-1, keepdims=True)
    centered = values - average
    variance = jnp.mean(centered * centered, axis=-1, keepdims=True)
    inverse = lax.rsqrt(variance + 1e-05)
    return centered * inverse, inverse


def row_standard_back(grad, standard, inverse):
    mean_grad = jnp.mean(grad, axis=-1, keepdims=True)
    mean_proj = jnp.mean(grad * standard, axis=-1, keepdims=True)
    return inverse * (grad - mean_grad - standard * mean_proj)


PART = 384


def attention_forward(queries, key_values, mask, part, ready):
    rows = queries.shape[0]
    n_kv = len(key_values)
    block = min(rows, 256)

    def body(*refs):
        q_ref, mask_ref = refs[:2]
        k_refs = refs[2 : 2 + n_kv]
        v_refs = refs[2 + n_kv : 2 + 2 * n_kv]
        a_ref, lse_ref, lse_acc = refs[2 + 2 * n_kv + len(ready) :]
        lse_acc[...] = jnp.zeros_like(lse_acc)
        lanes = lax.broadcasted_iota(jnp.int32, (block, 128), 1)
        def pair(p, carry):
            at = pl.ds(pl.multiple_of(p * 128, 128), 128)
            for r in range(rows // block):
                own = slice(r * block, (r + 1) * block)
                q_pair = q_ref[own, at].astype(F32)
                heads = []
                for head in range(2):
                    q_head = jnp.where(lanes // HD == head, q_pair, 0.0).astype(BF16)
                    scores = [
                        dot_nt(q_head, key[:, at]) + mask_ref[g : g + 1, :]
                        for g, key in enumerate(k_refs)
                    ]
                    peak = scores[0].max(axis=-1, keepdims=True)
                    for s in scores[1:]:
                        peak = jnp.maximum(peak, s.max(axis=-1, keepdims=True))
                    raised = [jnp.exp(s - peak) for s in scores]
                    total = raised[0].sum(axis=-1, keepdims=True)
                    for e in raised[1:]:
                        total = total + e.sum(axis=-1, keepdims=True)
                    mixed = dot_nn(raised[0].astype(BF16), v_refs[0][:, at])
                    for e, value in zip(raised[1:], v_refs[1:]):
                        mixed = mixed + dot_nn(e.astype(BF16), value[:, at])
                    heads.append(mixed / total)
                    lse_acc[own, :] = jnp.where(
                        lanes == 2 * p + head, peak + jnp.log(total), lse_acc[own, :]
                    )
                a_ref[own, at] = jnp.where(lanes < HD, heads[0], heads[1]).astype(BF16)
            return carry

        lax.fori_loop(0, PART // 128, pair, 0)
        lse_ref[...] = jnp.transpose(lse_acc[...])[:8]

    return run_kernel(
        body,
        "attention_forward",
        [lane_block(queries, PART, part), vmem(mask)]
        + [lane_block(kv, PART, part) for kv in key_values]
        + [lane_block(kv, PART, part + D // PART) for kv in key_values]
        + [loose(array) for array in ready],
        [((rows, PART), BF16, True), ((8, rows), F32, True)],
        [pltpu.VMEM((rows, 128), F32)],
        6,
        grid=(1,),
    )


def out_forward(x, attended, weight, vectors, ready):
    rows = x.shape[0]
    n_a = len(attended)
    n_w = weight.count()
    block = min(rows, 128)

    def body(*refs):
        x_ref, ob_ref, g_ref, b_ref = refs[:4]
        part_refs = refs[4 : 4 + n_a]
        w_refs = refs[4 + n_a : 4 + n_a + n_w]
        a_ref, n_ref, s_ref, h_ref, whole, held, sem, acc, whole_sem = refs[
            4 + n_a + n_w + len(ready) :
        ]
        weight.start(w_refs, held, sem)
        for k, part in enumerate(part_refs):
            a_ref[:, k * PART : (k + 1) * PART] = part[...]
        weight.wait(w_refs, held, sem)
        whole_there = fetch(held, whole, whole_sem)
        for t in range(weight.blocks):
            acc[:, t * BLOCK : (t + 1) * BLOCK] = dot_nn(a_ref[...], held[t])

        def row(r, carry):
            own = pl.ds(pl.multiple_of(r * block, block), block)
            branch = acc[own, :] + ob_ref[...]
            standard, inverse = row_standard(x_ref[own, :].astype(F32) + branch)
            n_ref[own, :] = standard
            s_ref[own, :] = jnp.broadcast_to(inverse, (block, 128))
            h_ref[own, :] = (standard * g_ref[...] + b_ref[...]).astype(BF16)
            return carry

        lax.fori_loop(0, rows // block, row, 0)
        whole_there.wait()

    return run_kernel(
        body,
        "out_forward",
        [lane_block(x, D, 0)]
        + [vmem(v) for v in vectors]
        + [vmem(part) for part in attended]
        + weight.ins()
        + [loose(array) for array in ready],
        [
            ((rows, D), BF16, True),
            ((rows, D), F32, True),
            ((rows, 128), F32, True),
            ((rows, D), BF16, True),
            ((weight.blocks, D, BLOCK), BF16, False),
        ],
        weight.scratch() + [pltpu.VMEM((rows, D), F32), pltpu.SemaphoreType.DMA(())],
        4,
        grid=(1,),
    )


def bell(u):
    size = jnp.abs(u)
    t = 1.0 / (1.0 + (0.3275911 / math.sqrt(2.0)) * size)
    raised = jnp.exp(-0.5 * u * u)
    poly = 0.5 * 1.061405429
    for c in (-1.453152027, 1.421413741, -0.284496736, 0.254829592):
        poly = poly * t + 0.5 * c
    tail = poly * t * raised
    return jnp.where(u >= 0.0, 1.0 - tail, tail), raised


def up_forward(h, weight, bias, ready):
    rows = h.shape[0]
    n_w = weight.count()

    def body(*refs):
        h_ref, b_ref = refs[:2]
        w_refs = refs[2 : 2 + n_w]
        g_out, slope_out, whole, *scratch = refs[2 + n_w + len(ready) :]
        held, sem, g_ref, g_sem, slope_ref, slope_sem, whole_sem = scratch
        weight.start(w_refs, held, sem)
        for first in weight.halves(w_refs, held, sem):
            part = pl.ds(first, weight.blocks // 2)
            pltpu.make_async_copy(held.at[part], whole.at[part], whole_sem).start()

            def step(t, carry, first=first):
                at = pl.ds(pl.multiple_of((first + t) * BLOCK, 128), BLOCK)
                u = dot_nn(h_ref[...], held[first + t]) + b_ref[:, at]
                share, raised = bell(u)
                g_ref[:, at] = (u * share).astype(BF16)
                slope_ref[:, at] = (
                    share + u * raised * (1.0 / math.sqrt(2.0 * math.pi))
                ).astype(BF16)
                pltpu.make_async_copy(g_ref.at[:, at], g_out.at[:, at], g_sem).start()
                pltpu.make_async_copy(slope_ref.at[:, at], slope_out.at[:, at], slope_sem).start()
                return carry

            lax.fori_loop(0, weight.blocks // 2, step, 0)
        pltpu.make_async_copy(held, whole, whole_sem).wait()
        pltpu.make_async_copy(g_ref, g_out, g_sem).wait()
        pltpu.make_async_copy(slope_ref, slope_out, slope_sem).wait()

    wide = jax.ShapeDtypeStruct((rows, FF), BF16)
    return run_kernel(
        body,
        "up_forward",
        [vmem(h), vmem(bias)] + weight.ins() + [loose(array) for array in ready],
        [
            ((rows, FF), BF16, False),
            ((rows, FF), BF16, False),
            ((weight.blocks, D, BLOCK), BF16, False),
        ],
        weight.scratch() + buffer(wide) + buffer(wide) + [pltpu.SemaphoreType.DMA(())],
        12,
    )


def down_both(active, weight, standard_one, cot, vectors):
    rows = active.shape[0]
    n_w = weight.count()
    block = min(rows, 128)

    def body(*refs):
        g_in, n_in, cot_in, g1_ref, b1_ref, db_ref, g2_ref, b2_ref = refs[:8]
        w_refs = refs[8 : 8 + n_w]
        out_ref, dr_ref, dz_ref, sums_ref, whole, held, sem, z_ref = refs[8 + n_w : 16 + n_w]
        g_ref, g_sem, n_ref, n_sem, cot_ref, cot_sem, whole_sem = refs[16 + n_w :]
        active_there = fetch(g_in, g_ref, g_sem)
        weight.start(w_refs, held, sem)
        others_there = [fetch(n_in, n_ref, n_sem), fetch(cot_in, cot_ref, cot_sem)]
        active_there.wait()
        weight.wait(w_refs, held, sem)
        whole_there = fetch(held, whole, whole_sem)
        for t in range(weight.blocks):
            z_ref[:, t * BLOCK : (t + 1) * BLOCK] = dot_nn(g_ref[...], held[t])
        for there in others_there:
            there.wait()
        sums_ref[...] = jnp.zeros_like(sums_ref)

        def row(r, carry):
            own = pl.ds(pl.multiple_of(r * block, block), block)
            h = n_ref[own, :] * g1_ref[...] + b1_ref[...]
            standard, inverse = row_standard(h + z_ref[own, :] + db_ref[...])
            out_ref[own, :] = (standard * g2_ref[...] + b2_ref[...]).astype(BF16)
            dy = cot_ref[own, :].astype(F32)
            dr = row_standard_back(dy * g2_ref[...], standard, inverse)
            dr_ref[own, :] = dr
            low = dr.astype(BF16)
            dz_ref[own, :] = low
            sums_ref[0:1, :] += jnp.sum(dy * standard, axis=0, keepdims=True)
            sums_ref[1:2, :] += jnp.sum(dy, axis=0, keepdims=True)
            sums_ref[2:3, :] += jnp.sum(low.astype(F32), axis=0, keepdims=True)
            return carry

        lax.fori_loop(0, rows // block, row, 0)
        whole_there.wait()

    return run_kernel(
        body,
        "down_both",
        [loose(active), loose(standard_one), loose(cot)]
        + [vmem(v) for v in vectors]
        + weight.ins(),
        [
            ((rows, D), BF16, True),
            ((rows, D), F32, True),
            ((rows, D), BF16, True),
            ((8, D), F32, True),
            ((weight.blocks, FF, BLOCK), BF16, False),
        ],
        weight.scratch()
        + [pltpu.VMEM((rows, D), F32)]
        + buffer(active)
        + buffer(standard_one)
        + buffer(cot)
        + [pltpu.SemaphoreType.DMA(())],
        10,
    )


def middle_back(dz, slope, down, up, out, dr2, standard, inverse, gain, ready):
    rows = dz.shape[0]
    block = min(rows, 128)
    steps = FF // BLOCK

    def body(*refs):
        dz_ref, slope_in, down_in, up_in, out_in, dr2_in, n_in, s_in, g_ref = refs[:9]
        rest = refs[9 + len(ready) :]
        du_out, up_sums_ref, dr_ref, do_ref, da_ref, sums_ref = rest[:6]
        down_w, down_sem, up_w, up_sem, out_w, out_sem = rest[6:12]
        slope_ref, slope_sem, du_ref, du_sem = rest[12:16]
        acc, acc_sem, n_ref, n_sem, s_ref, s_sem, slope_sems = rest[16:]
        del slope_sem
        for t in range(steps):
            at = slice(t * BLOCK, (t + 1) * BLOCK)
            fetch(down_in.at[:, at], down_w.at[:, at], down_sem.at[t])
            fetch(slope_in.at[:, at], slope_ref.at[:, at], slope_sems.at[t])
            fetch(up_in.at[t], up_w.at[t], up_sem.at[t])
            if t == 0:
                acc_there = fetch(dr2_in, acc, acc_sem)
        others_there = [
            fetch(n_in, n_ref, n_sem),
            fetch(s_in, s_ref, s_sem),
            fetch(out_in, out_w, out_sem.at[0]),
        ]
        up_sums_ref[...] = jnp.zeros_like(up_sums_ref)
        sums_ref[...] = jnp.zeros_like(sums_ref)
        acc_there.wait()

        def step(t, carry):
            at = pl.ds(pl.multiple_of(t * BLOCK, 128), BLOCK)
            pltpu.make_async_copy(down_in.at[:, at], down_w.at[:, at], down_sem.at[t]).wait()
            pltpu.make_async_copy(slope_in.at[:, at], slope_ref.at[:, at], slope_sems.at[t]).wait()
            grad = dot_nt(dz_ref[:, :BLOCK], down_w[0, at, :])
            for k in range(1, D // BLOCK):
                grad = grad + dot_nt(dz_ref[:, k * BLOCK : (k + 1) * BLOCK], down_w[k, at, :])
            du = (grad * slope_ref[:, at].astype(F32)).astype(BF16)
            du_ref[:, at] = du
            pltpu.make_async_copy(du_ref.at[:, at], du_out.at[:, at], du_sem).start()
            up_sums_ref[0:1, at] = jnp.sum(du.astype(F32), axis=0, keepdims=True)
            pltpu.make_async_copy(up_in.at[t], up_w.at[t], up_sem.at[t]).wait()
            acc[...] += dot_nt(du, up_w[t])
            return carry

        lax.fori_loop(0, steps, step, 0)
        for there in others_there:
            there.wait()

        def row(r, carry):
            own = pl.ds(pl.multiple_of(r * block, block), block)
            dh = acc[own, :]
            standard_own = n_ref[own, :]
            dr = row_standard_back(dh * g_ref[...], standard_own, s_ref[own, 0:1])
            dr_ref[own, :] = dr
            low = dr.astype(BF16)
            do_ref[own, :] = low
            sums_ref[0:1, :] += jnp.sum(dh * standard_own, axis=0, keepdims=True)
            sums_ref[1:2, :] += jnp.sum(dh, axis=0, keepdims=True)
            sums_ref[2:3, :] += jnp.sum(low.astype(F32), axis=0, keepdims=True)
            return carry

        lax.fori_loop(0, rows // block, row, 0)
        grad = dot_nt(do_ref[:, :BLOCK], out_w[0])
        for t in range(1, D // BLOCK):
            grad = grad + dot_nt(do_ref[:, t * BLOCK : (t + 1) * BLOCK], out_w[t])
        da_ref[...] = grad.astype(BF16)
        pltpu.make_async_copy(du_ref, du_out, du_sem).wait()

    return run_kernel(
        body,
        "middle_back",
        [vmem(dz), loose(slope), loose(down.array), loose(up.array), loose(out.array)]
        + [loose(dr2), loose(standard), loose(inverse), vmem(gain)]
        + [loose(array) for array in ready],
        [
            ((rows, FF), BF16, False),
            ((8, FF), F32, True),
            ((rows, D), F32, True),
            ((rows, D), BF16, True),
            ((rows, D), BF16, True),
            ((8, D), F32, True),
        ],
        down.scratch(steps)
        + up.scratch(steps)
        + out.scratch(1)
        + buffer(slope)
        + buffer(slope)
        + buffer(dr2)
        + buffer(standard)
        + buffer(inverse)
        + [pltpu.SemaphoreType.DMA((steps,))],
        14,
    )


def attention_back(
    queries, key_values, d_attended, attended, lse, mask, cosine, sine, part, ready
):
    rows = queries.shape[0]
    n_kv = len(key_values)
    block = min(rows, 256)
    scale = 1.0 / math.sqrt(HD)

    def body(*refs):
        q_ref, da_ref, a_ref, lse_ref, mask_ref, cos_ref, sin_ref = refs[:7]
        k_refs = refs[7 : 7 + n_kv]
        v_refs = refs[7 + n_kv : 7 + 2 * n_kv]
        dq_ref, *dkv_refs = refs[7 + 2 * n_kv + len(ready) :]
        lanes = lax.broadcasted_iota(jnp.int32, (rows, 128), 1)
        picks = lax.broadcasted_iota(jnp.int32, (8, 128), 1) // HD
        chosen = (picks == lax.broadcasted_iota(jnp.int32, (8, 128), 0)).astype(F32)

        def pair(p, carry):
            at = pl.ds(pl.multiple_of(p * 128, 128), 128)
            v_at = pl.ds(pl.multiple_of(PART + p * 128, 128), 128)
            q_pair = q_ref[:, at].astype(F32)
            da_pair = da_ref[:, at].astype(F32)
            dots = lax.dot_general(
                chosen,
                da_pair * a_ref[:, at].astype(F32),
                (((1,), (1,)), ((), ())),
                precision=lax.Precision.HIGHEST,
                preferred_element_type=F32,
            )
            q_heads = [
                jnp.where(lanes // HD == head, q_pair, 0.0).astype(BF16) for head in range(2)
            ]
            da_heads = [
                jnp.where(lanes // HD == head, da_pair, 0.0).astype(BF16) for head in range(2)
            ]
            lse_rows = [lse_ref[pl.ds(2 * p + head, 1), :] for head in range(2)]
            dq_heads = [None, None]
            for g in range(n_kv):
                for b in range(rows // block):
                    own = slice(b * block, (b + 1) * block)
                    keys = k_refs[g][own, at]
                    values = v_refs[g][own, at]
                    hidden = mask_ref[g * rows + b * block : g * rows + (b + 1) * block, 0:1]
                    dk, dv = None, None
                    for head in range(2):
                        s = dot_nt(keys, q_heads[head]) + hidden
                        prob = jnp.exp(s - lse_rows[head])
                        dp = dot_nt(values, da_heads[head])
                        ds = (prob * (dp - dots[head : head + 1, :])).astype(BF16)
                        dv_part = dot_nn(prob.astype(BF16), da_heads[head])
                        dk_part = dot_nn(ds, q_heads[head])
                        dq_part = dot_tn(keys, ds)
                        dv = dv_part if dv is None else dv + dv_part
                        dk = dk_part if dk is None else dk + dk_part
                        dq_heads[head] = (
                            dq_part if dq_heads[head] is None else dq_heads[head] + dq_part
                        )
                    kind = F32 if g == 0 else BF16
                    dkv_refs[g][own, at] = dk.astype(kind)
                    dkv_refs[g][own, v_at] = dv.astype(kind)
            flipped = lax.broadcasted_iota(jnp.int32, (128, rows), 0)
            dq = jnp.transpose(jnp.where(flipped < HD, dq_heads[0], dq_heads[1])) * scale
            dq_ref[:, at] = turned(dq, cos_ref[...], -sin_ref[...]).astype(BF16)
            return carry

        lax.fori_loop(0, PART // 128, pair, 0)

    return run_kernel(
        body,
        "attention_back",
        [
            lane_block(queries, PART, part),
            lane_block(d_attended, PART, part),
            lane_block(attended, PART, part),
            vmem(lse),
            vmem(mask),
            vmem(cosine),
            vmem(sine),
        ]
        + [lane_block(kv, PART, part) for kv in key_values]
        + [lane_block(kv, PART, part + D // PART) for kv in key_values]
        + [loose(array) for array in ready],
        [((rows, PART), BF16, True)]
        + [((rows, 2 * PART), F32 if g == 0 else BF16, True) for g in range(n_kv)],
        [],
        8,
        grid=(1,),
    )


def join_qkv(parts, cosine, sine, ready):
    rows = parts[0][0].shape[0]
    n_each = len(parts[0])

    def body(*refs):
        cos_ref, sin_ref = refs[:2]
        part_refs = refs[2 : 2 + n_each * len(parts)]
        out_ref, sums_ref = refs[2 + n_each * len(parts) + len(ready) :]
        sums_ref[...] = jnp.zeros_like(sums_ref)
        cos, sin = cos_ref[...], -sin_ref[...]

        def put(at, low):
            out_ref[:, at : at + 128] = low
            sums_ref[0:1, at : at + 128] = jnp.sum(low.astype(F32), axis=0, keepdims=True)

        for k in range(len(parts)):
            dq_ref, dkv_ref, *got_refs = part_refs[k * n_each : (k + 1) * n_each]
            for at in range(0, PART, 128):
                put(k * PART + at, dq_ref[:, at : at + 128])
            for at in range(0, 2 * PART, 128):
                value = dkv_ref[:, at : at + 128]
                for got in got_refs:
                    value = value + got[:, at : at + 128].astype(F32)
                if at < PART:
                    put(D + k * PART + at, turned(value, cos, sin).astype(BF16))
                else:
                    put(2 * D + k * PART + at - PART, value.astype(BF16))

    return run_kernel(
        body,
        "join_qkv",
        [vmem(cosine), vmem(sine)]
        + [vmem(array) for part in parts for array in part]
        + [loose(array) for array in ready],
        [((rows, 3 * D), BF16, True), ((8, 3 * D), F32, True)],
        [],
        4,
    )


def input_back(dproj, weight, dr1, sums, width, part_rows, ready):
    rows = dproj.shape[0]
    n = rows // part_rows
    blocks = weight.array.shape[0]
    n_s = len(sums)

    def body(*refs):
        dp_ref, dr_in = refs[:2]
        sum_refs = refs[2 : 2 + n_s]
        w_in = refs[2 + n_s]
        out_ref, held, sem, shares, dr_ref, dr_sem = refs[3 + n_s + len(ready) :]
        there = [fetch(w_in.at[t], held.at[t], sem.at[t]) for t in range(blocks)]
        dr_there = fetch(dr_in, dr_ref, dr_sem)
        shares[...] = jnp.zeros_like(shares)
        if n <= 64:
            for place, (_, line), ref in zip(range(n_s), sums, sum_refs):
                size = ref.shape[1] // n
                row, column = place % part_rows, place // part_rows * 128
                for k in range(n):
                    at = k * part_rows + row
                    shares[at : at + 1, column : column + size] = ref[
                        line : line + 1, k * size : (k + 1) * size
                    ]
        out_ref[:, D:] = shares[...].astype(BF16)
        dr_there.wait()
        grad = dr_ref[...]
        for t in range(blocks):
            there[t].wait()
            grad = grad + dot_nt(dp_ref[:, t * BLOCK : (t + 1) * BLOCK], held[t])
        out_ref[:, :D] = grad.astype(BF16)

    result = run_kernel(
        body,
        "input_back",
        [vmem(dproj), loose(dr1)]
        + [vmem(array) for array, _ in sums]
        + [loose(weight.array)]
        + [loose(array) for array in ready],
        [((rows, width), BF16, True)],
        weight.scratch(blocks) + [pltpu.VMEM((rows, width - D), F32)] + buffer(dr1),
        6,
    )[0]
    if n <= 64:
        return result
    shares = []
    for array, line in sums:
        size = array.shape[1] // n
        shares.append(jnp.pad(array[line].reshape(n, size), ((0, 0), (0, 128 - size))))
    spare = -len(shares) % part_rows
    shares = jnp.stack(shares + [jnp.zeros_like(shares[0])] * spare, axis=1)
    shares = shares.reshape(n, -1, part_rows, 128).transpose(0, 2, 1, 3).reshape(rows, -1)
    return jnp.concatenate([result[:, :D], shares.astype(BF16)], axis=1)


def unpack_vectors(moved, sizes, part_rows):
    rows = moved.shape[0]
    n = rows // part_rows
    if n > 64:
        shares = moved[:, D:].astype(F32).reshape(n, part_rows, -1, 128).transpose(0, 2, 1, 3)
        shares = shares.reshape(n, -1, 128)
        return [shares[:, k, :size].reshape(1, -1) for k, size in enumerate(sizes)]

    def body(moved_ref, *refs):
        shares = refs[-1]
        shares[...] = moved_ref[...].astype(F32)
        for place, (size, ref) in enumerate(zip(sizes, refs)):
            for k in range(n):
                at = k * part_rows + place
                ref[0:1, k * size : (k + 1) * size] = shares[at : at + 1, :size]

    return run_kernel(
        body,
        "unpack_vectors",
        [lane_block(moved, 128, D // 128)],
        [((1, n * size), F32, True) for size in sizes],
        [pltpu.VMEM((rows, 128), F32)],
        2,
        grid=(1,),
    )


def split_grad(products, table, turn, got, chips, direct, name, micros, ready):
    height = D
    rows = products[0][0].shape[0]
    blocks = [right.shape[1] // 2 // BLOCK for _, right in products]
    count = chips if direct else 1
    size = height // count
    total = sum(blocks)
    extra = [] if got is None else [loose(got)]
    parts = 2 if direct and got is not None else 1

    def body(*refs):
        pair_refs = refs[: 2 * len(products)]
        table_ref = refs[2 * len(products)]
        got_refs = refs[2 * len(products) + 1 :][: len(extra)]
        rest = refs[2 * len(products) + 1 + len(extra) + len(ready) :]
        outs, (held, sem, other, other_sem, columns, column_sems) = rest[:parts], rest[parts:]
        core = table_ref[2 * count]
        half = 1 - core if turn == 0 else core
        column_there = []
        for k, number in enumerate(blocks):
            for t in range(number):
                at = pl.ds(pl.multiple_of((half * number + t) * BLOCK, 128), BLOCK)
                spot = len(column_there)
                column_there.append(
                    fetch(
                        pair_refs[2 * k + 1].at[:, at], columns.at[spot], column_sems.at[spot]
                    )
                )
        for got_ref in got_refs:
            for k in range(count):
                pltpu.make_async_copy(
                    got_ref.at[table_ref[turn * count + k]],
                    other.at[:, pl.ds(k * size, size)],
                    other_sem,
                ).start()
        done = 0
        for k, number in enumerate(blocks):
            left_ref = pair_refs[2 * k]
            for t in range(number):
                column_there[done].wait()
                grad = dot_tn(left_ref[...], columns[done])
                if got_refs:
                    if done == 0:
                        pltpu.make_async_copy(other, other, other_sem).wait()
                    grad = grad + other[done].astype(F32)
                held[done] = grad.astype(BF16)
                done += 1
        for k in range(count):
            place = table_ref[turn * count + k]
            source = held.at[:, pl.ds(k * size, size)]
            if parts == 1:
                pltpu.make_async_copy(source, outs[0].at[place], sem).start()
            else:
                for part, out in enumerate(outs):

                    @pl.when(place // (count // 2) == part)
                    def _(source=source, out=out, place=place, part=part):
                        spot = place - part * (count // 2)
                        pltpu.make_async_copy(source, out.at[spot], sem).start()

        for out in outs:
            pltpu.make_async_copy(out, out, sem).wait()

    kept = pltpu.VMEM((total, height, BLOCK), BF16)
    return run_kernel(
        body,
        name,
        [spec for left, right in products for spec in (lane_block(left, D, 0), loose(right))]
        + [smem(table)]
        + extra
        + [loose(array) for array in ready],
        [((count // parts, total, size, BLOCK), BF16, False)] * parts,
        [
            kept,
            pltpu.SemaphoreType.DMA(()),
            kept if extra else pltpu.VMEM((1, 16, BLOCK), BF16),
            pltpu.SemaphoreType.DMA(()),
            pltpu.VMEM((total, rows, BLOCK), BF16),
            pltpu.SemaphoreType.DMA((total,)),
        ],
        micros,
        grid=(1,),
    )


def row_grad(left, right, table, chips, direct, name):
    height = left.shape[1]
    blocks = right.shape[1] // BLOCK
    tile = 768
    size = height // chips // 2
    shape = (chips, blocks, size, BLOCK)
    per_tile = tile // (2 * size)

    def body(left_in, right_ref, table_ref, par_ref, own_ref, *scratch):
        held, par_sem, own_sem, left_ref, left_sems = scratch
        core = table_ref[2 * chips]
        for t in range(height // tile):
            at = slice(t * tile, (t + 1) * tile)
            fetch(left_in.at[:, at], left_ref.at[:, at], left_sems.at[t])

        def step(t, carry):
            at = pl.ds(pl.multiple_of(t * tile, tile), tile)
            pltpu.make_async_copy(left_in.at[:, at], left_ref.at[:, at], left_sems.at[t]).wait()
            grad = dot_tn(left_ref[:, at], right_ref[...]).astype(BF16)
            for k in range(blocks):
                held[k, at, :] = grad[:, k * BLOCK : (k + 1) * BLOCK]
            for k in range(per_tile):
                chip = t * per_tile + k
                for turn, (out, sem) in enumerate(((par_ref, par_sem), (own_ref, own_sem))):
                    part = 1 - core if turn == 0 else core
                    start = pl.multiple_of((2 * chip + part) * size, 16)
                    pltpu.make_async_copy(
                        held.at[:, pl.ds(start, size)],
                        out.at[table_ref[turn * chips + chip]],
                        sem,
                    ).start()
            return carry

        lax.fori_loop(0, height // tile, step, 0)
        pltpu.make_async_copy(par_ref, par_ref, par_sem).wait()
        pltpu.make_async_copy(own_ref, own_ref, own_sem).wait()

    def whole(left_ref, right_ref, table_ref, out_ref):
        for t in range(height // tile):
            at = slice(t * tile, (t + 1) * tile)
            out_ref[at, :] = dot_tn(left_ref[:, at], right_ref[...]).astype(BF16)

    if not direct:
        return run_kernel(
            whole,
            name,
            [vmem(left), vmem(right), smem(table)],
            [((height, right.shape[1]), BF16, True)],
            [],
            6,
        )
    return run_kernel(
        body,
        name,
        [loose(left), vmem(right), smem(table)],
        [(shape, BF16, False), (shape, BF16, False)],
        [
            pltpu.VMEM((blocks, height, BLOCK), BF16),
            pltpu.SemaphoreType.DMA(()),
            pltpu.SemaphoreType.DMA(()),
            pltpu.VMEM(left.shape, left.dtype),
            pltpu.SemaphoreType.DMA((height // tile,)),
        ],
        6,
    )


def body(
    tokens,
    lengths,
    deal,
    w_qkv,
    b_qkv,
    w_out,
    b_out,
    norm1_gain,
    norm1_bias,
    w_up,
    b_up,
    w_down,
    b_down,
    norm2_gain,
    norm2_bias,
    cotangent,
):
    n_dp = lax.axis_size("dp")
    n_fsdp = lax.axis_size("fsdp")
    plan = Plan(n_dp, n_fsdp)
    n, chips = plan.n, plan.chips
    dp_place = lax.axis_index("dp")
    fsdp_place = lax.axis_index("fsdp")
    me = dp_place * n_fsdp + fsdp_place
    core = me % 2
    batches, slot_count, home_rows, width = tokens.shape
    group = n_fsdp // batches
    part_rows = home_rows // group
    rows = n * part_rows
    local = fsdp_place % group
    batch_place = fsdp_place // group
    mine = plan.order(me, core)
    other = plan.order(me, 1 - core)
    mine_place = plan.places(me, core)
    other_place = plan.places(me, 1 - core)
    stores = jnp.concatenate([other_place, mine_place, core[None]]).astype(jnp.int32)
    group_pairs = [
        [(i, i - i % group + (i + k) % group) for i in range(n)] for k in range(1, group)
    ]
    back_pairs = [[(b, a) for a, b in pairs] for pairs in group_pairs]

    def to_parts(array):
        parts = array.reshape(batches, slot_count, group, part_rows, width)
        return parts.transpose(1, 0, 2, 3, 4).reshape(n, part_rows, width)

    def exchange(parts):
        moved = lax.all_to_all(parts, AXES, split_axis=0, concat_axis=0, tiled=True)
        return moved.reshape(rows, -1)

    def from_parts(moved):
        moved = moved.reshape(slot_count, batches, group, part_rows, width)
        return moved.transpose(1, 0, 2, 3, 4).reshape(batches, slot_count, home_rows, width)

    def by_blocks(shard, columns):
        return shard.reshape(-1, columns // BLOCK, BLOCK).transpose(1, 0, 2)

    def whole(parts, place):
        joined = jnp.concatenate(parts)[place].transpose(1, 0, 2, 3)
        return joined.reshape(1, joined.shape[0], -1, BLOCK)

    def split_parts(gather, number):
        if gather.own[0].shape[2] % 16 == 0:
            return gather.own + gather.par
        own, par = [[part[:, :number] for part in parts] for parts in (gather.own, gather.par)]
        return [whole(own, mine_place), whole(par, other_place)]

    def split_places(number):
        size = D // chips
        spots = [mine, other] if size % 16 == 0 else [jnp.zeros((1,), jnp.int32)] * 2
        tables = []
        for half, spot in zip((core, 1 - core), spots):
            starts = jnp.full(spot.shape, half * number)
            tables.append(jnp.stack([starts, spot * size], axis=1))
        return jnp.concatenate(tables).reshape(-1).astype(jnp.int32)

    def row_places():
        size = FF // n
        if size % 16 != 0:
            return jnp.zeros((2,), jnp.int32)
        starts = jnp.concatenate([mine * 2 + core, other * 2 + 1 - core]) * size
        return jnp.stack([jnp.zeros_like(starts), starts], axis=1).reshape(-1).astype(jnp.int32)

    def split_weight(parts, places, first, number):
        return Weight([(part, first, number) for part in parts], places, 2 * number, D)

    def row_weight(gather, places, first, number, chunks):
        own, par = gather.own, gather.par
        size = own[0].shape[2]
        if size % 16 == 0:
            sources = [(part, first, number * chunks) for part in own + par]
            return Weight(sources, places, number, n * size * chunks, chunks)

        def joined(parts, place):
            parts = jnp.concatenate(parts)[place][:, first:]
            parts = parts.reshape(chips, chunks, number, size, BLOCK).transpose(0, 2, 1, 3, 4)
            return parts.reshape(chips, number, chunks * size, BLOCK)

        own, par = joined(own, mine_place), joined(par, other_place)
        both = jnp.where(core == 0, jnp.stack([own, par], 2), jnp.stack([par, own], 2))
        both = both.transpose(1, 0, 2, 3, 4).reshape(1, number, -1, BLOCK)
        return Weight([(both, 0, number)], jnp.zeros((2,), jnp.int32), number, FF)

    size = D // chips
    direct = size % 16 == 0
    no_table = jnp.concatenate([jnp.zeros((2,), jnp.int32), core[None].astype(jnp.int32)])

    def split_order(array, order):
        return array.reshape(-1, chips, size, BLOCK).transpose(1, 0, 2, 3)[order]

    def split_other(products, name, micros, ready=()):
        table = stores if direct else no_table
        (par,) = split_grad(products, table, 0, None, chips, direct, name, micros, ready)
        return par if direct else split_order(par, other)

    def split_own(products, got, name, micros, ready=()):
        if direct:
            return split_grad(products, stores, 1, got, chips, True, name, micros, ready)
        got = got[mine_place].transpose(1, 0, 2, 3).reshape(1, -1, D, BLOCK)
        (own,) = split_grad(products, no_table, 1, got, chips, False, name, micros, ready)
        own = split_order(own, mine)
        return own[: chips // 2], own[chips // 2 :]

    def split_result(block, numbers):
        halves = unsplit_columns(plan, core, block)
        results, at = [], 0
        for number in numbers:
            both = jnp.concatenate([half[at : at + number] for half in halves])
            results.append(both.transpose(1, 0, 2).reshape(-1))
            at += number
        return results

    def row_pieces(left, right, name):
        size = FF // n
        if size % 16 == 0:
            return row_grad(left, right, stores, chips, True, name)
        both = row_grad(left, right, stores, chips, False, name)[0]
        blocks = both.reshape(chips, 2, size, -1, BLOCK).transpose(0, 1, 3, 2, 4)
        par = jnp.where(core == 0, blocks[:, 1], blocks[:, 0])[other]
        own = jnp.where(core == 0, blocks[:, 0], blocks[:, 1])[mine]
        return par, own

    small_shards = (
        b_qkv,
        b_out,
        norm1_gain,
        norm1_bias,
        b_up,
        b_down,
        norm2_gain,
        norm2_bias,
    )
    sizes = [piece.shape[0] for piece in small_shards]
    spare = -len(sizes) % part_rows
    shares = [jnp.pad(piece[None], ((0, 0), (0, 128 - piece.shape[0]))) for piece in small_shards]
    shares = jnp.concatenate(shares + [jnp.zeros((1, 128), BF16)] * (max(spare, 0)))
    shares = shares.reshape(-1, part_rows, 128).transpose(1, 0, 2).reshape(1, part_rows, -1)
    wide = width + shares.shape[2]
    parts = jnp.concatenate(
        [to_parts(tokens), jnp.broadcast_to(shares, (n,) + shares.shape[1:])], axis=2
    )
    def in_halves(cuts):
        left = jnp.concatenate([cut[: cut.shape[0] // 2] for cut in cuts])
        right = jnp.concatenate([cut[cut.shape[0] // 2 :] for cut in cuts])
        return split_columns(plan, core, left, right)

    n_qkv, n_out, n_up = 3 * D // BLOCK // 2, D // BLOCK // 2, FF // BLOCK // 2
    first = Gather(plan, in_halves([by_blocks(w_qkv, 3 * D)]))
    second = Gather(plan, in_halves([by_blocks(w_out, D), by_blocks(w_up, FF)]))
    third = Gather(plan, by_blocks(w_down, D))
    last = plan.levels - 1
    own_deal = jnp.where(batch_place == 0, deal[0], deal[1])
    own_lengths = jnp.where(batch_place == 0, lengths[0], lengths[1])
    for m in range(2, batches):
        own_deal = jnp.where(batch_place == m, deal[m], own_deal)
        own_lengths = jnp.where(batch_place == m, lengths[m], own_lengths)
    seq_len = jnp.sum(jnp.where(own_deal == dp_place, own_lengths, 0))

    row_ids = jnp.arange(rows, dtype=jnp.int32)
    base_places = row_ids // part_rows * home_rows + row_ids % part_rows
    query_places = base_places + local * part_rows
    key_places = jnp.stack([base_places + (local + k) % group * part_rows for k in range(group)])
    mask = jnp.where(key_places < seq_len, 0.0, -1000000000.0).astype(F32)
    mask_columns = jnp.broadcast_to(mask.reshape(-1, 1), (group * rows, 128))
    half_lane = (jnp.arange(128) % HD // 2).astype(F32)
    frequency = 10000.0 ** (-(2.0 * half_lane) / HD)
    angles = query_places.astype(F32)[:, None] * frequency[None, :]
    cosine = jnp.cos(angles)
    sine = jnp.sin(angles) * jnp.where(jnp.arange(128) % 2 == 0, -1.0, 1.0)

    first.step()
    first.step()
    second.step(first.got[0])
    sent = second.step(first.got[1])
    parts = after(parts, sent)
    block_in = exchange(parts)
    first.step()
    for level in range(3, last):
        second.step()
        first.step()
    first.step(parts)
    cot_parts = to_parts(cotangent)
    qkv_places, out_places, up_places, down_places = (
        split_places(n_qkv),
        split_places(n_out),
        split_places(n_up),
        row_places(),
    )
    (
        first.got[-1],
        qkv_places,
        out_places,
        up_places,
        down_places,
        stores,
        cot_parts,
        mask,
        mask_columns,
        cosine,
        sine,
    ) = lax.optimization_barrier(
        (
            first.got[-1],
            qkv_places,
            out_places,
            up_places,
            down_places,
            stores,
            cot_parts,
            mask,
            mask_columns,
            cosine,
            sine,
        )
    )
    sent = second.step(first.got[-1])
    first.finish(sent)
    early = third.step(sent)
    qkv_weight = split_weight(split_parts(first, n_qkv), qkv_places, 0, n_qkv)
    vectors = unpack_vectors(block_in, sizes, part_rows)
    (qkv_bias, out_bias, gain_one, bias_one, up_bias, down_bias, gain_two, bias_two) = vectors

    queries, key_value, qkv_whole = qkv_forward(
        block_in, qkv_weight, qkv_bias, cosine, sine, [early, cot_parts]
    )
    key_values = [key_value] + [swap(key_value, pairs) for pairs in back_pairs]
    ready = [second.step(key_value)]
    while len(third.got) < last - 1:
        ready.append(third.step(key_value))
    heads, lses = [], []
    n_parts = D // PART
    for part in range(n_parts):
        head, lse = attention_forward(queries, key_values, mask, part, ready)
        heads.append(head)
        lses.append(lse)
        ready = [head]
        ready.append(third.merge(head))
    cot_parts = after(cot_parts, *heads)
    grad_top = exchange(cot_parts)
    second.finish(head)
    rest = split_parts(second, n_out + n_up)
    out_weight = split_weight(rest, out_places, 0, n_out)
    up_weight = split_weight(rest, up_places, n_out, n_up)
    sent = third.step(head, second.got[-1])
    attended, standard_one, inverse_one, normed_low, out_whole = out_forward(
        block_in, heads, out_weight, [out_bias, gain_one, bias_one], [sent]
    )
    sent = third.step(normed_low, late=True)
    active, slope, up_whole = up_forward(normed_low, up_weight, up_bias, [sent])
    third.finish(active)
    down_weight = row_weight(third, down_places, 0, D // BLOCK, 1)
    result, grad_two, down_grad, sums_two, down_whole = down_both(
        active,
        down_weight,
        standard_one,
        grad_top,
        [gain_one, bias_one, down_bias, gain_two, bias_two],
    )
    par, own = row_pieces(active, down_grad, "down_grad")
    got = swap(par, plan.core_pairs())
    got = swap(par, plan.core_pairs())
    home_out = from_parts(exchange(result.reshape(n, part_rows, width)).reshape(n, part_rows, width))
    hidden_grad, sums_up, grad_one, branch_grad, d_attended, sums_one = middle_back(
        down_grad,
        slope,
        Whole(down_whole),
        Whole(up_whole),
        Whole(out_whole),
        grad_two,
        standard_one,
        inverse_one,
        gain_one,
        [par],
    )
    got = after(got, hidden_grad)
    half = chips // 2
    sent = (own[half:].astype(F32) + got[half:].astype(F32)).astype(BF16)
    kept = after((own[:half].astype(F32) + got[:half].astype(F32)).astype(BF16))
    down_sum = Reduction(plan, kept, sent)
    products = [(normed_low, hidden_grad), (attended, branch_grad)]
    par = split_other(products, "up_out_other", 5, [sent, home_out])
    got = swap(par, plan.core_pairs())
    kept, away = split_own(products, after(got, down_sum.kept), "up_out_own", 6)
    up_sum = Reduction(plan, kept, away)
    ready = [away]
    parts = []
    for part in range(n_parts):
        query_grad, *kv_grads = attention_back(
            queries,
            key_values,
            d_attended,
            attended,
            lses[part],
            mask_columns,
            cosine,
            sine,
            part,
            ready,
        )
        received = [swap(grad, pairs) for grad, pairs in zip(kv_grads[1:], group_pairs)]
        parts.append([query_grad, kv_grads[0]] + received)
        ready = [query_grad, down_sum.step(query_grad)]
    ready = [query_grad, up_sum.step(query_grad)]
    qkv_grad, sums_qkv = join_qkv(parts, cosine, sine, ready)
    products = [(block_in, qkv_grad)]
    small_sums = [
        (sums_qkv, 0),
        (sums_one, 2),
        (sums_one, 0),
        (sums_one, 1),
        (sums_up, 0),
        (sums_two, 2),
        (sums_two, 0),
        (sums_two, 1),
    ]
    input_grad = input_back(
        qkv_grad, Whole(qkv_whole), grad_one, small_sums, wide, part_rows, []
    )
    ready = down_sum.steps_left(input_grad) + [up_sum.step(input_grad)]
    moved = exchange(after(input_grad, *ready).reshape(n, part_rows, wide))
    moved = moved.reshape(n, part_rows, wide)
    par = split_other(products, "qkv_other", 3, [input_grad] + ready)
    got = swap(par, plan.core_pairs())
    kept, away = split_own(products, after(got, par), "qkv_own", 4)
    qkv_sum = Reduction(plan, kept, away)
    moved = after(moved, qkv_sum.step())
    sent = qkv_sum.step()
    up_sum.steps_left(sent)
    sent = qkv_sum.step()
    down_mat_grad = down_sum.finish(sent).transpose(1, 0, 2).reshape(-1)
    up_total = up_sum.finish(sent)
    home_grad = from_parts(moved[:, :, :width])
    summed = jnp.sum(moved[:, :, width:].astype(F32), axis=0)
    summed = summed.reshape(part_rows, -1, 128).transpose(1, 0, 2).reshape(-1, 128)
    owned = [summed[k, :size] for k, size in enumerate(sizes)]
    up_mat_grad, out_mat_grad = split_result(up_total, [n_up, n_out])
    (qkv_mat_grad,) = split_result(qkv_sum.finish(), [n_qkv])
    return (
        home_out,
        home_grad,
        qkv_mat_grad,
        owned[0],
        out_mat_grad,
        owned[1],
        owned[2],
        owned[3],
        up_mat_grad,
        owned[4],
        down_mat_grad,
        owned[5],
        owned[6],
        owned[7],
    )


def solution(mesh):
    rows = P(None, None, AXES, None)
    flat = P(AXES)
    in_specs = (rows, P(), P()) + (flat,) * 12 + (rows,)
    out_specs = (rows, rows) + (flat,) * 12
    return jax.shard_map(body, mesh=mesh, in_specs=in_specs, out_specs=out_specs, check_vma=False)
```
